32 devices in a mesh: seq: 16 (over z, y, x), tp: 2 (over core).
Axes of the slice: x: 2, y: 2, z: 4, core: 2. Of those that a mesh axis runs over, the one named last changes fastest.
Arguments:
- tokens: bfloat16 [2048, 2048], P('seq'), may hold values from -6 to 6
- attn_gain: float32 [2048], replicated, may hold values from 0.1 to 1.9
- mlp_gain: float32 [2048], replicated, may hold values from 0.1 to 1.9
- w_query: float32 [2048, 2048], P('seq', 'tp'), may hold values from -0.70710678 to 0.70710678
- w_key: float32 [2048, 2048], P('seq', 'tp'), may hold values from -0.70710678 to 0.70710678
- w_value: float32 [2048, 2048], P('seq', 'tp'), may hold values from -0.125 to 0.125
- w_out: float32 [2048, 2048], P('tp', 'seq'), may hold values from -0.125 to 0.125
- sink_logits: float32 [16], P('tp'), may hold values from 8 to 16
- router: float32 [2048, 16], P('seq'), may hold values from -0.25 to 0.25
- expert_gate: float32 [16, 2048, 1024], P(None, 'seq', 'tp'), may hold values from -0.125 to 0.125
- expert_up: float32 [16, 2048, 1024], P(None, 'seq', 'tp'), may hold values from -0.125 to 0.125
- expert_down: float32 [16, 2048, 1024], P(None, 'seq', 'tp'), may hold values from -0.1875 to 0.1875
- layout_map: int32 [16], replicated, may hold values from 0 to 15, each once
- real_lengths: int32 [2], replicated, may hold values from 256 to 1088, as said below
- routes: int32 [2048, 8], P('seq'), may hold values from 0 to 15, all different within a row; in each aligned block of 128 rows (0 to 127, 128 to 255, ...) at most 72 rows name the same one
Outputs:
- layer_out: bfloat16 [2048, 2048], P('seq', 'tp')
The draws below stay inside these ranges and needn't reach their ends.
Inputs may be any that keep to these rules, and one draw needn't show every extreme that they name: Prompt p has real tokens in the first real_lengths[p] of its slots and padding after them; each length is at least 256; the last prompt has no padding. `routes`: each row names 8 different experts; among the rows of one device no expert is named more than 72 times, and in some device some expert exactly 72 times. `layout_map`: each trainer expert is held by exactly one server expert number.
All inputs are finite; a program needn't handle non-finite values.
Results may differ from the reference program's by a relative error of at most 0.0075.
The reference program's roundings to bfloat16 on the way count: a program that leaves them out, or rounds other values in their place, can miss the bound.
Values may be sent and summed in bfloat16 or wider, within the bound.
No kernel may reach another device: no remote copies, remote signals or barrier semaphores. Data moves between devices by JAX's collectives and lax.ppermute only.
A program may use at most 128 MiB of HBM per device.

```python
import math
import jax
import jax.numpy as jnp
import numpy as np
from jax import lax

D = 2048
HEADS = 16
HEAD = 128
FFE = 1024
TOPK = 8
HALF_WIN = 2048
TOK_DEV = 128
PROMPTS = 2
EXPERTS = 16
TOKENS = 2048
SLOT = 1024
STAGGER = 64
CAP = 72
N_SEQ = 16
N_TP = 2


def draw_real_lengths(key, part):
    prompt_ids = jnp.arange(PROMPTS, dtype=jnp.int32)
    capacity = jnp.where(prompt_ids == 0, SLOT - STAGGER, jnp.where(prompt_ids == PROMPTS - 1, SLOT + STAGGER, SLOT)).astype(jnp.int32)
    shortest = max(SLOT // 4, SLOT - HALF_WIN // 2)
    spread = jax.random.randint(jax.random.fold_in(key, 11), (PROMPTS,), shortest, capacity + 1)
    return jnp.where(prompt_ids == PROMPTS - 1, capacity, spread).astype(jnp.int32)


def head_boost(key):
    offset = jax.random.randint(jax.random.fold_in(key, 31), (), 0, 4)
    head_ids = jnp.arange(HEADS, dtype=jnp.int32)
    boost = jnp.where((head_ids + offset) % 4 == 0, 4.0, 1.0).astype(jnp.float32)
    return jnp.repeat(boost, HEAD)


def boosted_weight(key, salt):
    inner = jax.random.fold_in(key, salt)
    base = jnp.clip(jax.random.normal(inner, (D, HEADS * HEAD), jnp.float32), -4.0, 4.0)
    return base * (2.0 / math.sqrt(D)) * head_boost(key)[None, :]


def draw_w_query(key, part):
    return boosted_weight(key, 41)


def draw_w_key(key, part):
    return boosted_weight(key, 42)


def level_of(key, dims, cuts, smallest, top_value):
    gain = 1.0
    for dim, blocks in cuts:
        heights = jax.random.uniform(jax.random.fold_in(jax.random.fold_in(key, 6), dim), (blocks,), jnp.float32, smallest / len(cuts), top_value / len(cuts))
        gain = gain * jnp.repeat(jnp.exp(heights), dims[dim] // blocks).reshape((-1,) + (1,) * (len(dims) - 1 - dim))
    return gain


def routed_block(key, own, number, rows, number_of, top, bound, lean):
    ranking = jax.random.permutation(key, number_of)
    packed, ordinary = shares(number_of, rows * top, bound, lean, True), shares(number_of, rows * top, bound, lean, False)
    places = jnp.arange(number_of)

    def named(lengths, offset_by):
        used = int((lengths > 0).sum())
        fixed = max(1, used // 4)
        shifted = fixed + (places - fixed + offset_by * (used - fixed)) % max(1, number_of - fixed)
        return jnp.zeros((number_of,), jnp.int32).at[ranking[jnp.where(places < fixed, places, shifted)]].set(jnp.asarray(lengths, jnp.int32))

    lengths = jnp.where(number % 4 == 0, named(packed, number // 4), named(ordinary, number - number // 4 - 1))
    mixed = jax.random.permutation(jax.random.fold_in(own, 3), number_of)
    giver, sink = mixed[0:number_of // 2 * 2:2], mixed[1:number_of // 2 * 2:2]
    room = jnp.minimum(lengths[giver] - 1, bound - lengths[sink]) // 2
    room = jnp.where((giver == ranking[0]) | (sink == ranking[0]) | (lengths[sink] == 0), 0, jnp.maximum(room, 0))
    shifted = jax.random.randint(jax.random.fold_in(own, 4), (number_of // 2,), 0, 1 << 20) % (room + 1)
    lengths = lengths.at[giver].add(-shifted).at[sink].add(shifted)
    items = jnp.searchsorted(jnp.cumsum(lengths), jnp.arange(rows * top), side="right").astype(jnp.int32)
    table = items.reshape(top, rows).T
    table = table[jax.random.permutation(jax.random.fold_in(own, 1), rows)]
    offset_by = jax.random.randint(jax.random.fold_in(own, 2), (rows, 1), 0, top)
    return jnp.take_along_axis(table, (jnp.arange(top)[None, :] + offset_by) % top, axis=1)


def shares(amount, total, bound, slope, full):
    loads = [(1 << 20) // math.isqrt(standing ** slope) + 1 for standing in range(1, amount + 1)]
    largest = bound if full else min(bound, max(-(-total // amount), total * loads[0] // sum(loads)))
    least = 1 if total - largest >= amount - 1 else 0
    holding, spare = [largest] + [least] * (amount - 1), total - largest - least * (amount - 1)
    while spare > 0:
        movable = [i for i in range(1, amount) if holding[i] < largest] or [i for i in range(1, amount) if holding[i] < bound]
        pool, left = sum([loads[i] for i in movable]), spare
        for i in movable:
            addition = min(bound - holding[i], max(1, left * loads[i] // pool), spare)
            holding[i] = holding[i] + addition
            spare = spare - addition
    return np.array(holding)


def noise(stream_key, extent, scale, limit, split=(), held_as=jnp.bfloat16):
    level = level_of(stream_key, extent, split, -0.22, 0.18) if split else 1.0
    array = jax.random.normal(stream_key, extent, jnp.float32) * scale * level
    return jnp.minimum(jnp.maximum(array, -limit), limit).astype(held_as)


def setup_inputs(seed: int = 0) -> dict:
    seeds = jax.random.split(jax.random.key(seed), 16)
    tokens = noise(seeds[0], (TOKENS, D), 1.0, 6.0, ((0, 16),))
    attn_gain = jnp.clip(1.0 + 0.18 * jax.random.normal(seeds[1], (D,), jnp.float32), 0.1, 1.9)
    mlp_gain = jnp.clip(1.0 + 0.18 * jax.random.normal(seeds[2], (D,), jnp.float32), 0.1, 1.9)
    w_query = draw_w_query(jax.random.fold_in(seeds[15], 71), 0)
    w_key = draw_w_key(jax.random.fold_in(seeds[15], 71), 0)
    w_value = noise(seeds[5], (D, HEADS * HEAD), D ** -0.5, 0.125, ((0, 16), (1, 2)), jnp.float32)
    w_out = noise(seeds[6], (HEADS * HEAD, D), (HEADS * HEAD) ** -0.5, 0.125, ((0, 2), (1, 16)), jnp.float32)
    sink_logits = jnp.clip(8.0 + 8.0 * jax.random.uniform(seeds[7], (HEADS,), jnp.float32) ** level_of(seeds[7], (HEADS,), ((0, 2),), -0.2, 0.2), 8.0, 16.0)
    router = noise(seeds[8], (D, EXPERTS), (D // 4) ** -0.5, 0.25, ((0, 16),), jnp.float32)
    expert_gate = noise(seeds[9], (EXPERTS, D, FFE), D ** -0.5, 0.125, ((1, 16), (2, 2)), jnp.float32)
    expert_up = noise(seeds[10], (EXPERTS, D, FFE), D ** -0.5, 0.125, ((1, 16), (2, 2)), jnp.float32)
    expert_down = noise(seeds[11], (EXPERTS, D, FFE), FFE ** -0.5, 0.1875, ((1, 16), (2, 2)), jnp.float32)
    layout_map = jax.random.permutation(seeds[12], EXPERTS).astype(jnp.int32)
    real_lengths = draw_real_lengths(jax.random.fold_in(seeds[15], 71), 0)
    routes_keys = jax.random.split(jax.random.fold_in(seeds[14], 1), TOKENS // TOK_DEV)
    routes_turns = jax.random.permutation(jax.random.fold_in(seeds[14], 3), TOKENS // TOK_DEV)
    routes = jax.vmap(lambda own, number: routed_block(jax.random.fold_in(seeds[14], 2), own, number, TOK_DEV, EXPERTS, TOPK, CAP, 2))(routes_keys, routes_turns).reshape((TOKENS, TOPK))
    return {"tokens": tokens, "attn_gain": attn_gain, "mlp_gain": mlp_gain, "w_query": w_query, "w_key": w_key, "w_value": w_value, "w_out": w_out, "sink_logits": sink_logits, "router": router, "expert_gate": expert_gate, "expert_up": expert_up, "expert_down": expert_down, "layout_map": layout_map, "real_lengths": real_lengths, "routes": routes}


EPSILON = 1e-05
ROPE_BASE = 50000.0
MASKED = -1e+30

def rms_scale(row_values, gain_vector):
    mean_square = lax.optimization_barrier(jnp.mean(row_values * row_values, axis=-1, keepdims=True))
    return row_values * lax.rsqrt(mean_square + EPSILON) * gain_vector

def rotate(head_block, positions):
    half_dim = head_block.shape[-1] // 2
    frequency = ROPE_BASE ** (-jnp.arange(half_dim, dtype=jnp.float32) / half_dim)
    angles = positions[:, None, None] * frequency[None, None, :]
    cosine = jnp.cos(angles)
    sine_part = jnp.sin(angles)
    first_half = head_block[..., :half_dim]
    second_half = head_block[..., half_dim:]
    return jnp.concatenate([first_half * cosine - second_half * sine_part, second_half * cosine + first_half * sine_part], axis=-1)

def length_of(prompt, real_lengths):
    one_hot = prompt[:, None] == jnp.arange(real_lengths.shape[0], dtype=jnp.int32)[None, :]
    return lax.optimization_barrier(jnp.sum(jnp.where(one_hot, real_lengths[None, :], 0), axis=1))

def prompt_split(slot_ids):
    prompt = jnp.minimum((slot_ids + STAGGER) // SLOT, PROMPTS - 1)
    start = jnp.maximum(prompt * SLOT - STAGGER, 0)
    return (prompt, slot_ids - start)

def coarsen(value_rows):
    return lax.optimization_barrier(value_rows.astype(jnp.bfloat16)).astype(jnp.float32)

def reference(tokens, attn_gain, mlp_gain, w_query, w_key, w_value, w_out, sink_logits, router, expert_gate, expert_up, expert_down, layout_map, real_lengths, routes):
    slot_ids = jnp.arange(TOKENS, dtype=jnp.int32)
    prompt, position = prompt_split(slot_ids)
    valid_token = position < length_of(prompt, real_lengths)
    proj_width = HEADS * HEAD
    normed = rms_scale(tokens.astype(jnp.float32), attn_gain).astype(jnp.bfloat16)
    rotary_positions = position.astype(jnp.float32)

    def project(weight):
        return jnp.dot(normed, weight.astype(jnp.bfloat16), preferred_element_type=jnp.float32).reshape(TOKENS, HEADS, HEAD)
    query_rows = rotate(project(w_query), rotary_positions).astype(jnp.bfloat16)
    key_rows = rotate(project(w_key), rotary_positions).astype(jnp.bfloat16)
    value_rows = project(w_value).astype(jnp.bfloat16)
    query_block = min(512, TOKENS)
    key_span = query_block + 2 * HALF_WIN
    pad_keys = jnp.pad(key_rows, ((HALF_WIN, HALF_WIN), (0, 0), (0, 0)))
    pad_values = jnp.pad(value_rows, ((HALF_WIN, HALF_WIN), (0, 0), (0, 0)))
    pad_ids = jnp.arange(TOKENS + 2 * HALF_WIN, dtype=jnp.int32) - HALF_WIN
    pad_live = jnp.pad(valid_token, (HALF_WIN, HALF_WIN))
    pad_prompt = jnp.pad(prompt, (HALF_WIN, HALF_WIN), constant_values=-1)
    score_scale = HEAD ** (-0.5)

    def one_block(first_row):
        block_queries = lax.dynamic_slice_in_dim(query_rows, first_row, query_block, 0).astype(jnp.float32)
        block_keys = lax.dynamic_slice_in_dim(pad_keys, first_row, key_span, 0).astype(jnp.float32)
        block_values = lax.dynamic_slice_in_dim(pad_values, first_row, key_span, 0).astype(jnp.float32)
        key_ids = lax.dynamic_slice_in_dim(pad_ids, first_row, key_span, 0)
        key_live = lax.dynamic_slice_in_dim(pad_live, first_row, key_span, 0)
        key_prompt = lax.dynamic_slice_in_dim(pad_prompt, first_row, key_span, 0)
        query_ids = first_row + jnp.arange(query_block, dtype=jnp.int32)
        query_prompt = prompt_split(query_ids)[0]
        allowed = (query_prompt[:, None] == key_prompt[None, :]) & key_live[None, :] & (jnp.abs(query_ids[:, None] - key_ids[None, :]) < HALF_WIN)
        scores = jnp.einsum('qhd,khd->hqk', block_queries, block_keys) * score_scale
        scores = jnp.where(allowed[None], scores, MASKED)
        running_max = jnp.maximum(sink_logits[:, None], lax.optimization_barrier(jnp.max(scores, axis=2)))
        weight_tensors = jnp.exp(scores - running_max[:, :, None])
        denominator = jnp.exp(sink_logits[:, None] - running_max) + lax.optimization_barrier(jnp.sum(weight_tensors, axis=2))
        block_mix = jnp.einsum('hqk,khd->hqd', weight_tensors, block_values, precision=lax.Precision.HIGHEST) / denominator[:, :, None]
        return jnp.transpose(block_mix, (1, 0, 2)).reshape(query_block, proj_width).astype(jnp.bfloat16)
    first_rows = jnp.arange(TOKENS // query_block, dtype=jnp.int32) * query_block
    attention_result = lax.map(one_block, first_rows).reshape(TOKENS, proj_width)
    residual = tokens.astype(jnp.float32) + jnp.dot(attention_result, w_out.astype(jnp.bfloat16), preferred_element_type=jnp.float32)
    mlp_in = rms_scale(residual, mlp_gain).astype(jnp.bfloat16)
    logits = jnp.dot(mlp_in, router.astype(jnp.bfloat16), preferred_element_type=jnp.float32)
    route_logits = jnp.take_along_axis(logits, routes, axis=1)
    route_weight = jax.nn.softmax(route_logits, axis=1) * valid_token[:, None]
    flat_routes = routes.reshape(-1)
    live_route = jnp.repeat(valid_token, TOPK)
    one_hot = ((flat_routes[:, None] == jnp.arange(EXPERTS, dtype=jnp.int32)[None, :]) & live_route[:, None]).astype(jnp.int32)
    per_device = one_hot.reshape(N_SEQ, TOK_DEV * TOPK, EXPERTS)
    rank_within = lax.optimization_barrier(jnp.sum((jnp.cumsum(per_device, axis=1) - per_device) * per_device, axis=2)).reshape(-1)
    device_of = jnp.repeat(slot_ids // TOK_DEV, TOPK)
    expert_token_rows = N_SEQ * CAP
    total_slots = EXPERTS * expert_token_rows
    slot_index = flat_routes * expert_token_rows + device_of * CAP + rank_within
    target_slot = jnp.where(live_route, slot_index, total_slots)
    source_row = jnp.zeros((total_slots,), jnp.int32).at[target_slot].set(jnp.repeat(slot_ids, TOPK) + 1, mode='drop')
    gathered = jnp.where((source_row > 0)[:, None], mlp_in[jnp.maximum(source_row - 1, 0)], jnp.zeros((), jnp.bfloat16))
    gathered = gathered.reshape(EXPERTS, expert_token_rows, D)
    hidden_share = FFE // N_TP

    def one_expert(pack):
        block_rows, gate_rows, up_rows, down_rows = pack
        inputs = block_rows.astype(jnp.float32)
        gate_proj = jnp.dot(inputs, gate_rows.astype(jnp.bfloat16).astype(jnp.float32), precision=lax.Precision.HIGHEST)
        up_proj = jnp.dot(inputs, up_rows.astype(jnp.bfloat16).astype(jnp.float32), precision=lax.Precision.HIGHEST)
        hidden_state = coarsen(jax.nn.silu(gate_proj) * up_proj).reshape(expert_token_rows, N_TP, hidden_share)
        down_parts = down_rows.astype(jnp.bfloat16).astype(jnp.float32).reshape(D, N_TP, hidden_share)
        partial_out = jnp.einsum('rpf,dpf->prd', hidden_state, down_parts, precision=lax.Precision.HIGHEST)
        return lax.optimization_barrier(jnp.sum(coarsen(partial_out), axis=0)).astype(jnp.bfloat16)
    expert_out = lax.map(one_expert, (gathered, expert_gate[layout_map], expert_up[layout_map], expert_down[layout_map]))
    expert_out = expert_out.reshape(total_slots, D)
    picked = expert_out[jnp.where(live_route, slot_index, 0)].reshape(TOKENS, TOPK, D)
    expert_mix = lax.optimization_barrier(jnp.sum(route_weight[:, :, None] * picked.astype(jnp.float32), axis=1))
    return (residual + expert_mix).astype(jnp.bfloat16)
```

```python
import jax
import jax.numpy as jnp
from jax import lax
from jax.experimental import pallas as pl
from jax.experimental.pallas import tpu as pltpu
from jax.sharding import PartitionSpec as P

HEAD = 128
HALF_WIN = 2048


EPSILON = 1e-05
ROPE_BASE = 50000.0
MASKED = -1e30


def from_behind(value, axis, steps):
    count = lax.axis_size(axis)
    first, last = (max(0, -steps), min(count, count - steps))
    return lax.ppermute(value, axis, [(source, source + steps) for source in range(first, last)])


def from_turned(value, axis, turn):
    count = lax.axis_size(axis)
    return lax.ppermute(value, axis, [((place + turn) % count, place) for place in range(count)])


def rms_scale(row_values, gain_vector):
    mean_square = jnp.mean(row_values * row_values, axis=-1, keepdims=True)
    return row_values * lax.rsqrt(mean_square + EPSILON) * gain_vector


def rotate(rows, cosine, sine_part):
    half_dim = rows.shape[-1] // 2
    first_half = rows[:, :half_dim]
    second_half = rows[:, half_dim:]
    return jnp.concatenate(
        [
            first_half * cosine - second_half * sine_part,
            second_half * cosine + first_half * sine_part,
        ],
        axis=-1,
    )


def length_of(prompt, real_lengths):
    one_hot = prompt[:, None] == jnp.arange(real_lengths.shape[0], dtype=jnp.int32)[None, :]
    return jnp.sum(jnp.where(one_hot, real_lengths[None, :], 0), axis=1)


def prompt_split(slot_ids, slot_len, stagger, prompt_count):
    prompt = jnp.minimum((slot_ids + stagger) // slot_len, prompt_count - 1)
    start = jnp.maximum(prompt * slot_len - stagger, 0)
    return (prompt, slot_ids - start)


def key_rules(query_ids, key_ids, slot_len, stagger, total_slots, real_lengths):
    prompt_count = real_lengths.shape[0]
    key_prompt, key_pos = prompt_split(key_ids, slot_len, stagger, prompt_count)
    query_prompt = prompt_split(query_ids, slot_len, stagger, prompt_count)[0]
    inside = (key_ids >= 0) & (key_ids < total_slots)
    key_live = inside & (key_pos < length_of(key_prompt, real_lengths))
    same_prompt = query_prompt[:, None] == key_prompt[None, :]
    nearby = jnp.abs(query_ids[:, None] - key_ids[None, :]) < HALF_WIN
    return same_prompt & nearby & key_live[None, :]


def parts_of(values, count):
    rest = values
    pieces = []
    for _ in range(count):
        piece = lax.reduce_precision(rest, 8, 7)
        rest = rest - piece
        pieces.append(piece.astype(jnp.bfloat16))
    return pieces


def attend(softmax_state, query_rows, key_rows, value_rows, allowed):
    running_max, denominator, accumulated = softmax_state
    scores = lax.dot_general(
        query_rows, key_rows, (((1,), (1,)), ((), ())), preferred_element_type=jnp.float32
    ) * HEAD ** (-0.5)
    scores = jnp.where(allowed, scores, MASKED)
    new_max = jnp.maximum(running_max, jnp.max(scores, axis=1, keepdims=True))
    rescale = jnp.exp(running_max - new_max)
    weight_tensors = jnp.exp(scores - new_max)
    denominator = denominator * rescale + jnp.sum(weight_tensors, axis=1, keepdims=True)
    high, low = parts_of(weight_tensors, 2)
    accumulated = (
        accumulated * rescale
        + jnp.dot(high, value_rows, preferred_element_type=jnp.float32)
        + jnp.dot(low, value_rows, preferred_element_type=jnp.float32)
    )
    return (new_max, denominator, accumulated)


def order_body(order_ref, gate_ref, up_ref, down_ref, both_ref, last_ref):
    width = gate_ref.shape[2]
    both_ref[0, :, :width] = gate_ref[0].astype(jnp.bfloat16)
    both_ref[0, :, width:] = up_ref[0].astype(jnp.bfloat16)
    last_ref[0] = down_ref[0].astype(jnp.bfloat16)


def order_experts(layout_map, gate, up, down):
    count, rows, width = gate.shape
    source = pl.BlockSpec((1, rows, width), lambda place, order: (order[place], 0, 0))
    return pl.pallas_call(
        order_body,
        grid_spec=pltpu.PrefetchScalarGridSpec(
            num_scalar_prefetch=1,
            grid=(count,),
            in_specs=[source, source, source],
            out_specs=[
                pl.BlockSpec((1, rows, 2 * width), lambda place, order: (place, 0, 0)),
                pl.BlockSpec((1, rows, width), lambda place, order: (place, 0, 0)),
            ],
        ),
        out_shape=[
            jax.ShapeDtypeStruct((count, rows, 2 * width), jnp.bfloat16),
            jax.ShapeDtypeStruct((count, rows, width), jnp.bfloat16),
        ],
        name="order_experts",
    )(layout_map, gate, up, down)


def shards(
    tokens,
    attn_gain,
    mlp_gain,
    w_query,
    w_key,
    w_value,
    w_out,
    sink_logits,
    router,
    expert_gate,
    expert_up,
    expert_down,
    layout_map,
    real_lengths,
    routes,
):
    token_count, model_width = tokens.shape
    seq_count = lax.axis_size("seq")
    tp_count = lax.axis_size("tp")
    expert_count = router.shape[1]
    route_count = routes.shape[1]
    head_count = sink_logits.shape[0]
    col_share = model_width // tp_count
    total_slots = token_count * seq_count
    prompt_count = real_lengths.shape[0]
    slot_len = total_slots // prompt_count
    stagger = token_count // 2
    capacity = max(2, min(token_count, 9 * token_count * route_count // (8 * expert_count)))
    part_count = seq_count // head_count
    part_slots = head_count * token_count
    local_experts = expert_count // seq_count
    seq_place = lax.axis_index("seq")
    tp_place = lax.axis_index("tp")
    part = seq_place // head_count
    head = seq_place % head_count
    groups = [[first + k for k in range(head_count)] for first in range(0, seq_count, head_count)]

    def tp_blocks(value):
        return [value] + [from_turned(value, "tp", turn) for turn in range(1, tp_count)]

    def tp_rows(weights, turn):
        block = (tp_place + turn) % tp_count
        return lax.dynamic_slice_in_dim(weights, block * col_share, col_share, 0)

    offsets = jnp.arange(token_count, dtype=jnp.int32)
    token_index = seq_place * token_count + offsets
    prompt, position = prompt_split(token_index, slot_len, stagger, prompt_count)
    valid_token = position < length_of(prompt, real_lengths)

    normed = rms_scale(tokens.astype(jnp.float32), attn_gain).astype(jnp.bfloat16)
    share = lax.dynamic_slice_in_dim(normed, tp_place * col_share, col_share, 1)
    part_rows = lax.all_to_all(
        jnp.broadcast_to(share[None], (head_count, token_count, col_share)),
        "seq",
        split_axis=0,
        concat_axis=0,
        tiled=True,
        axis_index_groups=groups,
    ).reshape(part_slots, col_share)
    by_head = jnp.concatenate(
        [
            w.reshape(token_rows, head_count, HEAD).transpose(1, 0, 2)
            for w in (w_query, w_key, w_value)
            for token_rows in (w.shape[0],)
        ],
        axis=2,
    ).astype(jnp.bfloat16)
    head_weights = lax.all_to_all(
        jnp.broadcast_to(by_head[None], (part_count, *by_head.shape)).reshape(
            seq_count, *by_head.shape[1:]
        ),
        "seq",
        split_axis=0,
        concat_axis=0,
        tiled=True,
    ).reshape(model_width, 3 * HEAD)
    out_weights = lax.all_gather(w_out.astype(jnp.bfloat16), "seq", axis=1, tiled=True)
    router_full = lax.all_gather(router.astype(jnp.bfloat16), "seq", axis=0, tiled=True)

    both, last = order_experts(layout_map, expert_gate, expert_up, expert_down)
    both, last, head_weights, part_rows = lax.optimization_barrier(
        (both, last, head_weights, part_rows)
    )

    def to_owner(blocks):
        taken = lax.all_to_all(blocks, "seq", split_axis=0, concat_axis=0, tiled=True)
        taken = taken.reshape(seq_count, local_experts, *blocks.shape[1:])
        return jnp.swapaxes(taken, 0, 1).reshape(local_experts, -1, blocks.shape[2])

    server_both = to_owner(both)
    server_down = to_owner(last)

    product = sum(
        jnp.dot(rows, tp_rows(head_weights, turn), preferred_element_type=jnp.float32)
        for turn, rows in enumerate(tp_blocks(part_rows))
    )
    part_ids = part * part_slots + jnp.arange(part_slots, dtype=jnp.int32)
    part_positions = prompt_split(part_ids, slot_len, stagger, prompt_count)[1]
    half_dim = HEAD // 2
    frequency = ROPE_BASE ** (-jnp.arange(half_dim, dtype=jnp.float32) / half_dim)
    angles = part_positions.astype(jnp.float32)[:, None] * frequency[None, :]
    cosine = jnp.cos(angles)
    sine_part = jnp.sin(angles)
    query_rows = rotate(product[:, :HEAD], cosine, sine_part).astype(jnp.bfloat16)
    key_rows = rotate(product[:, HEAD : 2 * HEAD], cosine, sine_part).astype(jnp.bfloat16)
    value_rows = product[:, 2 * HEAD :].astype(jnp.bfloat16)
    sink = lax.dynamic_slice_in_dim(sink_logits, head, 1, 0)

    def start_state(row_count):
        return (
            jnp.broadcast_to(sink[:, None], (row_count, 1)),
            jnp.ones((row_count, 1), jnp.float32),
            jnp.zeros((row_count, HEAD), jnp.float32),
        )

    if part_count == prompt_count:
        rows = jnp.concatenate([query_rows, key_rows, value_rows], axis=1)
        edge = from_behind(rows[part_slots - stagger :], "seq", head_count)
        rows = jnp.concatenate([edge, rows], axis=0)
        row_ids = part * part_slots - stagger + jnp.arange(part_slots + stagger, dtype=jnp.int32)
        allowed = key_rules(row_ids, row_ids, slot_len, stagger, total_slots, real_lengths)
        _, denominator, accumulated = attend(
            start_state(part_slots + stagger),
            rows[:, :HEAD],
            rows[:, HEAD : 2 * HEAD],
            rows[:, 2 * HEAD :],
            allowed,
        )
        mixed = (accumulated / denominator).astype(jnp.bfloat16)
        edge_back = from_behind(mixed[:stagger], "seq", -head_count)
        tail = jnp.where(part < part_count - 1, edge_back, mixed[part_slots:])
        mixed = jnp.concatenate([mixed[stagger:part_slots], tail], axis=0)
    else:
        softmax_state = attend(
            start_state(part_slots),
            query_rows,
            key_rows,
            value_rows,
            key_rules(part_ids, part_ids, slot_len, stagger, total_slots, real_lengths),
        )
        from_below = from_above = jnp.concatenate([key_rows, value_rows], axis=1)
        for turn in range(1, min(part_count - 1, -(-HALF_WIN // part_slots)) + 1):
            from_below = from_behind(from_below, "seq", head_count)
            from_above = from_behind(from_above, "seq", -head_count)
            reach = turn * part_slots
            key_ids = jnp.concatenate([part_ids - reach, part_ids + reach])
            pair = jnp.concatenate([from_below, from_above], axis=0)
            softmax_state = attend(
                softmax_state,
                query_rows,
                pair[:, :HEAD],
                pair[:, HEAD:],
                key_rules(part_ids, key_ids, slot_len, stagger, total_slots, real_lengths),
            )
        _, denominator, accumulated = softmax_state
        mixed = (accumulated / denominator).astype(jnp.bfloat16)
    attention_result = lax.all_to_all(
        mixed.reshape(head_count, token_count, HEAD),
        "seq",
        split_axis=0,
        concat_axis=0,
        tiled=True,
        axis_index_groups=groups,
    )
    attention_result = jnp.swapaxes(attention_result, 0, 1).reshape(token_count, head_count * HEAD)
    partial_out = jnp.dot(attention_result, out_weights, preferred_element_type=jnp.float32)
    if tp_count == 2:
        mixed_full = partial_out + from_turned(partial_out, "tp", 1)
    else:
        mixed_full = lax.psum(partial_out, "tp")
    full_rows = tokens.astype(jnp.float32) + mixed_full
    outgoing = rms_scale(full_rows, mlp_gain).astype(jnp.bfloat16)
    logits = jnp.dot(outgoing, router_full, preferred_element_type=jnp.float32)
    residual = lax.dynamic_slice_in_dim(full_rows, tp_place * col_share, col_share, 1)
    outgoing_share = lax.dynamic_slice_in_dim(outgoing, tp_place * col_share, col_share, 1)

    expert_ids = jnp.arange(expert_count, dtype=jnp.int32)
    chosen = jnp.any(routes[:, :, None] == expert_ids[None, None, :], axis=1)
    live = chosen & valid_token[:, None]
    earlier = (offsets[:, None] > offsets[None, :]).astype(jnp.bfloat16)
    rank_within = jnp.dot(earlier, live.astype(jnp.bfloat16), preferred_element_type=jnp.float32)
    rank_within = jnp.where(live, rank_within, -1.0)
    columns = jnp.arange(expert_count * capacity, dtype=jnp.int32)
    spread = (columns[None, :] // capacity == expert_ids[:, None]).astype(jnp.bfloat16)
    wanted = (columns % capacity).astype(jnp.float32)
    placed = (
        jnp.dot(rank_within.astype(jnp.bfloat16), spread, preferred_element_type=jnp.float32)
        == wanted[None, :]
    )
    buffer = lax.dot_general(
        placed.astype(jnp.bfloat16),
        outgoing_share,
        (((0,), (0,)), ((), ())),
        preferred_element_type=jnp.float32,
    ).astype(jnp.bfloat16)
    block_rows = local_experts * capacity
    received = lax.all_to_all(
        buffer.reshape(seq_count, block_rows, col_share),
        "seq",
        split_axis=0,
        concat_axis=0,
        tiled=True,
    )
    received = jnp.swapaxes(
        received.reshape(seq_count, local_experts, capacity, col_share), 0, 1
    ).reshape(local_experts, seq_count * capacity, col_share)
    hidden_share = expert_gate.shape[2]
    gate_up = sum(
        jnp.einsum(
            "acd,adf->acf",
            rows,
            lax.dynamic_slice_in_dim(
                server_both, (tp_place + turn) % tp_count * col_share, col_share, 1
            ),
            preferred_element_type=jnp.float32,
        )
        for turn, rows in enumerate(tp_blocks(received))
    )
    hidden_state = (jax.nn.silu(gate_up[..., :hidden_share]) * gate_up[..., hidden_share:]).astype(
        jnp.bfloat16
    )

    def down_columns(block):
        return jnp.einsum(
            "acf,adf->acd",
            hidden_state,
            lax.dynamic_slice_in_dim(server_down, block * col_share, col_share, 1),
            preferred_element_type=jnp.float32,
        ).astype(jnp.bfloat16)

    summed = 0.0
    sent = []
    for turn in range(1, tp_count):
        sent.append(from_turned(down_columns((tp_place - turn) % tp_count), "tp", turn))
    own = lax.optimization_barrier(down_columns(tp_place))
    summed = sum([piece.astype(jnp.float32) for piece in sent], own.astype(jnp.float32))
    summed = jnp.swapaxes(
        summed.astype(jnp.bfloat16).reshape(local_experts, seq_count, capacity, col_share), 0, 1
    ).reshape(seq_count, block_rows, col_share)
    returned = lax.all_to_all(
        summed, "seq", split_axis=0, concat_axis=0, tiled=True
    ).reshape(expert_count * capacity, col_share)

    route_logits = jnp.where(chosen, logits, -jnp.inf)
    route_exp = jnp.exp(route_logits - jnp.max(route_logits, axis=1, keepdims=True))
    route_weight = route_exp / jnp.sum(route_exp, axis=1, keepdims=True)
    route_weight = route_weight * valid_token[:, None]
    weight_parts = parts_of(route_weight, 3)
    stacked = jnp.concatenate(
        [
            jnp.where(
                placed, jnp.dot(piece, spread, preferred_element_type=jnp.float32), 0.0
            ).astype(jnp.bfloat16)
            for piece in weight_parts
        ],
        axis=0,
    )
    mixes = jnp.dot(stacked, returned, preferred_element_type=jnp.float32)
    expert_mix = sum(
        mixes[k * token_count : (k + 1) * token_count] for k in range(len(weight_parts))
    )
    return (residual + expert_mix).astype(jnp.bfloat16)


def solution(mesh):
    placed = (
        P("seq", None),
        P(),
        P(),
        P("seq", "tp"),
        P("seq", "tp"),
        P("seq", "tp"),
        P("tp", "seq"),
        P("tp"),
        P("seq", None),
        P(None, "seq", "tp"),
        P(None, "seq", "tp"),
        P(None, "seq", "tp"),
        P(),
        P(),
        P("seq", None),
    )
    return jax.shard_map(
        shards, mesh=mesh, in_specs=placed, out_specs=P("seq", "tp"), check_vma=False
    )
```

```python
import jax
import jax.numpy as jnp
from jax import lax
from jax.experimental import pallas as pl
from jax.experimental.pallas import tpu as pltpu
from jax.sharding import PartitionSpec as P

HEAD = 128
HALF_WIN = 2048


EPSILON = 1e-05
ROPE_BASE = 50000.0
MASKED = -1e30


def from_behind(value, axis, steps):
    count = lax.axis_size(axis)
    first, last = (max(0, -steps), min(count, count - steps))
    return lax.ppermute(value, axis, [(source, source + steps) for source in range(first, last)])


def from_turned(value, axis, turn):
    count = lax.axis_size(axis)
    return lax.ppermute(value, axis, [((place + turn) % count, place) for place in range(count)])


def swapped(value, axis, mask):
    count = lax.axis_size(axis)
    return lax.ppermute(value, axis, [(place, place ^ mask) for place in range(count)])


def doubled(value, masks, axis):
    turns = [0]
    for mask in masks:
        value = jnp.concatenate([value, swapped(value, "seq", mask)], axis=axis)
        turns = turns + [turn ^ mask for turn in turns]
    return (value, turns)


def masks_below(count, least=1):
    masks = []
    while count > least:
        count //= 2
        masks.append(count)
    return masks


def rms_scale(row_values, gain_vector):
    mean_square = jnp.mean(row_values * row_values, axis=-1, keepdims=True)
    return row_values * lax.rsqrt(mean_square + EPSILON) * gain_vector


def rotate(rows, cosine, sine_part):
    half_dim = rows.shape[-1] // 2
    first_half = rows[:, :half_dim]
    second_half = rows[:, half_dim:]
    return jnp.concatenate(
        [
            first_half * cosine - second_half * sine_part,
            second_half * cosine + first_half * sine_part,
        ],
        axis=-1,
    )


def length_of(prompt, real_lengths):
    one_hot = prompt[:, None] == jnp.arange(real_lengths.shape[0], dtype=jnp.int32)[None, :]
    return jnp.sum(jnp.where(one_hot, real_lengths[None, :], 0), axis=1)


def prompt_split(slot_ids, slot_len, stagger, prompt_count):
    prompt = jnp.minimum((slot_ids + stagger) // slot_len, prompt_count - 1)
    start = jnp.maximum(prompt * slot_len - stagger, 0)
    return (prompt, slot_ids - start)


def key_rules(query_ids, key_ids, slot_len, stagger, total_slots, real_lengths):
    prompt_count = real_lengths.shape[0]
    key_prompt, key_pos = prompt_split(key_ids, slot_len, stagger, prompt_count)
    query_prompt = prompt_split(query_ids, slot_len, stagger, prompt_count)[0]
    inside = (key_ids >= 0) & (key_ids < total_slots)
    key_live = inside & (key_pos < length_of(key_prompt, real_lengths))
    same_prompt = query_prompt[:, None] == key_prompt[None, :]
    nearby = jnp.abs(query_ids[:, None] - key_ids[None, :]) < HALF_WIN
    return same_prompt & nearby & key_live[None, :]


def parts_of(values, count):
    rest = values
    pieces = []
    for _ in range(count):
        piece = lax.reduce_precision(rest, 8, 7)
        rest = rest - piece
        pieces.append(piece.astype(jnp.bfloat16))
    return pieces


def attend(softmax_state, query_rows, key_rows, value_rows, allowed):
    running_max, denominator, accumulated = softmax_state
    scores = lax.dot_general(
        query_rows, key_rows, (((1,), (1,)), ((), ())), preferred_element_type=jnp.float32
    ) * HEAD ** (-0.5)
    scores = jnp.where(allowed, scores, MASKED)
    new_max = jnp.maximum(running_max, jnp.max(scores, axis=1, keepdims=True))
    rescale = jnp.exp(running_max - new_max)
    weight_tensors = jnp.exp(scores - new_max)
    denominator = denominator * rescale + jnp.sum(weight_tensors, axis=1, keepdims=True)
    high, low = parts_of(weight_tensors, 2)
    accumulated = (
        accumulated * rescale
        + jnp.dot(high, value_rows, preferred_element_type=jnp.float32)
        + jnp.dot(low, value_rows, preferred_element_type=jnp.float32)
    )
    return (new_max, denominator, accumulated)


def order_body(order_ref, gate_ref, up_ref, down_ref, both_ref, last_ref):
    width = gate_ref.shape[2]
    both_ref[0, :, :width] = gate_ref[0].astype(jnp.bfloat16)
    both_ref[0, :, width:] = up_ref[0].astype(jnp.bfloat16)
    last_ref[0] = down_ref[0].astype(jnp.bfloat16)


def order_experts(layout_map, gate, up, down):
    count, rows, width = gate.shape
    source = pl.BlockSpec((1, rows, width), lambda place, order: (order[place], 0, 0))
    return pl.pallas_call(
        order_body,
        grid_spec=pltpu.PrefetchScalarGridSpec(
            num_scalar_prefetch=1,
            grid=(count,),
            in_specs=[source, source, source],
            out_specs=[
                pl.BlockSpec((1, rows, 2 * width), lambda place, order: (place, 0, 0)),
                pl.BlockSpec((1, rows, width), lambda place, order: (place, 0, 0)),
            ],
        ),
        out_shape=[
            jax.ShapeDtypeStruct((count, rows, 2 * width), jnp.bfloat16),
            jax.ShapeDtypeStruct((count, rows, width), jnp.bfloat16),
        ],
        name="order_experts",
    )(layout_map, gate, up, down)


def shards(
    tokens,
    attn_gain,
    mlp_gain,
    w_query,
    w_key,
    w_value,
    w_out,
    sink_logits,
    router,
    expert_gate,
    expert_up,
    expert_down,
    layout_map,
    real_lengths,
    routes,
):
    token_count, model_width = tokens.shape
    seq_count = lax.axis_size("seq")
    tp_count = lax.axis_size("tp")
    expert_count = router.shape[1]
    route_count = routes.shape[1]
    head_count = sink_logits.shape[0]
    col_share = model_width // tp_count
    total_slots = token_count * seq_count
    prompt_count = real_lengths.shape[0]
    slot_len = total_slots // prompt_count
    stagger = token_count // 2
    capacity = max(2, min(token_count, 9 * token_count * route_count // (8 * expert_count)))
    part_count = seq_count // head_count
    part_slots = head_count * token_count
    local_experts = expert_count // seq_count
    seq_place = lax.axis_index("seq")
    tp_place = lax.axis_index("tp")
    part = seq_place // head_count
    head = seq_place % head_count

    def tp_blocks(value):
        return [value] + [from_turned(value, "tp", turn) for turn in range(1, tp_count)]

    def tp_rows(weights, turn):
        block = (tp_place + turn) % tp_count
        return lax.dynamic_slice_in_dim(weights, block * col_share, col_share, 0)

    offsets = jnp.arange(token_count, dtype=jnp.int32)
    turns = jnp.arange(head_count, dtype=jnp.int32)
    group_masks = masks_below(head_count)
    part_masks = masks_below(seq_count, head_count)

    by_head = jnp.concatenate(
        [
            w.reshape(w.shape[0], head_count, HEAD).transpose(1, 0, 2)
            for w in (w_query, w_key, w_value)
        ],
        axis=2,
    ).astype(jnp.bfloat16)
    head_weights = lax.all_to_all(
        jnp.broadcast_to(by_head[None], (part_count, *by_head.shape)).reshape(
            seq_count, *by_head.shape[1:]
        ),
        "seq",
        split_axis=0,
        concat_axis=0,
        tiled=True,
    ).reshape(model_width, 3 * HEAD)

    normed = rms_scale(tokens.astype(jnp.float32), attn_gain).astype(jnp.bfloat16)
    share = lax.dynamic_slice_in_dim(normed, tp_place * col_share, col_share, 1)
    first_rows, first_turns = doubled(share[None], group_masks[:1], 0)
    pieces = []
    for piece, masks in (
        (first_rows[:, :, : col_share // 2], group_masks[1:]),
        (first_rows[:, :, col_share // 2 :], group_masks[1:][::-1]),
    ):
        rows, row_turns = doubled(piece, masks, 0)
        known = []
        for turn in row_turns:
            known.extend([first ^ turn for first in first_turns])
        pieces.append(jnp.concatenate([rows[known.index(m)] for m in range(head_count)], axis=0))
    part_rows = jnp.concatenate(pieces, axis=1)

    both, last = order_experts(layout_map, expert_gate, expert_up, expert_down)
    both, last, head_weights = lax.optimization_barrier((both, last, head_weights))

    def to_owner(blocks):
        taken = lax.all_to_all(blocks, "seq", split_axis=0, concat_axis=0, tiled=True)
        taken = taken.reshape(seq_count, local_experts, *blocks.shape[1:])
        return jnp.swapaxes(taken, 0, 1).reshape(local_experts, -1, blocks.shape[2])

    server_both = to_owner(both)
    server_down = to_owner(last)

    out_local = jnp.concatenate([w_out, router.T], axis=0).astype(jnp.bfloat16)
    out_all, out_turns = doubled(out_local, masks_below(seq_count), 1)
    width = out_local.shape[1]
    bits = len(out_turns).bit_length() - 1

    def in_order(value):
        blocks = []
        for place in range(seq_count):
            turn = seq_place ^ place
            index = sum(((turn >> k) & 1) << (bits - 1 - k) for k in range(bits))
            blocks.append(lax.dynamic_slice_in_dim(value, index * width, width, 1))
        return jnp.concatenate(blocks, axis=1)

    all_routes, part_turns = doubled(routes[None], part_masks, 0)
    expert_ids = jnp.arange(expert_count, dtype=jnp.int32)
    block_rows = local_experts * capacity
    columns = jnp.arange(head_count * block_rows, dtype=jnp.int32)
    column_owner = part * head_count + (head ^ (columns // block_rows))
    column_expert = column_owner * local_experts + columns // capacity % local_experts
    spread = (column_expert[None, :] == expert_ids[:, None]).astype(jnp.bfloat16)
    wanted = (columns % capacity).astype(jnp.float32)
    earlier = (offsets[:, None] > offsets[None, :]).astype(jnp.bfloat16)

    def routing(turn, own_routes):
        ids = (seq_place ^ turn) * token_count + offsets
        prompt, position = prompt_split(ids, slot_len, stagger, prompt_count)
        valid_token = position < length_of(prompt, real_lengths)
        chosen = jnp.any(own_routes[:, :, None] == expert_ids[None, None, :], axis=1)
        live = chosen & valid_token[:, None]
        rank = jnp.dot(earlier, live.astype(jnp.bfloat16), preferred_element_type=jnp.float32)
        rank = jnp.where(live, rank, -1.0).astype(jnp.bfloat16)
        placed = jnp.dot(rank, spread, preferred_element_type=jnp.float32) == wanted[None, :]
        return (chosen, valid_token, placed)

    routings = [routing(turn, all_routes[k]) for k, turn in enumerate(part_turns)]
    chosen, valid_token, _ = routings[0]

    product = sum(
        jnp.dot(rows, tp_rows(head_weights, turn), preferred_element_type=jnp.float32)
        for turn, rows in enumerate(tp_blocks(part_rows))
    )
    part_ids = (part * head_count + (head ^ turns))[:, None] * token_count + offsets[None, :]
    part_ids = part_ids.reshape(-1)
    part_positions = prompt_split(part_ids, slot_len, stagger, prompt_count)[1]
    half_dim = HEAD // 2
    frequency = ROPE_BASE ** (-jnp.arange(half_dim, dtype=jnp.float32) / half_dim)
    angles = part_positions.astype(jnp.float32)[:, None] * frequency[None, :]
    cosine = jnp.cos(angles)
    sine_part = jnp.sin(angles)
    query_rows = rotate(product[:, :HEAD], cosine, sine_part).astype(jnp.bfloat16)
    key_rows = rotate(product[:, HEAD : 2 * HEAD], cosine, sine_part).astype(jnp.bfloat16)
    value_rows = product[:, 2 * HEAD :].astype(jnp.bfloat16)
    sink = lax.dynamic_slice_in_dim(sink_logits, head, 1, 0)

    def start_state(row_count):
        return (
            jnp.broadcast_to(sink[:, None], (row_count, 1)),
            jnp.ones((row_count, 1), jnp.float32),
            jnp.zeros((row_count, HEAD), jnp.float32),
        )

    if part_count == prompt_count:
        rows = jnp.concatenate([query_rows, key_rows, value_rows], axis=1)
        edge_start = (head ^ (head_count - 1)) * token_count + token_count - stagger
        edge = from_behind(
            lax.dynamic_slice_in_dim(rows, edge_start, stagger, 0), "seq", head_count
        )
        rows = jnp.concatenate([rows, edge], axis=0)
        edge_ids = part * part_slots - stagger + jnp.arange(stagger, dtype=jnp.int32)
        row_ids = jnp.concatenate([part_ids, edge_ids])
        allowed = key_rules(row_ids, row_ids, slot_len, stagger, total_slots, real_lengths)
        _, denominator, accumulated = attend(
            start_state(part_slots + stagger),
            rows[:, :HEAD],
            rows[:, HEAD : 2 * HEAD],
            rows[:, 2 * HEAD :],
            allowed,
        )
        mixed = (accumulated / denominator).astype(jnp.bfloat16)
        edge_back = from_behind(mixed[part_slots:], "seq", -head_count)
        mixed = mixed[:part_slots]
        kept = lax.dynamic_slice_in_dim(mixed, edge_start, stagger, 0)
        mixed = lax.dynamic_update_slice_in_dim(
            mixed, jnp.where(part < part_count - 1, edge_back, kept), edge_start, 0
        )
    else:
        softmax_state = attend(
            start_state(part_slots),
            query_rows,
            key_rows,
            value_rows,
            key_rules(part_ids, part_ids, slot_len, stagger, total_slots, real_lengths),
        )
        from_below = from_above = jnp.concatenate([key_rows, value_rows], axis=1)
        for turn in range(1, min(part_count - 1, -(-HALF_WIN // part_slots)) + 1):
            from_below = from_behind(from_below, "seq", head_count)
            from_above = from_behind(from_above, "seq", -head_count)
            reach = turn * part_slots
            key_ids = jnp.concatenate([part_ids - reach, part_ids + reach])
            pair = jnp.concatenate([from_below, from_above], axis=0)
            softmax_state = attend(
                softmax_state,
                query_rows,
                pair[:, :HEAD],
                pair[:, HEAD:],
                key_rules(part_ids, key_ids, slot_len, stagger, total_slots, real_lengths),
            )
        _, denominator, accumulated = softmax_state
        mixed = (accumulated / denominator).astype(jnp.bfloat16)
    blocks = mixed.reshape(head_count, token_count, HEAD)
    heads = jnp.stack(
        [blocks[0]] + [swapped(blocks[m], "seq", m) for m in range(1, head_count)]
    )
    attention_result = jnp.concatenate(
        [lax.dynamic_index_in_dim(heads, head ^ h, 0, keepdims=False) for h in range(head_count)],
        axis=1,
    )
    partial_out = jnp.dot(
        attention_result, out_all[: head_count * HEAD], preferred_element_type=jnp.float32
    )
    if tp_count == 2:
        mixed_full = partial_out + from_turned(partial_out, "tp", 1)
    else:
        mixed_full = lax.psum(partial_out, "tp")
    full_rows = tokens.astype(jnp.float32) + in_order(mixed_full)
    outgoing = rms_scale(full_rows, mlp_gain).astype(jnp.bfloat16)
    residual = lax.dynamic_slice_in_dim(full_rows, tp_place * col_share, col_share, 1)
    outgoing_share = lax.dynamic_slice_in_dim(outgoing, tp_place * col_share, col_share, 1)

    all_rows, _ = doubled(outgoing_share[None], part_masks, 0)
    buffer = jnp.stack(
        [
            lax.dot_general(
                placed.astype(jnp.bfloat16),
                all_rows[k],
                (((0,), (0,)), ((), ())),
                preferred_element_type=jnp.float32,
            )
            .astype(jnp.bfloat16)
            .reshape(head_count, block_rows, col_share)
            for k, (_, _, placed) in enumerate(routings)
        ],
        axis=1,
    )
    received = jnp.stack(
        [buffer[0]] + [swapped(buffer[m], "seq", m) for m in range(1, head_count)]
    )
    row_count = head_count * part_count * capacity
    received = jnp.moveaxis(
        received.reshape(head_count, part_count, local_experts, capacity, col_share), 2, 0
    ).reshape(local_experts, row_count, col_share)
    hidden_share = expert_gate.shape[2]
    gate_up = sum(
        jnp.einsum(
            "acd,adf->acf",
            rows,
            lax.dynamic_slice_in_dim(
                server_both, (tp_place + turn) % tp_count * col_share, col_share, 1
            ),
            preferred_element_type=jnp.float32,
        )
        for turn, rows in enumerate(tp_blocks(received))
    )
    hidden_state = (jax.nn.silu(gate_up[..., :hidden_share]) * gate_up[..., hidden_share:]).astype(
        jnp.bfloat16
    )

    def down_columns(block):
        return jnp.einsum(
            "acf,adf->acd",
            hidden_state,
            lax.dynamic_slice_in_dim(server_down, block * col_share, col_share, 1),
            preferred_element_type=jnp.float32,
        ).astype(jnp.bfloat16)

    sent = [
        from_turned(down_columns((tp_place - turn) % tp_count), "tp", turn)
        for turn in range(1, tp_count)
    ]
    own = lax.optimization_barrier(down_columns(tp_place))
    summed = sum([piece.astype(jnp.float32) for piece in sent], own.astype(jnp.float32))
    summed = jnp.moveaxis(
        summed.astype(jnp.bfloat16).reshape(
            local_experts, head_count, part_count, capacity, col_share
        ),
        0,
        2,
    ).reshape(head_count, part_count, block_rows, col_share)

    logits = lax.dot_general(
        outgoing,
        in_order(out_all[head_count * HEAD :]),
        (((1,), (1,)), ((), ())),
        preferred_element_type=jnp.float32,
    )
    route_logits = jnp.where(chosen, logits, -jnp.inf)
    route_exp = jnp.exp(route_logits - jnp.max(route_logits, axis=1, keepdims=True))
    route_weight = route_exp / jnp.sum(route_exp, axis=1, keepdims=True)
    route_weight = route_weight * valid_token[:, None]
    all_weights, _ = doubled(route_weight[None], part_masks, 0)

    def weighted(k, rows):
        placed = routings[k][2]
        stacked = jnp.concatenate(
            [
                jnp.where(
                    placed, jnp.dot(piece, spread, preferred_element_type=jnp.float32), 0.0
                ).astype(jnp.bfloat16)
                for piece in parts_of(all_weights[k], 3)
            ],
            axis=0,
        )
        mixes = jnp.dot(stacked, rows, preferred_element_type=jnp.float32)
        return sum(mixes[k * token_count : (k + 1) * token_count] for k in range(3))

    def back(blocks):
        return jnp.stack(
            [blocks[0]] + [swapped(blocks[m], "seq", m) for m in range(1, head_count)]
        )

    others = back(summed[:, 1:])
    expert_mix = 0.0
    for k, turn in enumerate(part_turns[1:]):
        mix = weighted(k + 1, others[:, k].reshape(-1, col_share))
        expert_mix = expert_mix + swapped(mix, "seq", turn)
    own_mix = weighted(0, back(summed[:, 0]).reshape(-1, col_share))
    return (residual + (expert_mix + own_mix)).astype(jnp.bfloat16)


def solution(mesh):
    placed = (
        P("seq", None),
        P(),
        P(),
        P("seq", "tp"),
        P("seq", "tp"),
        P("seq", "tp"),
        P("tp", "seq"),
        P("tp"),
        P("seq", None),
        P(None, "seq", "tp"),
        P(None, "seq", "tp"),
        P(None, "seq", "tp"),
        P(),
        P(),
        P("seq", None),
    )
    return jax.shard_map(
        shards, mesh=mesh, in_specs=placed, out_specs=P("seq", "tp"), check_vma=False
    )
```

```python
import jax
import jax.numpy as jnp
from jax import lax
from jax.experimental import pallas as pl
from jax.experimental.pallas import tpu as pltpu
from jax.sharding import PartitionSpec as P

HEAD = 128
HALF_WIN = 2048


EPSILON = 1e-05
ROPE_BASE = 50000.0
MASKED = -1e30
SMALL = pl.CostEstimate(flops=1, bytes_accessed=1, transcendentals=1)


def from_behind(value, axis, steps):
    count = lax.axis_size(axis)
    first, last = (max(0, -steps), min(count, count - steps))
    return lax.ppermute(value, axis, [(source, source + steps) for source in range(first, last)])


def from_turned(value, axis, turn):
    count = lax.axis_size(axis)
    return lax.ppermute(value, axis, [((place + turn) % count, place) for place in range(count)])


def swapped(value, axis, mask):
    count = lax.axis_size(axis)
    return lax.ppermute(value, axis, [(place, place ^ mask) for place in range(count)])


def doubled(value, masks, axis):
    turns = [0]
    for mask in masks:
        value = jnp.concatenate([value, swapped(value, "seq", mask)], axis=axis)
        turns = turns + [turn ^ mask for turn in turns]
    return (value, turns)


def masks_below(count, least=1):
    masks = []
    while count > least:
        count //= 2
        masks.append(count)
    return masks


def rms_scale(row_values, gain_vector):
    mean_square = jnp.mean(row_values * row_values, axis=-1, keepdims=True)
    return row_values * lax.rsqrt(mean_square + EPSILON) * gain_vector


def rotate(rows, cosine, sine_part):
    half_dim = rows.shape[-1] // 2
    first_half = rows[:, :half_dim]
    second_half = rows[:, half_dim:]
    return jnp.concatenate(
        [
            first_half * cosine - second_half * sine_part,
            second_half * cosine + first_half * sine_part,
        ],
        axis=-1,
    )


def length_of(prompt, real_lengths):
    one_hot = prompt[:, None] == jnp.arange(real_lengths.shape[0], dtype=jnp.int32)[None, :]
    return jnp.sum(jnp.where(one_hot, real_lengths[None, :], 0), axis=1)


def prompt_split(slot_ids, slot_len, stagger, prompt_count):
    prompt = jnp.minimum((slot_ids + stagger) // slot_len, prompt_count - 1)
    start = jnp.maximum(prompt * slot_len - stagger, 0)
    return (prompt, slot_ids - start)


def key_rules(query_ids, key_ids, slot_len, stagger, total_slots, real_lengths):
    prompt_count = real_lengths.shape[0]
    key_prompt, key_pos = prompt_split(key_ids, slot_len, stagger, prompt_count)
    query_prompt = prompt_split(query_ids, slot_len, stagger, prompt_count)[0]
    inside = (key_ids >= 0) & (key_ids < total_slots)
    key_live = inside & (key_pos < length_of(key_prompt, real_lengths))
    same_prompt = query_prompt[:, None] == key_prompt[None, :]
    nearby = jnp.abs(query_ids[:, None] - key_ids[None, :]) < HALF_WIN
    return same_prompt & nearby & key_live[None, :]


def parts_of(values, count):
    rest = values
    pieces = []
    for _ in range(count):
        piece = lax.reduce_precision(rest, 8, 7)
        rest = rest - piece
        pieces.append(piece.astype(jnp.bfloat16))
    return pieces


def attend(softmax_state, query_rows, key_rows, value_rows, allowed):
    running_max, denominator, accumulated = softmax_state
    scores = lax.dot_general(
        query_rows, key_rows, (((1,), (1,)), ((), ())), preferred_element_type=jnp.float32
    ) * HEAD ** (-0.5)
    scores = jnp.where(allowed, scores, MASKED)
    new_max = jnp.maximum(running_max, jnp.max(scores, axis=1, keepdims=True))
    rescale = jnp.exp(running_max - new_max)
    weight_tensors = jnp.exp(scores - new_max)
    denominator = denominator * rescale + jnp.sum(weight_tensors, axis=1, keepdims=True)
    high, low = parts_of(weight_tensors, 2)
    accumulated = (
        accumulated * rescale
        + jnp.dot(high, value_rows, preferred_element_type=jnp.float32)
        + jnp.dot(low, value_rows, preferred_element_type=jnp.float32)
    )
    return (new_max, denominator, accumulated)


def order_body(order_ref, gate_ref, up_ref, down_ref, out_ref):
    width = gate_ref.shape[2]
    for k, source in enumerate((gate_ref, up_ref, down_ref)):
        out_ref[:, :, k * width : (k + 1) * width] = source[...].astype(jnp.bfloat16)


def order_experts(layout_map, gate, up, down):
    count, rows, width = gate.shape
    source = pl.BlockSpec((1, rows, width), lambda place, order: (order[place], 0, 0))
    return pl.pallas_call(
        order_body,
        grid_spec=pltpu.PrefetchScalarGridSpec(
            num_scalar_prefetch=1,
            grid=(count,),
            in_specs=[source, source, source],
            out_specs=pl.BlockSpec((1, rows, 3 * width), lambda place, order: (place, 0, 0)),
        ),
        out_shape=jax.ShapeDtypeStruct((count, rows, 3 * width), jnp.bfloat16),
        name="order_experts",
    )(layout_map, gate, up, down)


def pack_body(query_ref, key_ref, value_ref, out_ref):
    out_ref[0, :, :HEAD] = query_ref[...].astype(jnp.bfloat16)
    out_ref[0, :, HEAD : 2 * HEAD] = key_ref[...].astype(jnp.bfloat16)
    out_ref[0, :, 2 * HEAD :] = value_ref[...].astype(jnp.bfloat16)


def pack_heads(w_query, w_key, w_value, copies):
    rows, width = w_query.shape
    heads = width // HEAD
    source = pl.BlockSpec((rows, HEAD), lambda place: (0, place % heads))
    return pl.pallas_call(
        pack_body,
        grid=(copies * heads,),
        in_specs=[source, source, source],
        out_specs=pl.BlockSpec((1, rows, 3 * HEAD), lambda place: (place, 0, 0)),
        out_shape=jax.ShapeDtypeStruct((copies * heads, rows, 3 * HEAD), jnp.bfloat16),
        name="pack_heads",
    )(w_query, w_key, w_value)


def project_body(turn_count, share, start_ref, *refs):
    rows, (weight_ref, cosine_ref, sine_ref, out_ref) = (refs[:turn_count], refs[turn_count:])
    product = 0.0
    for turn in range(turn_count):
        first = pl.multiple_of(start_ref[turn], share)
        product = product + jnp.dot(
            rows[turn][...], weight_ref[pl.ds(first, share), :], preferred_element_type=jnp.float32
        )
    cosine, sine_part = (cosine_ref[...], sine_ref[...])
    out_ref[:, :HEAD] = rotate(product[:, :HEAD], cosine, sine_part).astype(jnp.bfloat16)
    out_ref[:, HEAD : 2 * HEAD] = rotate(
        product[:, HEAD : 2 * HEAD], cosine, sine_part
    ).astype(jnp.bfloat16)
    out_ref[:, 2 * HEAD :] = product[:, 2 * HEAD :].astype(jnp.bfloat16)


def project(starts, row_blocks, weights, cosine, sine_part):
    row_count, share = row_blocks[0].shape
    step = row_count // 4
    whole = pl.BlockSpec(weights.shape, lambda place, starts: (0, 0))
    angle = pl.BlockSpec((step, cosine.shape[1]), lambda place, starts: (place, 0))
    return pl.pallas_call(
        lambda *refs: project_body(len(row_blocks), share, *refs),
        grid_spec=pltpu.PrefetchScalarGridSpec(
            num_scalar_prefetch=1,
            grid=(4,),
            in_specs=[pl.BlockSpec((step, share), lambda place, starts: (place, 0))]
            * len(row_blocks)
            + [whole, angle, angle],
            out_specs=pl.BlockSpec((step, weights.shape[1]), lambda place, starts: (place, 0)),
        ),
        out_shape=jax.ShapeDtypeStruct((row_count, weights.shape[1]), jnp.bfloat16),
        compiler_params=pltpu.CompilerParams(vmem_limit_bytes=32 * 2**20),
        cost_estimate=SMALL,
        name="project",
    )(starts, *row_blocks, weights, cosine, sine_part)


def attend_body(sink_ref, query_prompt_ref, key_prompt_ref, query_ref, key_ref, value_ref, out_ref):
    sink = sink_ref[0]
    scores = lax.dot_general(
        query_ref[...],
        key_ref[...],
        (((1,), (1,)), ((), ())),
        preferred_element_type=jnp.float32,
    ) * HEAD ** (-0.5)
    scores = jnp.where(query_prompt_ref[...] == key_prompt_ref[...], scores, MASKED)
    top = jnp.maximum(sink, jnp.max(scores, axis=1, keepdims=True))
    weights = jnp.exp(scores - top)
    denominator = jnp.exp(sink - top) + jnp.sum(weights, axis=1, keepdims=True)
    high = weights.astype(jnp.bfloat16)
    low = (weights - high.astype(jnp.float32)).astype(jnp.bfloat16)
    values = value_ref[...]
    mix = jnp.dot(high, values, preferred_element_type=jnp.float32) + jnp.dot(
        low, values, preferred_element_type=jnp.float32
    )
    out_ref[...] = (mix / denominator).astype(jnp.bfloat16)


def attend_once(sink, query_prompt, key_prompt, rows):
    row_count = rows.shape[0]
    steps = 4 if row_count % 64 == 0 else 1
    step = row_count // steps
    return pl.pallas_call(
        attend_body,
        grid=(steps,),
        in_specs=[
            pl.BlockSpec(memory_space=pltpu.SMEM),
            pl.BlockSpec((step, 1), lambda place: (place, 0)),
            pl.BlockSpec((1, row_count), lambda place: (0, 0)),
            pl.BlockSpec((step, HEAD), lambda place: (place, 0)),
            pl.BlockSpec((row_count, HEAD), lambda place: (0, 1)),
            pl.BlockSpec((row_count, HEAD), lambda place: (0, 2)),
        ],
        out_specs=pl.BlockSpec((step, HEAD), lambda place: (place, 0)),
        out_shape=jax.ShapeDtypeStruct((row_count, HEAD), jnp.bfloat16),
        compiler_params=pltpu.CompilerParams(vmem_limit_bytes=32 * 2**20),
        cost_estimate=SMALL,
        name="attend_once",
    )(sink, query_prompt[:, None], key_prompt[None, :], rows, rows, rows)


def settle_body(part_count, width, place_ref, *refs):
    pieces = refs[:part_count]
    token_ref, gain_ref, router_ref, full_ref, outgoing_ref, logit_ref, router_all = refs[
        part_count:
    ]
    count = full_ref.shape[1] // width
    for place in range(count):
        first = pl.multiple_of(place_ref[place] * width, width)
        block = sum(piece[:, pl.ds(first, width)] for piece in pieces)
        here = slice(place * width, (place + 1) * width)
        full_ref[:, here] = token_ref[:, here].astype(jnp.float32) + block
        router_all[:, here] = router_ref[:, pl.ds(first, width)]
    outgoing = rms_scale(full_ref[...], gain_ref[...]).astype(jnp.bfloat16)
    outgoing_ref[...] = outgoing
    logit_ref[...] = lax.dot_general(
        outgoing,
        router_all[...],
        (((1,), (1,)), ((), ())),
        preferred_element_type=jnp.float32,
    )


def settle(places, pieces, tokens, gain, router, width):
    rows, columns = tokens.shape
    vmem = pl.BlockSpec(memory_space=pltpu.VMEM)
    return pl.pallas_call(
        lambda *refs: settle_body(len(pieces), width, *refs),
        in_specs=[pl.BlockSpec(memory_space=pltpu.SMEM)] + [vmem] * (len(pieces) + 3),
        out_specs=[vmem] * 3,
        out_shape=[
            jax.ShapeDtypeStruct((rows, columns), jnp.float32),
            jax.ShapeDtypeStruct((rows, columns), jnp.bfloat16),
            jax.ShapeDtypeStruct((rows, router.shape[0]), jnp.float32),
        ],
        scratch_shapes=[pltpu.VMEM(router.shape, jnp.bfloat16)],
        compiler_params=pltpu.CompilerParams(vmem_limit_bytes=32 * 2**20),
        cost_estimate=SMALL,
        name="settle",
    )(places, *pieces, tokens, gain[None, :], router)


def shards(
    tokens,
    attn_gain,
    mlp_gain,
    w_query,
    w_key,
    w_value,
    w_out,
    sink_logits,
    router,
    expert_gate,
    expert_up,
    expert_down,
    layout_map,
    real_lengths,
    routes,
):
    token_count, model_width = tokens.shape
    seq_count = lax.axis_size("seq")
    tp_count = lax.axis_size("tp")
    expert_count = router.shape[1]
    route_count = routes.shape[1]
    head_count = sink_logits.shape[0]
    col_share = model_width // tp_count
    total_slots = token_count * seq_count
    prompt_count = real_lengths.shape[0]
    slot_len = total_slots // prompt_count
    stagger = token_count // 2
    capacity = max(2, min(token_count, 9 * token_count * route_count // (8 * expert_count)))
    part_count = seq_count // head_count
    part_slots = head_count * token_count
    local_experts = expert_count // seq_count
    seq_place = lax.axis_index("seq")
    tp_place = lax.axis_index("tp")
    part = seq_place // head_count
    head = seq_place % head_count

    def tp_blocks(value):
        return [value] + [from_turned(value, "tp", turn) for turn in range(1, tp_count)]

    offsets = jnp.arange(token_count, dtype=jnp.int32)
    turns = jnp.arange(head_count, dtype=jnp.int32)
    group_masks = masks_below(head_count)
    groups = [[first + k for k in range(head_count)] for first in range(0, seq_count, head_count)]
    part_masks = masks_below(seq_count, head_count)

    head_weights = lax.all_to_all(
        pack_heads(w_query, w_key, w_value, part_count),
        "seq",
        split_axis=0,
        concat_axis=0,
        tiled=True,
    ).reshape(model_width, 3 * HEAD)

    normed = rms_scale(tokens.astype(jnp.float32), attn_gain).astype(jnp.bfloat16)
    share = lax.dynamic_slice_in_dim(normed, tp_place * col_share, col_share, 1)
    first_rows, first_turns = doubled(share[None], group_masks[:1], 0)
    pieces = []
    for piece, masks in (
        (first_rows[:, :, : col_share // 2], group_masks[1:]),
        (first_rows[:, :, col_share // 2 :], group_masks[1:][::-1]),
    ):
        rows, row_turns = doubled(piece, masks, 0)
        known = []
        for turn in row_turns:
            known.extend([first ^ turn for first in first_turns])
        pieces.append(jnp.concatenate([rows[known.index(m)] for m in range(head_count)], axis=0))
    part_rows = jnp.concatenate(pieces, axis=1)

    own_blocks = order_experts(layout_map, expert_gate, expert_up, expert_down)
    own_blocks, head_weights = lax.optimization_barrier((own_blocks, head_weights))

    def to_owner(blocks):
        taken = lax.all_to_all(blocks, "seq", split_axis=0, concat_axis=0, tiled=True)
        taken = taken.reshape(seq_count, local_experts, *blocks.shape[1:])
        return jnp.swapaxes(taken, 0, 1).reshape(local_experts, -1, blocks.shape[2])

    server = to_owner(own_blocks)

    out_local = jnp.concatenate([w_out, router.T], axis=0).astype(jnp.bfloat16)
    width = out_local.shape[1]
    out_rows = out_local.shape[0] // 32 * 16
    seq_masks = masks_below(seq_count)
    bits = len(seq_masks)
    out_some, out_turns = doubled(out_local, seq_masks[:-2], 1)
    out_halves = []
    for piece, (second, third) in (
        (out_some[:out_rows], seq_masks[-2:]),
        (out_some[out_rows:], seq_masks[-2:][::-1]),
    ):
        piece, _ = doubled(piece, [second], 1)
        out_halves.append((piece, swapped(piece, "seq", third)))

    def times_columns(rows, half, first_row, last_row):
        own, other = (piece[first_row:last_row] for piece in out_halves[half])
        value = jnp.concatenate(
            [
                jnp.dot(rows, piece, preferred_element_type=jnp.float32)
                if rows is not None
                else piece
                for piece in (own, other)
            ],
            axis=1,
        )
        if half == 0:
            return value
        span = len(out_turns) * width
        quarters = [value[:, k * span : (k + 1) * span] for k in range(4)]
        return jnp.concatenate([quarters[k] for k in (0, 2, 1, 3)], axis=1)

    turn_places = seq_place ^ jnp.arange(seq_count, dtype=jnp.int32)
    out_places = sum(((turn_places >> k) & 1) << (bits - 1 - k) for k in range(bits))

    all_routes, part_turns = doubled(routes[None], part_masks, 0)
    expert_ids = jnp.arange(expert_count, dtype=jnp.int32)
    block_rows = local_experts * capacity
    columns = jnp.arange(head_count * block_rows, dtype=jnp.int32)
    column_owner = part * head_count + (head ^ (columns // block_rows))
    column_expert = column_owner * local_experts + columns // capacity % local_experts
    spread = (column_expert[None, :] == expert_ids[:, None]).astype(jnp.bfloat16)
    wanted = (columns % capacity).astype(jnp.float32)
    earlier = (offsets[:, None] > offsets[None, :]).astype(jnp.bfloat16)

    def routing(turn, own_routes):
        ids = (seq_place ^ turn) * token_count + offsets
        prompt, position = prompt_split(ids, slot_len, stagger, prompt_count)
        valid_token = position < length_of(prompt, real_lengths)
        chosen = jnp.any(own_routes[:, :, None] == expert_ids[None, None, :], axis=1)
        live = chosen & valid_token[:, None]
        rank = jnp.dot(earlier, live.astype(jnp.bfloat16), preferred_element_type=jnp.float32)
        rank = jnp.where(live, rank, -1.0).astype(jnp.bfloat16)
        placed = jnp.dot(rank, spread, preferred_element_type=jnp.float32) == wanted[None, :]
        return (chosen, valid_token, placed)

    routings = [routing(turn, all_routes[k]) for k, turn in enumerate(part_turns)]
    chosen, valid_token, _ = routings[0]

    part_ids = (part * head_count + (head ^ turns))[:, None] * token_count + offsets[None, :]
    part_ids = part_ids.reshape(-1)
    part_positions = prompt_split(part_ids, slot_len, stagger, prompt_count)[1]
    half_dim = HEAD // 2
    frequency = ROPE_BASE ** (-jnp.arange(half_dim, dtype=jnp.float32) / half_dim)
    angles = part_positions.astype(jnp.float32)[:, None] * frequency[None, :]
    cosine = jnp.cos(angles)
    sine_part = jnp.sin(angles)
    starts = (tp_place + jnp.arange(tp_count, dtype=jnp.int32)) % tp_count * col_share
    rows = project(starts, tp_blocks(part_rows), head_weights, cosine, sine_part)
    sink = lax.dynamic_slice_in_dim(sink_logits, head, 1, 0)

    def start_state(row_count):
        return (
            jnp.broadcast_to(sink[:, None], (row_count, 1)),
            jnp.ones((row_count, 1), jnp.float32),
            jnp.zeros((row_count, HEAD), jnp.float32),
        )

    if part_count == prompt_count and part_slots + stagger <= HALF_WIN:
        edge_start = (head ^ (head_count - 1)) * token_count + token_count - stagger
        edge = from_behind(
            lax.dynamic_slice_in_dim(rows, edge_start, stagger, 0), "seq", head_count
        )
        edge_ids = part * part_slots - stagger + jnp.arange(stagger, dtype=jnp.int32)
        row_ids = jnp.concatenate([part_ids, edge_ids])
        row_prompt, row_position = prompt_split(row_ids, slot_len, stagger, prompt_count)
        row_live = (row_ids >= 0) & (row_position < length_of(row_prompt, real_lengths))
        mixed = attend_once(
            sink,
            row_prompt,
            jnp.where(row_live, row_prompt, -1),
            jnp.concatenate([rows, edge], axis=0),
        )
        edge_back = from_behind(mixed[part_slots:], "seq", -head_count)
        mixed = mixed[:part_slots]
        kept = lax.dynamic_slice_in_dim(mixed, edge_start, stagger, 0)
        mixed = lax.dynamic_update_slice_in_dim(
            mixed, jnp.where(part < part_count - 1, edge_back, kept), edge_start, 0
        )
    else:
        query_rows, key_rows, value_rows = (rows[:, k * HEAD : (k + 1) * HEAD] for k in range(3))
        softmax_state = attend(
            start_state(part_slots),
            query_rows,
            key_rows,
            value_rows,
            key_rules(part_ids, part_ids, slot_len, stagger, total_slots, real_lengths),
        )
        from_below = from_above = jnp.concatenate([key_rows, value_rows], axis=1)
        for turn in range(1, min(part_count - 1, -(-HALF_WIN // part_slots)) + 1):
            from_below = from_behind(from_below, "seq", head_count)
            from_above = from_behind(from_above, "seq", -head_count)
            reach = turn * part_slots
            key_ids = jnp.concatenate([part_ids - reach, part_ids + reach])
            pair = jnp.concatenate([from_below, from_above], axis=0)
            softmax_state = attend(
                softmax_state,
                query_rows,
                pair[:, :HEAD],
                pair[:, HEAD:],
                key_rules(part_ids, key_ids, slot_len, stagger, total_slots, real_lengths),
            )
        _, denominator, accumulated = softmax_state
        mixed = (accumulated / denominator).astype(jnp.bfloat16)
    blocks = mixed.reshape(head_count, token_count, HEAD)
    heads = jnp.stack(
        [blocks[0]] + [swapped(blocks[m], "seq", m) for m in range(1, head_count)]
    )
    attention_result = jnp.concatenate(
        [lax.dynamic_index_in_dim(heads, head ^ h, 0, keepdims=False) for h in range(head_count)],
        axis=1,
    )
    proj_width = head_count * HEAD
    partial_out = times_columns(attention_result[:, :out_rows], 0, 0, out_rows) + times_columns(
        attention_result[:, out_rows:], 1, 0, proj_width - out_rows
    )
    if tp_count == 2:
        out_pieces = [partial_out, from_turned(partial_out, "tp", 1)]
    else:
        out_pieces = [lax.psum(partial_out, "tp")]
    router_rows = times_columns(None, 1, proj_width - out_rows, None)
    if width % 128:

        def in_order(value):
            blocks = [
                lax.dynamic_slice_in_dim(value, out_places[place] * width, width, 1)
                for place in range(seq_count)
            ]
            return jnp.concatenate(blocks, axis=1)

        out_pieces, router_rows = ([in_order(piece) for piece in out_pieces], in_order(router_rows))
        out_places, width = (jnp.zeros((1,), jnp.int32), model_width)
    full_rows, outgoing, logits = settle(
        out_places, out_pieces, tokens, mlp_gain, router_rows, width
    )
    residual = lax.dynamic_slice_in_dim(full_rows, tp_place * col_share, col_share, 1)
    outgoing_share = lax.dynamic_slice_in_dim(outgoing, tp_place * col_share, col_share, 1)


    all_rows, _ = doubled(outgoing_share[None], part_masks, 0)
    buffer = jnp.stack(
        [
            lax.dot_general(
                placed.astype(jnp.bfloat16),
                all_rows[k],
                (((0,), (0,)), ((), ())),
                preferred_element_type=jnp.float32,
            )
            .astype(jnp.bfloat16)
            .reshape(head_count, block_rows, col_share)
            for k, (_, _, placed) in enumerate(routings)
        ],
        axis=1,
    )
    received = jnp.stack(
        [buffer[0]] + [swapped(buffer[m], "seq", m) for m in range(1, head_count)]
    )
    row_count = head_count * part_count * capacity
    received = jnp.moveaxis(
        received.reshape(head_count, part_count, local_experts, capacity, col_share), 2, 0
    ).reshape(local_experts, row_count, col_share)
    hidden_share = expert_gate.shape[2]
    row_blocks = tp_blocks(received)
    gate_up = (
        sum(
            jnp.einsum(
                "acd,adf->acf",
                rows,
                lax.dynamic_slice_in_dim(
                    server[:, :, : 2 * hidden_share],
                    (tp_place + turn) % tp_count * col_share,
                    col_share,
                    1,
                ),
                preferred_element_type=jnp.float32,
            )
            for turn, rows in enumerate(row_blocks)
        )
    )
    hidden_state = (jax.nn.silu(gate_up[..., :hidden_share]) * gate_up[..., hidden_share:]).astype(
        jnp.bfloat16
    )
    server_down = server[:, :, 2 * hidden_share :]

    def down_columns(block):
        return jnp.einsum(
            "acf,adf->acd",
            hidden_state,
            lax.dynamic_slice_in_dim(server_down, block * col_share, col_share, 1),
            preferred_element_type=jnp.float32,
        ).astype(jnp.bfloat16)

    sent = [
        from_turned(down_columns((tp_place - turn) % tp_count), "tp", turn)
        for turn in range(1, tp_count)
    ]
    own = lax.optimization_barrier(down_columns(tp_place))
    summed = sum([piece.astype(jnp.float32) for piece in sent], own.astype(jnp.float32))
    summed = jnp.moveaxis(
        summed.astype(jnp.bfloat16).reshape(
            local_experts, head_count, part_count, capacity, col_share
        ),
        0,
        2,
    ).reshape(head_count, part_count, block_rows, col_share)

    route_logits = jnp.where(chosen, logits, -jnp.inf)
    route_exp = jnp.exp(route_logits - jnp.max(route_logits, axis=1, keepdims=True))
    route_weight = route_exp / jnp.sum(route_exp, axis=1, keepdims=True)
    route_weight = route_weight * valid_token[:, None]
    all_weights, _ = doubled(route_weight[None], part_masks, 0)

    def weighted(k, rows):
        placed = routings[k][2]
        stacked = jnp.concatenate(
            [
                jnp.where(
                    placed, jnp.dot(piece, spread, preferred_element_type=jnp.float32), 0.0
                ).astype(jnp.bfloat16)
                for piece in parts_of(all_weights[k], 3)
            ],
            axis=0,
        )
        mixes = jnp.dot(stacked, rows, preferred_element_type=jnp.float32)
        return sum(mixes[k * token_count : (k + 1) * token_count] for k in range(3))

    def back(blocks):
        return lax.all_to_all(
            blocks, "seq", split_axis=0, concat_axis=0, tiled=True, axis_index_groups=groups
        )

    def by_place(blocks):
        return jnp.stack(
            [
                lax.dynamic_index_in_dim(blocks, head ^ place, 0, keepdims=False)
                for place in range(head_count)
            ]
        )

    summed = by_place(summed)
    others, own_rows = summed[:, 1:], summed[:, :1]
    others = back(others)
    others, own_rows = lax.optimization_barrier((others, own_rows))
    expert_mix = 0.0
    for k, turn in enumerate(part_turns[1:]):
        mix = weighted(k + 1, by_place(others[:, k]).reshape(-1, col_share))
        expert_mix = expert_mix + swapped(mix, "seq", turn)
    own_mix = weighted(0, by_place(back(own_rows)[:, 0]).reshape(-1, col_share))
    return (residual + (expert_mix + own_mix)).astype(jnp.bfloat16)


def solution(mesh):
    placed = (
        P("seq", None),
        P(),
        P(),
        P("seq", "tp"),
        P("seq", "tp"),
        P("seq", "tp"),
        P("tp", "seq"),
        P("tp"),
        P("seq", None),
        P(None, "seq", "tp"),
        P(None, "seq", "tp"),
        P(None, "seq", "tp"),
        P(),
        P(),
        P("seq", None),
    )
    return jax.shard_map(
        shards, mesh=mesh, in_specs=placed, out_specs=P("seq", "tp"), check_vma=False
    )
```

```python
import jax
import jax.numpy as jnp
from jax import lax
from jax.experimental import pallas as pl
from jax.experimental.pallas import tpu as pltpu
from jax.sharding import PartitionSpec as P

HEAD = 128
HALF_WIN = 2048


EPSILON = 1e-05
ROPE_BASE = 50000.0
MASKED = -1e30
SMALL = pl.CostEstimate(flops=1, bytes_accessed=1, transcendentals=1)


def from_behind(value, axis, steps):
    count = lax.axis_size(axis)
    first, last = (max(0, -steps), min(count, count - steps))
    return lax.ppermute(value, axis, [(source, source + steps) for source in range(first, last)])


def from_turned(value, axis, turn):
    count = lax.axis_size(axis)
    return lax.ppermute(value, axis, [((place + turn) % count, place) for place in range(count)])


def swapped(value, axis, mask):
    count = lax.axis_size(axis)
    return lax.ppermute(value, axis, [(place, place ^ mask) for place in range(count)])


def doubled(value, masks, axis):
    turns = [0]
    for mask in masks:
        value = jnp.concatenate([value, swapped(value, "seq", mask)], axis=axis)
        turns = turns + [turn ^ mask for turn in turns]
    return (value, turns)


def masks_below(count, least=1):
    masks = []
    while count > least:
        count //= 2
        masks.append(count)
    return masks


def rms_scale(row_values, gain_vector):
    mean_square = jnp.mean(row_values * row_values, axis=-1, keepdims=True)
    return row_values * lax.rsqrt(mean_square + EPSILON) * gain_vector


def rotate(rows, cosine, sine_part):
    half_dim = rows.shape[-1] // 2
    first_half = rows[:, :half_dim]
    second_half = rows[:, half_dim:]
    return jnp.concatenate(
        [
            first_half * cosine - second_half * sine_part,
            second_half * cosine + first_half * sine_part,
        ],
        axis=-1,
    )


def length_of(prompt, real_lengths):
    one_hot = prompt[:, None] == jnp.arange(real_lengths.shape[0], dtype=jnp.int32)[None, :]
    return jnp.sum(jnp.where(one_hot, real_lengths[None, :], 0), axis=1)


def prompt_split(slot_ids, slot_len, stagger, prompt_count):
    prompt = jnp.minimum((slot_ids + stagger) // slot_len, prompt_count - 1)
    start = jnp.maximum(prompt * slot_len - stagger, 0)
    return (prompt, slot_ids - start)


def key_rules(query_ids, key_ids, slot_len, stagger, total_slots, real_lengths):
    prompt_count = real_lengths.shape[0]
    key_prompt, key_pos = prompt_split(key_ids, slot_len, stagger, prompt_count)
    query_prompt = prompt_split(query_ids, slot_len, stagger, prompt_count)[0]
    inside = (key_ids >= 0) & (key_ids < total_slots)
    key_live = inside & (key_pos < length_of(key_prompt, real_lengths))
    same_prompt = query_prompt[:, None] == key_prompt[None, :]
    nearby = jnp.abs(query_ids[:, None] - key_ids[None, :]) < HALF_WIN
    return same_prompt & nearby & key_live[None, :]


def parts_of(values, count):
    rest = values
    pieces = []
    for _ in range(count):
        piece = lax.reduce_precision(rest, 8, 7)
        rest = rest - piece
        pieces.append(piece.astype(jnp.bfloat16))
    return pieces


def attend(softmax_state, query_rows, key_rows, value_rows, allowed):
    running_max, denominator, accumulated = softmax_state
    scores = lax.dot_general(
        query_rows, key_rows, (((1,), (1,)), ((), ())), preferred_element_type=jnp.float32
    ) * HEAD ** (-0.5)
    scores = jnp.where(allowed, scores, MASKED)
    new_max = jnp.maximum(running_max, jnp.max(scores, axis=1, keepdims=True))
    rescale = jnp.exp(running_max - new_max)
    weight_tensors = jnp.exp(scores - new_max)
    denominator = denominator * rescale + jnp.sum(weight_tensors, axis=1, keepdims=True)
    high, low = parts_of(weight_tensors, 2)
    accumulated = (
        accumulated * rescale
        + jnp.dot(high, value_rows, preferred_element_type=jnp.float32)
        + jnp.dot(low, value_rows, preferred_element_type=jnp.float32)
    )
    return (new_max, denominator, accumulated)


def order_body(order_ref, gate_ref, up_ref, down_ref, out_ref):
    width = gate_ref.shape[2]
    for k, source in enumerate((gate_ref, up_ref, down_ref)):
        out_ref[:, :, k * width : (k + 1) * width] = source[...].astype(jnp.bfloat16)


def order_experts(layout_map, gate, up, down):
    count, rows, width = gate.shape
    source = pl.BlockSpec((1, rows, width), lambda place, order: (order[place], 0, 0))
    return pl.pallas_call(
        order_body,
        grid_spec=pltpu.PrefetchScalarGridSpec(
            num_scalar_prefetch=1,
            grid=(count,),
            in_specs=[source, source, source],
            out_specs=pl.BlockSpec((1, rows, 3 * width), lambda place, order: (place, 0, 0)),
        ),
        out_shape=jax.ShapeDtypeStruct((count, rows, 3 * width), jnp.bfloat16),
        name="order_experts",
    )(layout_map, gate, up, down)


def pack_body(query_ref, key_ref, value_ref, out_ref):
    heads = query_ref.shape[1] // HEAD
    for place in range(out_ref.shape[0]):
        head = place % heads
        for k, source in enumerate((query_ref, key_ref, value_ref)):
            out_ref[place, :, k * HEAD : (k + 1) * HEAD] = source[
                :, head * HEAD : (head + 1) * HEAD
            ].astype(jnp.bfloat16)


def pack_heads(w_query, w_key, w_value, copies):
    rows, width = w_query.shape
    places = copies * (width // HEAD)
    step = rows // 4 if rows % 64 == 0 else rows
    source = pl.BlockSpec((step, width), lambda place: (place, 0))
    return pl.pallas_call(
        pack_body,
        grid=(rows // step,),
        in_specs=[source, source, source],
        out_specs=pl.BlockSpec((places, step, 3 * HEAD), lambda place: (0, place, 0)),
        out_shape=jax.ShapeDtypeStruct((places, rows, 3 * HEAD), jnp.bfloat16),
        compiler_params=pltpu.CompilerParams(vmem_limit_bytes=32 * 2**20),
        cost_estimate=SMALL,
        name="pack_heads",
    )(w_query, w_key, w_value)


def project_body(turn_count, share, start_ref, *refs):
    rows, (weight_ref, cosine_ref, sine_ref, out_ref) = (refs[:turn_count], refs[turn_count:])
    product = 0.0
    for turn in range(turn_count):
        first = pl.multiple_of(start_ref[turn], share)
        product = product + jnp.dot(
            rows[turn][...], weight_ref[pl.ds(first, share), :], preferred_element_type=jnp.float32
        )
    cosine, sine_part = (cosine_ref[...], sine_ref[...])
    out_ref[:, :HEAD] = rotate(product[:, :HEAD], cosine, sine_part).astype(jnp.bfloat16)
    out_ref[:, HEAD : 2 * HEAD] = rotate(
        product[:, HEAD : 2 * HEAD], cosine, sine_part
    ).astype(jnp.bfloat16)
    out_ref[:, 2 * HEAD :] = product[:, 2 * HEAD :].astype(jnp.bfloat16)


def project(starts, row_blocks, weights, cosine, sine_part):
    row_count, share = row_blocks[0].shape
    step = row_count // 4
    whole = pl.BlockSpec(weights.shape, lambda place, starts: (0, 0))
    angle = pl.BlockSpec((step, cosine.shape[1]), lambda place, starts: (place, 0))
    return pl.pallas_call(
        lambda *refs: project_body(len(row_blocks), share, *refs),
        grid_spec=pltpu.PrefetchScalarGridSpec(
            num_scalar_prefetch=1,
            grid=(4,),
            in_specs=[pl.BlockSpec((step, share), lambda place, starts: (place, 0))]
            * len(row_blocks)
            + [whole, angle, angle],
            out_specs=pl.BlockSpec((step, weights.shape[1]), lambda place, starts: (place, 0)),
        ),
        out_shape=jax.ShapeDtypeStruct((row_count, weights.shape[1]), jnp.bfloat16),
        compiler_params=pltpu.CompilerParams(vmem_limit_bytes=32 * 2**20),
        cost_estimate=SMALL,
        name="project",
    )(starts, *row_blocks, weights, cosine, sine_part)


def attend_body(sink_ref, query_prompt_ref, key_prompt_ref, query_ref, key_ref, value_ref, out_ref):
    sink = sink_ref[0]
    scores = lax.dot_general(
        query_ref[...],
        key_ref[...],
        (((1,), (1,)), ((), ())),
        preferred_element_type=jnp.float32,
    ) * HEAD ** (-0.5)
    scores = jnp.where(query_prompt_ref[...] == key_prompt_ref[...], scores, MASKED)
    top = jnp.maximum(sink, jnp.max(scores, axis=1, keepdims=True))
    weights = jnp.exp(scores - top)
    denominator = jnp.exp(sink - top) + jnp.sum(weights, axis=1, keepdims=True)
    high = weights.astype(jnp.bfloat16)
    low = (weights - high.astype(jnp.float32)).astype(jnp.bfloat16)
    values = value_ref[...]
    mix = jnp.dot(high, values, preferred_element_type=jnp.float32) + jnp.dot(
        low, values, preferred_element_type=jnp.float32
    )
    out_ref[...] = (mix / denominator).astype(jnp.bfloat16)


def attend_once(sink, query_prompt, key_prompt, rows):
    row_count = rows.shape[0]
    steps = 4 if row_count % 64 == 0 else 1
    step = row_count // steps
    return pl.pallas_call(
        attend_body,
        grid=(steps,),
        in_specs=[
            pl.BlockSpec(memory_space=pltpu.SMEM),
            pl.BlockSpec((step, 1), lambda place: (place, 0)),
            pl.BlockSpec((1, row_count), lambda place: (0, 0)),
            pl.BlockSpec((step, HEAD), lambda place: (place, 0)),
            pl.BlockSpec((row_count, HEAD), lambda place: (0, 1)),
            pl.BlockSpec((row_count, HEAD), lambda place: (0, 2)),
        ],
        out_specs=pl.BlockSpec((step, HEAD), lambda place: (place, 0)),
        out_shape=jax.ShapeDtypeStruct((row_count, HEAD), jnp.bfloat16),
        compiler_params=pltpu.CompilerParams(vmem_limit_bytes=32 * 2**20),
        cost_estimate=SMALL,
        name="attend_once",
    )(sink, query_prompt[:, None], key_prompt[None, :], rows, rows, rows)


def settle_body(piece_count, *refs):
    pieces = refs[:piece_count]
    token_ref, gain_ref, router_ref, full_ref, outgoing_ref, logit_ref = refs[piece_count:]
    full = token_ref[...].astype(jnp.float32) + sum(piece[...] for piece in pieces)
    full_ref[...] = full
    outgoing = rms_scale(full, gain_ref[...]).astype(jnp.bfloat16)
    outgoing_ref[...] = outgoing
    logit_ref[...] = lax.dot_general(
        outgoing,
        router_ref[...],
        (((1,), (1,)), ((), ())),
        preferred_element_type=jnp.float32,
    )


def settle(pieces, tokens, gain, router):
    rows, columns = tokens.shape
    vmem = pl.BlockSpec(memory_space=pltpu.VMEM)
    return pl.pallas_call(
        lambda *refs: settle_body(len(pieces), *refs),
        in_specs=[vmem] * (len(pieces) + 3),
        out_specs=[vmem] * 3,
        out_shape=[
            jax.ShapeDtypeStruct((rows, columns), jnp.float32),
            jax.ShapeDtypeStruct((rows, columns), jnp.bfloat16),
            jax.ShapeDtypeStruct((rows, router.shape[0]), jnp.float32),
        ],
        compiler_params=pltpu.CompilerParams(vmem_limit_bytes=32 * 2**20),
        cost_estimate=SMALL,
        name="settle",
    )(*pieces, tokens, gain[None, :], router)


def expert_body(turn_count, share, in_ref, out_ref, *refs):
    rows, weight_ref, outs = (refs[:turn_count], refs[turn_count], refs[turn_count + 1 :])
    hidden = weight_ref.shape[2] // 3
    gate_up = 0.0
    for turn in range(turn_count):
        first = pl.multiple_of(in_ref[turn], share)
        gate_up = gate_up + jnp.dot(
            rows[turn][0],
            weight_ref[0, pl.ds(first, share), : 2 * hidden],
            preferred_element_type=jnp.float32,
        )
    gate, up = (gate_up[:, :hidden], gate_up[:, hidden:])
    state = (gate / (1.0 + jnp.exp(-gate)) * up).astype(jnp.bfloat16)
    for turn in range(turn_count):
        first = pl.multiple_of(out_ref[turn], share)
        outs[turn][0] = lax.dot_general(
            state,
            weight_ref[0, pl.ds(first, share), 2 * hidden :],
            (((1,), (1,)), ((), ())),
            preferred_element_type=jnp.float32,
        ).astype(jnp.bfloat16)


def experts(in_starts, out_starts, row_blocks, weights):
    local_experts, row_count, share = row_blocks[0].shape
    step = row_count // 2 if row_count % 32 == 0 else row_count
    block = pl.BlockSpec((1, step, share), lambda e, place, a, b: (e, place, 0))
    whole = pl.BlockSpec((1, *weights.shape[1:]), lambda e, place, a, b: (e, 0, 0))
    count = len(row_blocks)
    return pl.pallas_call(
        lambda *refs: expert_body(count, share, *refs),
        grid_spec=pltpu.PrefetchScalarGridSpec(
            num_scalar_prefetch=2,
            grid=(local_experts, row_count // step),
            in_specs=[block] * count + [whole],
            out_specs=[block] * count,
        ),
        out_shape=[jax.ShapeDtypeStruct(row_blocks[0].shape, jnp.bfloat16)] * count,
        compiler_params=pltpu.CompilerParams(vmem_limit_bytes=52 * 2**20),
        cost_estimate=SMALL,
        name="experts",
    )(in_starts, out_starts, *row_blocks, weights)


def shards(
    tokens,
    attn_gain,
    mlp_gain,
    w_query,
    w_key,
    w_value,
    w_out,
    sink_logits,
    router,
    expert_gate,
    expert_up,
    expert_down,
    layout_map,
    real_lengths,
    routes,
):
    token_count, model_width = tokens.shape
    seq_count = lax.axis_size("seq")
    tp_count = lax.axis_size("tp")
    expert_count = router.shape[1]
    route_count = routes.shape[1]
    head_count = sink_logits.shape[0]
    col_share = model_width // tp_count
    total_slots = token_count * seq_count
    prompt_count = real_lengths.shape[0]
    slot_len = total_slots // prompt_count
    stagger = token_count // 2
    capacity = max(2, min(token_count, 9 * token_count * route_count // (8 * expert_count)))
    part_count = seq_count // head_count
    part_slots = head_count * token_count
    local_experts = expert_count // seq_count
    seq_place = lax.axis_index("seq")
    tp_place = lax.axis_index("tp")
    part = seq_place // head_count
    head = seq_place % head_count

    def tp_blocks(value):
        return [value] + [from_turned(value, "tp", turn) for turn in range(1, tp_count)]

    offsets = jnp.arange(token_count, dtype=jnp.int32)
    turns = jnp.arange(head_count, dtype=jnp.int32)
    group_masks = masks_below(head_count)
    groups = [[first + k for k in range(head_count)] for first in range(0, seq_count, head_count)]
    part_masks = masks_below(seq_count, head_count)

    head_weights = lax.all_to_all(
        pack_heads(w_query, w_key, w_value, part_count),
        "seq",
        split_axis=0,
        concat_axis=0,
        tiled=True,
    ).reshape(model_width, 3 * HEAD)

    normed = rms_scale(tokens.astype(jnp.float32), attn_gain).astype(jnp.bfloat16)
    share = lax.dynamic_slice_in_dim(normed, tp_place * col_share, col_share, 1)
    own_blocks = order_experts(layout_map, expert_gate, expert_up, expert_down)
    first_rows, first_turns = doubled(share[None], group_masks[:1], 0)
    pieces = []
    for piece, masks in (
        (first_rows[:, :, : col_share // 2], group_masks[1:]),
        (first_rows[:, :, col_share // 2 :], group_masks[1:][::-1]),
    ):
        known = first_turns
        for mask in masks:
            if mask == masks[-1]:
                piece, own_blocks = lax.optimization_barrier((piece, own_blocks))
            piece = jnp.concatenate([piece, swapped(piece, "seq", mask)], axis=0)
            known = known + [turn ^ mask for turn in known]
        pieces.append(jnp.concatenate([piece[known.index(m)] for m in range(head_count)], axis=0))
    part_rows = jnp.concatenate(pieces, axis=1)

    out_all = lax.all_gather(
        jnp.concatenate([w_out, router.T], axis=0).astype(jnp.bfloat16), "seq", axis=1, tiled=True
    )

    def by_place(blocks):
        return jnp.stack(
            [
                lax.dynamic_index_in_dim(blocks, head ^ place, 0, keepdims=False)
                for place in range(head_count)
            ]
        )

    all_routes, part_turns = doubled(routes[None], part_masks, 0)
    expert_ids = jnp.arange(expert_count, dtype=jnp.int32)
    block_rows = local_experts * capacity
    columns = jnp.arange(head_count * block_rows, dtype=jnp.int32)
    column_owner = part * head_count + columns // block_rows
    column_expert = column_owner * local_experts + columns // capacity % local_experts
    spread = (column_expert[None, :] == expert_ids[:, None]).astype(jnp.bfloat16)
    wanted = (columns % capacity).astype(jnp.float32)
    earlier = (offsets[:, None] > offsets[None, :]).astype(jnp.bfloat16)

    def routing(turn, own_routes):
        ids = (seq_place ^ turn) * token_count + offsets
        prompt, position = prompt_split(ids, slot_len, stagger, prompt_count)
        valid_token = position < length_of(prompt, real_lengths)
        chosen = jnp.any(own_routes[:, :, None] == expert_ids[None, None, :], axis=1)
        live = chosen & valid_token[:, None]
        rank = jnp.dot(earlier, live.astype(jnp.bfloat16), preferred_element_type=jnp.float32)
        rank = jnp.where(live, rank, -1.0).astype(jnp.bfloat16)
        placed = jnp.dot(rank, spread, preferred_element_type=jnp.float32) == wanted[None, :]
        return (chosen, valid_token, placed)

    routings = [routing(turn, all_routes[k]) for k, turn in enumerate(part_turns)]
    chosen, valid_token, _ = routings[0]

    part_ids = (part * head_count + (head ^ turns))[:, None] * token_count + offsets[None, :]
    part_ids = part_ids.reshape(-1)
    part_positions = prompt_split(part_ids, slot_len, stagger, prompt_count)[1]
    half_dim = HEAD // 2
    frequency = ROPE_BASE ** (-jnp.arange(half_dim, dtype=jnp.float32) / half_dim)
    angles = part_positions.astype(jnp.float32)[:, None] * frequency[None, :]
    cosine = jnp.cos(angles)
    sine_part = jnp.sin(angles)
    starts = (tp_place + jnp.arange(tp_count, dtype=jnp.int32)) % tp_count * col_share
    rows = project(starts, tp_blocks(part_rows), head_weights, cosine, sine_part)
    sink = lax.dynamic_slice_in_dim(sink_logits, head, 1, 0)

    def start_state(row_count):
        return (
            jnp.broadcast_to(sink[:, None], (row_count, 1)),
            jnp.ones((row_count, 1), jnp.float32),
            jnp.zeros((row_count, HEAD), jnp.float32),
        )

    if part_count == prompt_count and part_slots + stagger <= HALF_WIN:
        edge_start = (head ^ (head_count - 1)) * token_count + token_count - stagger
        edge = from_behind(
            lax.dynamic_slice_in_dim(rows, edge_start, stagger, 0), "seq", head_count
        )
        edge_ids = part * part_slots - stagger + jnp.arange(stagger, dtype=jnp.int32)
        row_ids = jnp.concatenate([part_ids, edge_ids])
        row_prompt, row_position = prompt_split(row_ids, slot_len, stagger, prompt_count)
        row_live = (row_ids >= 0) & (row_position < length_of(row_prompt, real_lengths))
        mixed = attend_once(
            sink,
            row_prompt,
            jnp.where(row_live, row_prompt, -1),
            jnp.concatenate([rows, edge], axis=0),
        )
        edge_back = from_behind(mixed[part_slots:], "seq", -head_count)
        mixed = mixed[:part_slots]
        kept = lax.dynamic_slice_in_dim(mixed, edge_start, stagger, 0)
        mixed = lax.dynamic_update_slice_in_dim(
            mixed, jnp.where(part < part_count - 1, edge_back, kept), edge_start, 0
        )
    else:
        query_rows, key_rows, value_rows = (rows[:, k * HEAD : (k + 1) * HEAD] for k in range(3))
        softmax_state = attend(
            start_state(part_slots),
            query_rows,
            key_rows,
            value_rows,
            key_rules(part_ids, part_ids, slot_len, stagger, total_slots, real_lengths),
        )
        from_below = from_above = jnp.concatenate([key_rows, value_rows], axis=1)
        for turn in range(1, min(part_count - 1, -(-HALF_WIN // part_slots)) + 1):
            from_below = from_behind(from_below, "seq", head_count)
            from_above = from_behind(from_above, "seq", -head_count)
            reach = turn * part_slots
            key_ids = jnp.concatenate([part_ids - reach, part_ids + reach])
            pair = jnp.concatenate([from_below, from_above], axis=0)
            softmax_state = attend(
                softmax_state,
                query_rows,
                pair[:, :HEAD],
                pair[:, HEAD:],
                key_rules(part_ids, key_ids, slot_len, stagger, total_slots, real_lengths),
            )
        _, denominator, accumulated = softmax_state
        mixed = (accumulated / denominator).astype(jnp.bfloat16)
    attention_result = lax.all_to_all(
        by_place(mixed.reshape(head_count, token_count, HEAD)),
        "seq",
        split_axis=0,
        concat_axis=0,
        tiled=True,
        axis_index_groups=groups,
    )

    attention_result, own_blocks = lax.optimization_barrier((attention_result, own_blocks))
    server = lax.all_to_all(own_blocks, "seq", split_axis=0, concat_axis=0, tiled=True)
    server = jnp.swapaxes(
        server.reshape(seq_count, local_experts, *own_blocks.shape[1:]), 0, 1
    ).reshape(local_experts, model_width, own_blocks.shape[2])

    proj_width = head_count * HEAD
    partial_out = jnp.dot(
        jnp.swapaxes(attention_result, 0, 1).reshape(token_count, proj_width),
        out_all[:proj_width],
        preferred_element_type=jnp.float32,
    )
    if tp_count == 2:
        out_pieces = [partial_out, from_turned(partial_out, "tp", 1)]
    else:
        out_pieces = [lax.psum(partial_out, "tp")]
    full_rows, outgoing, logits = settle(out_pieces, tokens, mlp_gain, out_all[proj_width:])
    residual = lax.dynamic_slice_in_dim(full_rows, tp_place * col_share, col_share, 1)
    outgoing_share = lax.dynamic_slice_in_dim(outgoing, tp_place * col_share, col_share, 1)


    all_rows, _ = doubled(outgoing_share[None], part_masks, 0)
    buffer = jnp.stack(
        [
            lax.dot_general(
                placed.astype(jnp.bfloat16),
                all_rows[k],
                (((0,), (0,)), ((), ())),
                preferred_element_type=jnp.float32,
            )
            .astype(jnp.bfloat16)
            .reshape(head_count, block_rows, col_share)
            for k, (_, _, placed) in enumerate(routings)
        ],
        axis=1,
    )
    def to_mate(m):
        block = lax.dynamic_index_in_dim(buffer, head ^ m, 0, keepdims=False)
        return swapped(block, "seq", m) if m else block

    received = by_place(jnp.stack([to_mate(m) for m in range(head_count)]))
    received = received.reshape(head_count, part_count, local_experts, capacity, col_share)
    turn_ids = jnp.arange(tp_count, dtype=jnp.int32)
    in_starts = (tp_place + turn_ids) % tp_count * col_share
    out_starts = (tp_place - turn_ids) % tp_count * col_share

    halves = [
        tp_blocks(jnp.moveaxis(rows, 2, 0).reshape(local_experts, -1, col_share))
        for rows in (received[:, 1:], received[:, :1])
    ]
    halves, server = lax.optimization_barrier((halves, server))

    def through_experts(row_blocks, parts):
        outs = experts(in_starts, out_starts, row_blocks, server)
        outs = [outs[0]] + [from_turned(outs[k], "tp", k) for k in range(1, tp_count)]
        summed = sum(piece.astype(jnp.float32) for piece in outs).astype(jnp.bfloat16)
        summed = summed.reshape(local_experts, head_count, parts, capacity, col_share)
        return jnp.moveaxis(summed, 0, 2).reshape(head_count, parts, block_rows, col_share)

    others = through_experts(halves[0], part_count - 1)
    own_rows = through_experts(halves[1], 1)

    route_logits = jnp.where(chosen, logits, -jnp.inf)
    route_exp = jnp.exp(route_logits - jnp.max(route_logits, axis=1, keepdims=True))
    route_weight = route_exp / jnp.sum(route_exp, axis=1, keepdims=True)
    route_weight = route_weight * valid_token[:, None]
    all_weights, _ = doubled(route_weight[None], part_masks, 0)

    def weighted(k, rows):
        placed = routings[k][2]
        stacked = jnp.concatenate(
            [
                jnp.where(
                    placed, jnp.dot(piece, spread, preferred_element_type=jnp.float32), 0.0
                ).astype(jnp.bfloat16)
                for piece in parts_of(all_weights[k], 3)
            ],
            axis=0,
        )
        mixes = jnp.dot(stacked, rows, preferred_element_type=jnp.float32)
        return sum(mixes[k * token_count : (k + 1) * token_count] for k in range(3))

    def back(blocks):
        return lax.all_to_all(
            blocks, "seq", split_axis=0, concat_axis=0, tiled=True, axis_index_groups=groups
        )

    others = back(others)
    others, own_rows = lax.optimization_barrier((others, own_rows))
    expert_mix = 0.0
    for k, turn in enumerate(part_turns[1:]):
        mix = weighted(k + 1, others[:, k].reshape(-1, col_share))
        expert_mix = expert_mix + swapped(mix, "seq", turn)
    own_mix = weighted(0, back(own_rows)[:, 0].reshape(-1, col_share))
    return (residual + (expert_mix + own_mix)).astype(jnp.bfloat16)


def solution(mesh):
    placed = (
        P("seq", None),
        P(),
        P(),
        P("seq", "tp"),
        P("seq", "tp"),
        P("seq", "tp"),
        P("tp", "seq"),
        P("tp"),
        P("seq", None),
        P(None, "seq", "tp"),
        P(None, "seq", "tp"),
        P(None, "seq", "tp"),
        P(),
        P(),
        P("seq", None),
    )
    return jax.shard_map(
        shards, mesh=mesh, in_specs=placed, out_specs=P("seq", "tp"), check_vma=False
    )
```

```python
import jax
import jax.numpy as jnp
from jax import lax
from jax.experimental import pallas as pl
from jax.experimental.pallas import tpu as pltpu
from jax.sharding import PartitionSpec as P

HEAD = 128
HALF_WIN = 2048


EPSILON = 1e-05
ROPE_BASE = 50000.0
MASKED = -1e30
SMALL = pl.CostEstimate(flops=1, bytes_accessed=1, transcendentals=1)


def from_behind(value, axis, steps):
    count = lax.axis_size(axis)
    first, last = (max(0, -steps), min(count, count - steps))
    return lax.ppermute(value, axis, [(source, source + steps) for source in range(first, last)])


def from_turned(value, axis, turn):
    count = lax.axis_size(axis)
    return lax.ppermute(value, axis, [((place + turn) % count, place) for place in range(count)])


def swapped(value, axis, mask):
    count = lax.axis_size(axis)
    return lax.ppermute(value, axis, [(place, place ^ mask) for place in range(count)])


def doubled(value, masks, axis):
    turns = [0]
    for mask in masks:
        value = jnp.concatenate([value, swapped(value, "seq", mask)], axis=axis)
        turns = turns + [turn ^ mask for turn in turns]
    return (value, turns)


def masks_below(count, least=1):
    masks = []
    while count > least:
        count //= 2
        masks.append(count)
    return masks


def rms_scale(row_values, gain_vector):
    mean_square = jnp.mean(row_values * row_values, axis=-1, keepdims=True)
    return row_values * lax.rsqrt(mean_square + EPSILON) * gain_vector


def rotate(rows, cosine, sine_part):
    half_dim = rows.shape[-1] // 2
    first_half = rows[:, :half_dim]
    second_half = rows[:, half_dim:]
    return jnp.concatenate(
        [
            first_half * cosine - second_half * sine_part,
            second_half * cosine + first_half * sine_part,
        ],
        axis=-1,
    )


def length_of(prompt, real_lengths):
    one_hot = prompt[:, None] == jnp.arange(real_lengths.shape[0], dtype=jnp.int32)[None, :]
    return jnp.sum(jnp.where(one_hot, real_lengths[None, :], 0), axis=1)


def prompt_split(slot_ids, slot_len, stagger, prompt_count):
    prompt = jnp.minimum((slot_ids + stagger) // slot_len, prompt_count - 1)
    start = jnp.maximum(prompt * slot_len - stagger, 0)
    return (prompt, slot_ids - start)


def key_rules(query_ids, key_ids, slot_len, stagger, total_slots, real_lengths):
    prompt_count = real_lengths.shape[0]
    key_prompt, key_pos = prompt_split(key_ids, slot_len, stagger, prompt_count)
    query_prompt = prompt_split(query_ids, slot_len, stagger, prompt_count)[0]
    inside = (key_ids >= 0) & (key_ids < total_slots)
    key_live = inside & (key_pos < length_of(key_prompt, real_lengths))
    same_prompt = query_prompt[:, None] == key_prompt[None, :]
    nearby = jnp.abs(query_ids[:, None] - key_ids[None, :]) < HALF_WIN
    return same_prompt & nearby & key_live[None, :]


def parts_of(values, count):
    rest = values
    pieces = []
    for _ in range(count):
        piece = lax.reduce_precision(rest, 8, 7)
        rest = rest - piece
        pieces.append(piece.astype(jnp.bfloat16))
    return pieces


def attend(softmax_state, query_rows, key_rows, value_rows, allowed):
    running_max, denominator, accumulated = softmax_state
    scores = lax.dot_general(
        query_rows, key_rows, (((1,), (1,)), ((), ())), preferred_element_type=jnp.float32
    ) * HEAD ** (-0.5)
    scores = jnp.where(allowed, scores, MASKED)
    new_max = jnp.maximum(running_max, jnp.max(scores, axis=1, keepdims=True))
    rescale = jnp.exp(running_max - new_max)
    weight_tensors = jnp.exp(scores - new_max)
    denominator = denominator * rescale + jnp.sum(weight_tensors, axis=1, keepdims=True)
    high, low = parts_of(weight_tensors, 2)
    accumulated = (
        accumulated * rescale
        + jnp.dot(high, value_rows, preferred_element_type=jnp.float32)
        + jnp.dot(low, value_rows, preferred_element_type=jnp.float32)
    )
    return (new_max, denominator, accumulated)


def order_body(order_ref, gate_ref, up_ref, down_ref, gate_out, up_out, down_out):
    gate_out[...] = gate_ref[...].astype(jnp.bfloat16)
    up_out[...] = up_ref[...].astype(jnp.bfloat16)
    down_out[...] = down_ref[...].astype(jnp.bfloat16)


def order_experts(layout_map, gate, up, down):
    count, rows, width = gate.shape
    source = pl.BlockSpec((1, rows, width), lambda place, order: (order[place], 0, 0))
    target = pl.BlockSpec((1, rows, width), lambda place, order: (place, 0, 0))
    return pl.pallas_call(
        order_body,
        grid_spec=pltpu.PrefetchScalarGridSpec(
            num_scalar_prefetch=1,
            grid=(count,),
            in_specs=[source, source, source],
            out_specs=[target, target, target],
        ),
        out_shape=[jax.ShapeDtypeStruct((count, rows, width), jnp.bfloat16)] * 3,
        cost_estimate=SMALL,
        name="order_experts",
    )(layout_map, gate, up, down)


def pack_body(query_ref, key_ref, value_ref, out_ref):
    heads = query_ref.shape[1] // HEAD
    for place in range(out_ref.shape[0]):
        head = place % heads
        for k, source in enumerate((query_ref, key_ref, value_ref)):
            out_ref[place, :, k * HEAD : (k + 1) * HEAD] = source[
                :, head * HEAD : (head + 1) * HEAD
            ].astype(jnp.bfloat16)


def pack_heads(w_query, w_key, w_value, copies):
    rows, width = w_query.shape
    places = copies * (width // HEAD)
    step = rows // 4 if rows % 64 == 0 else rows
    source = pl.BlockSpec((step, width), lambda place: (place, 0))
    return pl.pallas_call(
        pack_body,
        grid=(rows // step,),
        in_specs=[source, source, source],
        out_specs=pl.BlockSpec((places, step, 3 * HEAD), lambda place: (0, place, 0)),
        out_shape=jax.ShapeDtypeStruct((places, rows, 3 * HEAD), jnp.bfloat16),
        compiler_params=pltpu.CompilerParams(vmem_limit_bytes=32 * 2**20),
        cost_estimate=SMALL,
        name="pack_heads",
    )(w_query, w_key, w_value)


def project_body(turn_count, share, start_ref, *refs):
    rows, (weight_ref, cosine_ref, sine_ref, out_ref) = (refs[:turn_count], refs[turn_count:])
    product = 0.0
    for turn in range(turn_count):
        first = pl.multiple_of(start_ref[turn], share)
        product = product + jnp.dot(
            rows[turn][...], weight_ref[pl.ds(first, share), :], preferred_element_type=jnp.float32
        )
    cosine, sine_part = (cosine_ref[...], sine_ref[...])
    out_ref[:, :HEAD] = rotate(product[:, :HEAD], cosine, sine_part).astype(jnp.bfloat16)
    out_ref[:, HEAD : 2 * HEAD] = rotate(
        product[:, HEAD : 2 * HEAD], cosine, sine_part
    ).astype(jnp.bfloat16)
    out_ref[:, 2 * HEAD :] = product[:, 2 * HEAD :].astype(jnp.bfloat16)


def project(starts, row_blocks, weights, cosine, sine_part):
    row_count, share = row_blocks[0].shape
    step = row_count // 4
    whole = pl.BlockSpec(weights.shape, lambda place, starts: (0, 0))
    angle = pl.BlockSpec((step, cosine.shape[1]), lambda place, starts: (place, 0))
    return pl.pallas_call(
        lambda *refs: project_body(len(row_blocks), share, *refs),
        grid_spec=pltpu.PrefetchScalarGridSpec(
            num_scalar_prefetch=1,
            grid=(4,),
            in_specs=[pl.BlockSpec((step, share), lambda place, starts: (place, 0))]
            * len(row_blocks)
            + [whole, angle, angle],
            out_specs=pl.BlockSpec((step, weights.shape[1]), lambda place, starts: (place, 0)),
        ),
        out_shape=jax.ShapeDtypeStruct((row_count, weights.shape[1]), jnp.bfloat16),
        compiler_params=pltpu.CompilerParams(vmem_limit_bytes=32 * 2**20),
        cost_estimate=SMALL,
        name="project",
    )(starts, *row_blocks, weights, cosine, sine_part)


def attend_body(sink_ref, query_prompt_ref, key_prompt_ref, query_ref, key_ref, value_ref, out_ref):
    sink = sink_ref[0]
    scores = lax.dot_general(
        query_ref[...],
        key_ref[...],
        (((1,), (1,)), ((), ())),
        preferred_element_type=jnp.float32,
    ) * HEAD ** (-0.5)
    scores = jnp.where(query_prompt_ref[...] == key_prompt_ref[...], scores, MASKED)
    top = jnp.maximum(sink, jnp.max(scores, axis=1, keepdims=True))
    weights = jnp.exp(scores - top)
    denominator = jnp.exp(sink - top) + jnp.sum(weights, axis=1, keepdims=True)
    high = weights.astype(jnp.bfloat16)
    low = (weights - high.astype(jnp.float32)).astype(jnp.bfloat16)
    values = value_ref[...]
    mix = jnp.dot(high, values, preferred_element_type=jnp.float32) + jnp.dot(
        low, values, preferred_element_type=jnp.float32
    )
    out_ref[...] = (mix / denominator).astype(jnp.bfloat16)


def attend_once(sink, query_prompt, key_prompt, rows):
    row_count = rows.shape[0]
    steps = 4 if row_count % 64 == 0 else 1
    step = row_count // steps
    return pl.pallas_call(
        attend_body,
        grid=(steps,),
        in_specs=[
            pl.BlockSpec(memory_space=pltpu.SMEM),
            pl.BlockSpec((step, 1), lambda place: (place, 0)),
            pl.BlockSpec((1, row_count), lambda place: (0, 0)),
            pl.BlockSpec((step, HEAD), lambda place: (place, 0)),
            pl.BlockSpec((row_count, HEAD), lambda place: (0, 1)),
            pl.BlockSpec((row_count, HEAD), lambda place: (0, 2)),
        ],
        out_specs=pl.BlockSpec((step, HEAD), lambda place: (place, 0)),
        out_shape=jax.ShapeDtypeStruct((row_count, HEAD), jnp.bfloat16),
        compiler_params=pltpu.CompilerParams(vmem_limit_bytes=32 * 2**20),
        cost_estimate=SMALL,
        name="attend_once",
    )(sink, query_prompt[:, None], key_prompt[None, :], rows, rows, rows)


def settle_body(piece_count, *refs):
    pieces = refs[:piece_count]
    token_ref, gain_ref, router_ref, full_ref, outgoing_ref, logit_ref = refs[piece_count:]
    full = token_ref[...].astype(jnp.float32) + sum(piece[...] for piece in pieces)
    full_ref[...] = full
    outgoing = rms_scale(full, gain_ref[...]).astype(jnp.bfloat16)
    outgoing_ref[...] = outgoing
    logit_ref[...] = lax.dot_general(
        outgoing,
        router_ref[...],
        (((1,), (1,)), ((), ())),
        preferred_element_type=jnp.float32,
    )


def settle(pieces, tokens, gain, router):
    rows, columns = tokens.shape
    vmem = pl.BlockSpec(memory_space=pltpu.VMEM)
    return pl.pallas_call(
        lambda *refs: settle_body(len(pieces), *refs),
        in_specs=[vmem] * (len(pieces) + 3),
        out_specs=[vmem] * 3,
        out_shape=[
            jax.ShapeDtypeStruct((rows, columns), jnp.float32),
            jax.ShapeDtypeStruct((rows, columns), jnp.bfloat16),
            jax.ShapeDtypeStruct((rows, router.shape[0]), jnp.float32),
        ],
        compiler_params=pltpu.CompilerParams(vmem_limit_bytes=32 * 2**20),
        cost_estimate=SMALL,
        name="settle",
    )(*pieces, tokens, gain[None, :], router)


def expert_body(turn_count, share, in_ref, out_ref, *refs):
    rows, (gate_ref, up_ref, down_ref), outs = (
        refs[:turn_count],
        refs[turn_count : turn_count + 3],
        refs[turn_count + 3 :],
    )
    gate = up = 0.0
    for turn in range(turn_count):
        here = pl.ds(pl.multiple_of(in_ref[turn], share), share)
        gate = gate + jnp.dot(
            rows[turn][0], gate_ref[0, here, :], preferred_element_type=jnp.float32
        )
        up = up + jnp.dot(rows[turn][0], up_ref[0, here, :], preferred_element_type=jnp.float32)
    state = (gate / (1.0 + jnp.exp(-gate)) * up).astype(jnp.bfloat16)
    for turn in range(turn_count):
        here = pl.ds(pl.multiple_of(out_ref[turn], share), share)
        outs[turn][0] = lax.dot_general(
            state,
            down_ref[0, here, :],
            (((1,), (1,)), ((), ())),
            preferred_element_type=jnp.float32,
        ).astype(jnp.bfloat16)


def experts(in_starts, out_starts, row_blocks, weights):
    local_experts, row_count, share = row_blocks[0].shape
    step = row_count // 2 if row_count % 32 == 0 else row_count
    block = pl.BlockSpec((1, step, share), lambda e, place, a, b: (e, place, 0))
    whole = pl.BlockSpec((1, *weights[0].shape[1:]), lambda e, place, a, b: (e, 0, 0))
    count = len(row_blocks)
    return pl.pallas_call(
        lambda *refs: expert_body(count, share, *refs),
        grid_spec=pltpu.PrefetchScalarGridSpec(
            num_scalar_prefetch=2,
            grid=(local_experts, row_count // step),
            in_specs=[block] * count + [whole] * 3,
            out_specs=[block] * count,
        ),
        out_shape=[jax.ShapeDtypeStruct(row_blocks[0].shape, jnp.bfloat16)] * count,
        compiler_params=pltpu.CompilerParams(vmem_limit_bytes=52 * 2**20),
        cost_estimate=SMALL,
        name="experts",
    )(in_starts, out_starts, *row_blocks, *weights)


def shards(
    tokens,
    attn_gain,
    mlp_gain,
    w_query,
    w_key,
    w_value,
    w_out,
    sink_logits,
    router,
    expert_gate,
    expert_up,
    expert_down,
    layout_map,
    real_lengths,
    routes,
):
    token_count, model_width = tokens.shape
    seq_count = lax.axis_size("seq")
    tp_count = lax.axis_size("tp")
    expert_count = router.shape[1]
    route_count = routes.shape[1]
    head_count = sink_logits.shape[0]
    col_share = model_width // tp_count
    total_slots = token_count * seq_count
    prompt_count = real_lengths.shape[0]
    slot_len = total_slots // prompt_count
    stagger = token_count // 2
    capacity = max(2, min(token_count, 9 * token_count * route_count // (8 * expert_count)))
    part_count = seq_count // head_count
    part_slots = head_count * token_count
    local_experts = expert_count // seq_count
    seq_place = lax.axis_index("seq")
    tp_place = lax.axis_index("tp")
    part = seq_place // head_count
    head = seq_place % head_count

    def tp_blocks(value):
        return [value] + [from_turned(value, "tp", turn) for turn in range(1, tp_count)]

    offsets = jnp.arange(token_count, dtype=jnp.int32)
    turns = jnp.arange(head_count, dtype=jnp.int32)
    aligned = part_count == prompt_count and part_slots + stagger <= HALF_WIN
    group_masks = masks_below(head_count)
    groups = [[first + k for k in range(head_count)] for first in range(0, seq_count, head_count)]
    part_masks = masks_below(seq_count, head_count)

    head_weights = lax.all_to_all(
        pack_heads(w_query, w_key, w_value, part_count),
        "seq",
        split_axis=0,
        concat_axis=0,
        tiled=True,
    ).reshape(model_width, 3 * HEAD)

    normed = rms_scale(tokens.astype(jnp.float32), attn_gain).astype(jnp.bfloat16)
    share = lax.dynamic_slice_in_dim(normed, tp_place * col_share, col_share, 1)
    all_routes, part_turns = doubled(routes[None], part_masks, 0)
    if aligned:
        edge = from_behind(share[token_count - stagger :], "seq", head_count)
        edge = jnp.where(head == head_count - 1, edge, jnp.zeros((), jnp.bfloat16))
    own_gate, own_up, own_down = order_experts(layout_map, expert_gate, expert_up, expert_down)
    first_rows, first_turns = doubled(share[None], group_masks[:1], 0)
    first_rows, all_routes = lax.optimization_barrier((first_rows, all_routes))
    pieces = []
    for piece, masks in (
        (first_rows[:, :, : col_share // 2], group_masks[1:]),
        (first_rows[:, :, col_share // 2 :], group_masks[1:][::-1]),
    ):
        known = first_turns
        for mask in masks:
            if mask == masks[-1]:
                piece, own_gate = lax.optimization_barrier((piece, own_gate))
            piece = jnp.concatenate([piece, swapped(piece, "seq", mask)], axis=0)
            known = known + [turn ^ mask for turn in known]
        pieces.append(jnp.concatenate([piece[known.index(m)] for m in range(head_count)], axis=0))
    part_rows = jnp.concatenate(pieces, axis=1)
    part_ids = (part * head_count + (head ^ turns))[:, None] * token_count + offsets[None, :]
    part_ids = part_ids.reshape(-1)
    if aligned:
        for mask in group_masks:
            edge = edge + swapped(edge, "seq", mask)
        part_rows = jnp.concatenate([part_rows, edge], axis=0)
        edge_ids = part * part_slots - stagger + jnp.arange(stagger, dtype=jnp.int32)
        part_ids = jnp.concatenate([part_ids, edge_ids])

    def to_owner(blocks):
        taken = lax.all_to_all(blocks, "seq", split_axis=0, concat_axis=0, tiled=True)
        taken = taken.reshape(seq_count, local_experts, *blocks.shape[1:])
        return jnp.swapaxes(taken, 0, 1).reshape(local_experts, model_width, blocks.shape[2])

    own_gate, head_weights = lax.optimization_barrier((own_gate, head_weights))
    server_gate = to_owner(own_gate)

    out_all = lax.all_gather(
        jnp.concatenate([w_out, router.T], axis=0).astype(jnp.bfloat16), "seq", axis=1, tiled=True
    )

    def by_place(blocks):
        return jnp.stack(
            [
                lax.dynamic_index_in_dim(blocks, head ^ place, 0, keepdims=False)
                for place in range(head_count)
            ]
        )

    expert_ids = jnp.arange(expert_count, dtype=jnp.int32)
    block_rows = local_experts * capacity
    columns = jnp.arange(head_count * block_rows, dtype=jnp.int32)
    column_owner = part * head_count + columns // block_rows
    column_expert = column_owner * local_experts + columns // capacity % local_experts
    spread = (column_expert[None, :] == expert_ids[:, None]).astype(jnp.bfloat16)
    wanted = (columns % capacity).astype(jnp.float32)
    earlier = (offsets[:, None] > offsets[None, :]).astype(jnp.bfloat16)

    def routing(turn, own_routes):
        ids = (seq_place ^ turn) * token_count + offsets
        prompt, position = prompt_split(ids, slot_len, stagger, prompt_count)
        valid_token = position < length_of(prompt, real_lengths)
        chosen = jnp.any(own_routes[:, :, None] == expert_ids[None, None, :], axis=1)
        live = chosen & valid_token[:, None]
        rank = jnp.dot(earlier, live.astype(jnp.bfloat16), preferred_element_type=jnp.float32)
        rank = jnp.where(live, rank, -1.0).astype(jnp.bfloat16)
        placed = jnp.dot(rank, spread, preferred_element_type=jnp.float32) == wanted[None, :]
        return (chosen, valid_token, placed)

    routings = [routing(turn, all_routes[k]) for k, turn in enumerate(part_turns)]
    chosen, valid_token, _ = routings[0]

    part_positions = prompt_split(part_ids, slot_len, stagger, prompt_count)[1]
    half_dim = HEAD // 2
    frequency = ROPE_BASE ** (-jnp.arange(half_dim, dtype=jnp.float32) / half_dim)
    angles = part_positions.astype(jnp.float32)[:, None] * frequency[None, :]
    cosine = jnp.cos(angles)
    sine_part = jnp.sin(angles)
    starts = (tp_place + jnp.arange(tp_count, dtype=jnp.int32)) % tp_count * col_share
    rows = project(starts, tp_blocks(part_rows), head_weights, cosine, sine_part)
    sink = lax.dynamic_slice_in_dim(sink_logits, head, 1, 0)

    def start_state(row_count):
        return (
            jnp.broadcast_to(sink[:, None], (row_count, 1)),
            jnp.ones((row_count, 1), jnp.float32),
            jnp.zeros((row_count, HEAD), jnp.float32),
        )

    if aligned:
        row_prompt, row_position = prompt_split(part_ids, slot_len, stagger, prompt_count)
        row_live = (part_ids >= 0) & (row_position < length_of(row_prompt, real_lengths))
        mixed = attend_once(sink, row_prompt, jnp.where(row_live, row_prompt, -1), rows)
        mixed, server_gate = lax.optimization_barrier((mixed, server_gate))
        by_slot = by_place(mixed[:part_slots].reshape(head_count, token_count, HEAD))
        by_slot = jnp.concatenate([mixed[part_slots:], by_slot.reshape(part_slots, HEAD)], axis=0)
        by_slot = lax.dynamic_update_slice_in_dim(
            jnp.zeros((stagger + total_slots, HEAD), jnp.bfloat16), by_slot, part * part_slots, 0
        )[stagger:]
        taken = lax.all_to_all(
            by_slot.reshape(seq_count, token_count, HEAD),
            "seq",
            split_axis=0,
            concat_axis=0,
            tiled=True,
        )
        kept = lax.dynamic_slice_in_dim(taken, part * head_count, head_count, 0)
        next_part = jnp.minimum(part + 1, part_count - 1)
        moved = lax.dynamic_slice_in_dim(taken, next_part * head_count, head_count, 0)
        is_moved = (head == head_count - 1) & (offsets >= token_count - stagger)
        attention_result = jnp.where(is_moved[None, :, None], moved, kept)
    else:
        query_rows, key_rows, value_rows = (rows[:, k * HEAD : (k + 1) * HEAD] for k in range(3))
        softmax_state = attend(
            start_state(part_slots),
            query_rows,
            key_rows,
            value_rows,
            key_rules(part_ids, part_ids, slot_len, stagger, total_slots, real_lengths),
        )
        from_below = from_above = jnp.concatenate([key_rows, value_rows], axis=1)
        for turn in range(1, min(part_count - 1, -(-HALF_WIN // part_slots)) + 1):
            from_below = from_behind(from_below, "seq", head_count)
            from_above = from_behind(from_above, "seq", -head_count)
            reach = turn * part_slots
            key_ids = jnp.concatenate([part_ids - reach, part_ids + reach])
            pair = jnp.concatenate([from_below, from_above], axis=0)
            softmax_state = attend(
                softmax_state,
                query_rows,
                pair[:, :HEAD],
                pair[:, HEAD:],
                key_rules(part_ids, key_ids, slot_len, stagger, total_slots, real_lengths),
            )
        _, denominator, accumulated = softmax_state
        mixed = (accumulated / denominator).astype(jnp.bfloat16)
        mixed, server_gate = lax.optimization_barrier((mixed, server_gate))
        attention_result = lax.all_to_all(
            by_place(mixed.reshape(head_count, token_count, HEAD)),
            "seq",
            split_axis=0,
            concat_axis=0,
            tiled=True,
            axis_index_groups=groups,
        )
    attention_result, own_up = lax.optimization_barrier((attention_result, own_up))
    server_up = to_owner(own_up)

    proj_width = head_count * HEAD
    partial_out = jnp.dot(
        jnp.swapaxes(attention_result, 0, 1).reshape(token_count, proj_width),
        out_all[:proj_width],
        preferred_element_type=jnp.float32,
    )
    if tp_count == 2:
        out_pieces = [partial_out, from_turned(partial_out, "tp", 1)]
    else:
        out_pieces = [lax.psum(partial_out, "tp")]
    full_rows, outgoing, logits = settle(out_pieces, tokens, mlp_gain, out_all[proj_width:])
    residual = lax.dynamic_slice_in_dim(full_rows, tp_place * col_share, col_share, 1)
    outgoing_share = lax.dynamic_slice_in_dim(outgoing, tp_place * col_share, col_share, 1)


    route_logits = jnp.where(chosen, logits, -jnp.inf)
    route_exp = jnp.exp(route_logits - jnp.max(route_logits, axis=1, keepdims=True))
    route_weight = route_exp / jnp.sum(route_exp, axis=1, keepdims=True)
    route_weight = route_weight * valid_token[:, None]
    all_weights, _ = doubled(route_weight[None], part_masks, 0)
    all_rows, _ = doubled(outgoing_share[None], part_masks, 0)
    all_rows, all_weights, own_down = lax.optimization_barrier((all_rows, all_weights, own_down))
    server_down = to_owner(own_down)
    buffer = jnp.stack(
        [
            lax.dot_general(
                placed.astype(jnp.bfloat16),
                all_rows[k],
                (((0,), (0,)), ((), ())),
                preferred_element_type=jnp.float32,
            )
            .astype(jnp.bfloat16)
            .reshape(head_count, block_rows, col_share)
            for k, (_, _, placed) in enumerate(routings)
        ],
        axis=1,
    )
    def to_mate(m):
        block = lax.dynamic_index_in_dim(buffer, head ^ m, 0, keepdims=False)
        return swapped(block, "seq", m) if m else block

    received = by_place(jnp.stack([to_mate(m) for m in range(head_count)]))
    received = received.reshape(head_count, part_count, local_experts, capacity, col_share)
    turn_ids = jnp.arange(tp_count, dtype=jnp.int32)
    in_starts = (tp_place + turn_ids) % tp_count * col_share
    out_starts = (tp_place - turn_ids) % tp_count * col_share

    halves = [
        tp_blocks(jnp.moveaxis(rows, 2, 0).reshape(local_experts, -1, col_share))
        for rows in (received[:, 1:], received[:, :1])
    ]
    server = (server_gate, server_up, server_down)
    halves, server = lax.optimization_barrier((halves, server))

    def through_experts(row_blocks, parts):
        outs = experts(in_starts, out_starts, row_blocks, server)
        outs = [outs[0]] + [from_turned(outs[k], "tp", k) for k in range(1, tp_count)]
        summed = sum(piece.astype(jnp.float32) for piece in outs).astype(jnp.bfloat16)
        summed = summed.reshape(local_experts, head_count, parts, capacity, col_share)
        return jnp.moveaxis(summed, 0, 2).reshape(head_count, parts, block_rows, col_share)

    others = through_experts(halves[0], part_count - 1)
    own_rows = through_experts(halves[1], 1)

    def weighted(k, rows):
        placed = routings[k][2]
        stacked = jnp.concatenate(
            [
                jnp.where(
                    placed, jnp.dot(piece, spread, preferred_element_type=jnp.float32), 0.0
                ).astype(jnp.bfloat16)
                for piece in parts_of(all_weights[k], 3)
            ],
            axis=0,
        )
        mixes = jnp.dot(stacked, rows, preferred_element_type=jnp.float32)
        return sum(mixes[k * token_count : (k + 1) * token_count] for k in range(3))

    def back(blocks):
        return lax.all_to_all(
            blocks, "seq", split_axis=0, concat_axis=0, tiled=True, axis_index_groups=groups
        )

    others = back(others)
    mixes = [
        weighted(k, others[:, k - 1].reshape(-1, col_share)) for k in range(1, len(part_turns))
    ]
    mixes, own_rows = lax.optimization_barrier((mixes, own_rows))
    expert_mix = sum(swapped(mix, "seq", turn) for mix, turn in zip(mixes, part_turns[1:]))
    own_mix = weighted(0, back(own_rows)[:, 0].reshape(-1, col_share))
    return (residual + (expert_mix + own_mix)).astype(jnp.bfloat16)


def solution(mesh):
    placed = (
        P("seq", None),
        P(),
        P(),
        P("seq", "tp"),
        P("seq", "tp"),
        P("seq", "tp"),
        P("tp", "seq"),
        P("tp"),
        P("seq", None),
        P(None, "seq", "tp"),
        P(None, "seq", "tp"),
        P(None, "seq", "tp"),
        P(),
        P(),
        P("seq", None),
    )
    return jax.shard_map(
        shards, mesh=mesh, in_specs=placed, out_specs=P("seq", "tp"), check_vma=False
    )
```

```python
import jax
import jax.numpy as jnp
from jax import lax
from jax.experimental import pallas as pl
from jax.experimental.pallas import tpu as pltpu
from jax.sharding import PartitionSpec as P

HEAD = 128
HALF_WIN = 2048


EPSILON = 1e-05
ROPE_BASE = 50000.0
MASKED = -1e30
SMALL = pl.CostEstimate(flops=1, bytes_accessed=1, transcendentals=1)


def from_behind(value, axis, steps):
    count = lax.axis_size(axis)
    first, last = (max(0, -steps), min(count, count - steps))
    return lax.ppermute(value, axis, [(source, source + steps) for source in range(first, last)])


def from_turned(value, axis, turn):
    count = lax.axis_size(axis)
    return lax.ppermute(value, axis, [((place + turn) % count, place) for place in range(count)])


def swapped(value, axis, mask):
    count = lax.axis_size(axis)
    return lax.ppermute(value, axis, [(place, place ^ mask) for place in range(count)])


def doubled(value, masks, axis):
    turns = [0]
    for mask in masks:
        value = jnp.concatenate([value, swapped(value, "seq", mask)], axis=axis)
        turns = turns + [turn ^ mask for turn in turns]
    return (value, turns)


def masks_below(count, least=1):
    masks = []
    while count > least:
        count //= 2
        masks.append(count)
    return masks


def rms_scale(row_values, gain_vector):
    mean_square = jnp.mean(row_values * row_values, axis=-1, keepdims=True)
    return row_values * lax.rsqrt(mean_square + EPSILON) * gain_vector


def rotate(rows, cosine, sine_part):
    half_dim = rows.shape[-1] // 2
    first_half = rows[:, :half_dim]
    second_half = rows[:, half_dim:]
    return jnp.concatenate(
        [
            first_half * cosine - second_half * sine_part,
            second_half * cosine + first_half * sine_part,
        ],
        axis=-1,
    )


def length_of(prompt, real_lengths):
    one_hot = prompt[:, None] == jnp.arange(real_lengths.shape[0], dtype=jnp.int32)[None, :]
    return jnp.sum(jnp.where(one_hot, real_lengths[None, :], 0), axis=1)


def prompt_split(slot_ids, slot_len, stagger, prompt_count):
    prompt = jnp.minimum((slot_ids + stagger) // slot_len, prompt_count - 1)
    start = jnp.maximum(prompt * slot_len - stagger, 0)
    return (prompt, slot_ids - start)


def key_rules(query_ids, key_ids, slot_len, stagger, total_slots, real_lengths):
    prompt_count = real_lengths.shape[0]
    key_prompt, key_pos = prompt_split(key_ids, slot_len, stagger, prompt_count)
    query_prompt = prompt_split(query_ids, slot_len, stagger, prompt_count)[0]
    inside = (key_ids >= 0) & (key_ids < total_slots)
    key_live = inside & (key_pos < length_of(key_prompt, real_lengths))
    same_prompt = query_prompt[:, None] == key_prompt[None, :]
    nearby = jnp.abs(query_ids[:, None] - key_ids[None, :]) < HALF_WIN
    return same_prompt & nearby & key_live[None, :]


def parts_of(values, count):
    rest = values
    pieces = []
    for _ in range(count):
        piece = lax.reduce_precision(rest, 8, 7)
        rest = rest - piece
        pieces.append(piece.astype(jnp.bfloat16))
    return pieces


def attend(softmax_state, query_rows, key_rows, value_rows, allowed):
    running_max, denominator, accumulated = softmax_state
    scores = lax.dot_general(
        query_rows, key_rows, (((1,), (1,)), ((), ())), preferred_element_type=jnp.float32
    ) * HEAD ** (-0.5)
    scores = jnp.where(allowed, scores, MASKED)
    new_max = jnp.maximum(running_max, jnp.max(scores, axis=1, keepdims=True))
    rescale = jnp.exp(running_max - new_max)
    weight_tensors = jnp.exp(scores - new_max)
    denominator = denominator * rescale + jnp.sum(weight_tensors, axis=1, keepdims=True)
    high, low = parts_of(weight_tensors, 2)
    accumulated = (
        accumulated * rescale
        + jnp.dot(high, value_rows, preferred_element_type=jnp.float32)
        + jnp.dot(low, value_rows, preferred_element_type=jnp.float32)
    )
    return (new_max, denominator, accumulated)


def order_body(order_ref, gate_ref, up_ref, down_ref, gate_out, up_out, down_out):
    gate_out[...] = gate_ref[...].astype(jnp.bfloat16)
    up_out[...] = up_ref[...].astype(jnp.bfloat16)
    down_out[...] = down_ref[...].astype(jnp.bfloat16)


def order_experts(layout_map, gate, up, down):
    count, rows, width = gate.shape
    source = pl.BlockSpec((1, rows, width), lambda place, order: (order[place], 0, 0))
    target = pl.BlockSpec((1, rows, width), lambda place, order: (place, 0, 0))
    return pl.pallas_call(
        order_body,
        grid_spec=pltpu.PrefetchScalarGridSpec(
            num_scalar_prefetch=1,
            grid=(count,),
            in_specs=[source, source, source],
            out_specs=[target, target, target],
        ),
        out_shape=[jax.ShapeDtypeStruct((count, rows, width), jnp.bfloat16)] * 3,
        cost_estimate=SMALL,
        name="order_experts",
    )(layout_map, gate, up, down)


def pack_body(query_ref, key_ref, value_ref, out_ref):
    heads = query_ref.shape[1] // HEAD
    for place in range(out_ref.shape[0]):
        head = place % heads
        for k, source in enumerate((query_ref, key_ref, value_ref)):
            out_ref[place, :, k * HEAD : (k + 1) * HEAD] = source[
                :, head * HEAD : (head + 1) * HEAD
            ].astype(jnp.bfloat16)


def pack_heads(w_query, w_key, w_value, copies):
    rows, width = w_query.shape
    places = copies * (width // HEAD)
    step = rows // 4 if rows % 64 == 0 else rows
    source = pl.BlockSpec((step, width), lambda place: (place, 0))
    return pl.pallas_call(
        pack_body,
        grid=(rows // step,),
        in_specs=[source, source, source],
        out_specs=pl.BlockSpec((places, step, 3 * HEAD), lambda place: (0, place, 0)),
        out_shape=jax.ShapeDtypeStruct((places, rows, 3 * HEAD), jnp.bfloat16),
        compiler_params=pltpu.CompilerParams(vmem_limit_bytes=32 * 2**20),
        cost_estimate=SMALL,
        name="pack_heads",
    )(w_query, w_key, w_value)


def project_body(turn_count, share, start_ref, *refs):
    rows, (weight_ref, cosine_ref, sine_ref, out_ref) = (refs[:turn_count], refs[turn_count:])
    product = 0.0
    for turn in range(turn_count):
        first = pl.multiple_of(start_ref[turn], share)
        product = product + jnp.dot(
            rows[turn][...], weight_ref[pl.ds(first, share), :], preferred_element_type=jnp.float32
        )
    cosine, sine_part = (cosine_ref[...], sine_ref[...])
    out_ref[:, :HEAD] = rotate(product[:, :HEAD], cosine, sine_part).astype(jnp.bfloat16)
    out_ref[:, HEAD : 2 * HEAD] = rotate(
        product[:, HEAD : 2 * HEAD], cosine, sine_part
    ).astype(jnp.bfloat16)
    out_ref[:, 2 * HEAD :] = product[:, 2 * HEAD :].astype(jnp.bfloat16)


def project(starts, row_blocks, weights, cosine, sine_part):
    row_count, share = row_blocks[0].shape
    step = row_count // 4
    whole = pl.BlockSpec(weights.shape, lambda place, starts: (0, 0))
    angle = pl.BlockSpec((step, cosine.shape[1]), lambda place, starts: (place, 0))
    return pl.pallas_call(
        lambda *refs: project_body(len(row_blocks), share, *refs),
        grid_spec=pltpu.PrefetchScalarGridSpec(
            num_scalar_prefetch=1,
            grid=(4,),
            in_specs=[pl.BlockSpec((step, share), lambda place, starts: (place, 0))]
            * len(row_blocks)
            + [whole, angle, angle],
            out_specs=pl.BlockSpec((step, weights.shape[1]), lambda place, starts: (place, 0)),
        ),
        out_shape=jax.ShapeDtypeStruct((row_count, weights.shape[1]), jnp.bfloat16),
        compiler_params=pltpu.CompilerParams(vmem_limit_bytes=32 * 2**20),
        cost_estimate=SMALL,
        name="project",
    )(starts, *row_blocks, weights, cosine, sine_part)


def attend_body(sink_ref, query_prompt_ref, key_prompt_ref, query_ref, key_ref, value_ref, out_ref):
    sink = sink_ref[0]
    scores = lax.dot_general(
        query_ref[...],
        key_ref[...],
        (((1,), (1,)), ((), ())),
        preferred_element_type=jnp.float32,
    ) * HEAD ** (-0.5)
    scores = jnp.where(query_prompt_ref[...] == key_prompt_ref[...], scores, MASKED)
    top = jnp.maximum(sink, jnp.max(scores, axis=1, keepdims=True))
    weights = jnp.exp(scores - top)
    denominator = jnp.exp(sink - top) + jnp.sum(weights, axis=1, keepdims=True)
    high = weights.astype(jnp.bfloat16)
    low = (weights - high.astype(jnp.float32)).astype(jnp.bfloat16)
    values = value_ref[...]
    mix = jnp.dot(high, values, preferred_element_type=jnp.float32) + jnp.dot(
        low, values, preferred_element_type=jnp.float32
    )
    out_ref[...] = (mix / denominator).astype(jnp.bfloat16)


def attend_once(sink, query_prompt, key_prompt, rows):
    row_count = rows.shape[0]
    steps = 4 if row_count % 64 == 0 else 1
    step = row_count // steps
    return pl.pallas_call(
        attend_body,
        grid=(steps,),
        in_specs=[
            pl.BlockSpec(memory_space=pltpu.SMEM),
            pl.BlockSpec((step, 1), lambda place: (place, 0)),
            pl.BlockSpec((1, row_count), lambda place: (0, 0)),
            pl.BlockSpec((step, HEAD), lambda place: (place, 0)),
            pl.BlockSpec((row_count, HEAD), lambda place: (0, 1)),
            pl.BlockSpec((row_count, HEAD), lambda place: (0, 2)),
        ],
        out_specs=pl.BlockSpec((step, HEAD), lambda place: (place, 0)),
        out_shape=jax.ShapeDtypeStruct((row_count, HEAD), jnp.bfloat16),
        compiler_params=pltpu.CompilerParams(vmem_limit_bytes=32 * 2**20),
        cost_estimate=SMALL,
        name="attend_once",
    )(sink, query_prompt[:, None], key_prompt[None, :], rows, rows, rows)


def settle_body(piece_count, width, place_ref, *refs):
    pieces = refs[:piece_count]
    token_ref, gain_ref, router_ref, full_ref, outgoing_ref, logit_ref, router_all = refs[
        piece_count:
    ]
    for place in range(full_ref.shape[1] // width):
        here = slice(place * width, (place + 1) * width)
        there = pl.ds(pl.multiple_of(place_ref[place] * width, width), width)
        block = sum(piece[:, there] for piece in pieces)
        full_ref[:, here] = token_ref[:, here].astype(jnp.float32) + block
        router_all[:, here] = router_ref[:, there]
    outgoing = rms_scale(full_ref[...], gain_ref[...]).astype(jnp.bfloat16)
    outgoing_ref[...] = outgoing
    logit_ref[...] = lax.dot_general(
        outgoing,
        router_all[...],
        (((1,), (1,)), ((), ())),
        preferred_element_type=jnp.float32,
    )


def settle(places, pieces, tokens, gain, router, width):
    rows, columns = tokens.shape
    vmem = pl.BlockSpec(memory_space=pltpu.VMEM)
    return pl.pallas_call(
        lambda *refs: settle_body(len(pieces), width, *refs),
        in_specs=[pl.BlockSpec(memory_space=pltpu.SMEM)] + [vmem] * (len(pieces) + 3),
        out_specs=[vmem] * 3,
        out_shape=[
            jax.ShapeDtypeStruct((rows, columns), jnp.float32),
            jax.ShapeDtypeStruct((rows, columns), jnp.bfloat16),
            jax.ShapeDtypeStruct((rows, router.shape[0]), jnp.float32),
        ],
        scratch_shapes=[pltpu.VMEM(router.shape, jnp.bfloat16)],
        compiler_params=pltpu.CompilerParams(vmem_limit_bytes=32 * 2**20),
        cost_estimate=SMALL,
        name="settle",
    )(places, *pieces, tokens, gain[None, :], router)


def expert_body(turn_count, share, in_ref, out_ref, *refs):
    rows, (gate_ref, up_ref, down_ref) = (refs[:turn_count], refs[turn_count : turn_count + 3])
    outs = refs[turn_count + 3 : 2 * turn_count + 3]
    sums = refs[2 * turn_count + 3 :]
    block = pl.program_id(1)
    gate = up = 0.0
    for turn in range(turn_count):
        here = pl.ds(pl.multiple_of(in_ref[turn], share), share)
        gate = gate + jnp.dot(
            rows[turn][0], gate_ref[0, here, :], preferred_element_type=jnp.float32
        )
        up = up + jnp.dot(rows[turn][0], up_ref[0, here, :], preferred_element_type=jnp.float32)
    state = (gate / (1.0 + jnp.exp(-gate)) * up).astype(jnp.bfloat16)
    for turn in range(turn_count):
        here = pl.ds(pl.multiple_of(out_ref[turn], share), share)
        down = lax.dot_general(
            state,
            down_ref[0, here, :],
            (((1,), (1,)), ((), ())),
            preferred_element_type=jnp.float32,
        )

        @pl.when(block == 0)
        def _():
            sums[turn][...] = down

        @pl.when(block > 0)
        def _():
            outs[turn][0] = (sums[turn][...] + down).astype(jnp.bfloat16)


def experts(in_starts, out_starts, row_blocks, weights):
    local_experts, row_count, share = row_blocks[0].shape
    rows, width = weights[0].shape[1:]
    block = pl.BlockSpec((1, row_count, share), lambda e, f, a, b: (e, 0, 0))
    some = pl.BlockSpec((1, rows, width // 2), lambda e, f, a, b: (e, 0, f))
    count = len(row_blocks)
    return pl.pallas_call(
        lambda *refs: expert_body(count, share, *refs),
        grid_spec=pltpu.PrefetchScalarGridSpec(
            num_scalar_prefetch=2,
            grid=(local_experts, 2),
            in_specs=[block] * count + [some] * 3,
            out_specs=[block] * count,
            scratch_shapes=[pltpu.VMEM((row_count, share), jnp.float32)] * count,
        ),
        out_shape=[jax.ShapeDtypeStruct(row_blocks[0].shape, jnp.bfloat16)] * count,
        compiler_params=pltpu.CompilerParams(vmem_limit_bytes=52 * 2**20),
        cost_estimate=SMALL,
        name="experts",
    )(in_starts, out_starts, *row_blocks, *weights)


def shards(
    tokens,
    attn_gain,
    mlp_gain,
    w_query,
    w_key,
    w_value,
    w_out,
    sink_logits,
    router,
    expert_gate,
    expert_up,
    expert_down,
    layout_map,
    real_lengths,
    routes,
):
    token_count, model_width = tokens.shape
    seq_count = lax.axis_size("seq")
    tp_count = lax.axis_size("tp")
    expert_count = router.shape[1]
    route_count = routes.shape[1]
    head_count = sink_logits.shape[0]
    col_share = model_width // tp_count
    total_slots = token_count * seq_count
    prompt_count = real_lengths.shape[0]
    slot_len = total_slots // prompt_count
    stagger = token_count // 2
    capacity = max(2, min(token_count, 9 * token_count * route_count // (8 * expert_count)))
    part_count = seq_count // head_count
    part_slots = head_count * token_count
    local_experts = expert_count // seq_count
    seq_place = lax.axis_index("seq")
    tp_place = lax.axis_index("tp")
    part = seq_place // head_count
    head = seq_place % head_count

    def tp_blocks(value):
        return [value] + [from_turned(value, "tp", turn) for turn in range(1, tp_count)]

    offsets = jnp.arange(token_count, dtype=jnp.int32)
    turns = jnp.arange(head_count, dtype=jnp.int32)
    aligned = part_count == prompt_count and part_slots + stagger <= HALF_WIN
    group_masks = masks_below(head_count)
    groups = [[first + k for k in range(head_count)] for first in range(0, seq_count, head_count)]
    part_masks = masks_below(seq_count, head_count)

    head_weights = lax.all_to_all(
        pack_heads(w_query, w_key, w_value, part_count),
        "seq",
        split_axis=0,
        concat_axis=0,
        tiled=True,
    ).reshape(model_width, 3 * HEAD)

    normed = rms_scale(tokens.astype(jnp.float32), attn_gain).astype(jnp.bfloat16)
    share = lax.dynamic_slice_in_dim(normed, tp_place * col_share, col_share, 1)
    all_routes, part_turns = doubled(routes[None], part_masks, 0)
    if aligned:
        edge = from_behind(share[token_count - stagger :], "seq", head_count)
        edge = jnp.where(head == head_count - 1, edge, jnp.zeros((), jnp.bfloat16))
    out_all, _ = doubled(
        jnp.concatenate([w_out, router.T], axis=0).astype(jnp.bfloat16), part_masks, 1
    )
    first_rows, first_turns = doubled(share[None], group_masks[:1], 0)
    first_rows, all_routes, out_all, layout_map = lax.optimization_barrier(
        (first_rows, all_routes, out_all, layout_map)
    )
    out_all = lax.all_gather(out_all, "seq", axis=1, tiled=True, axis_index_groups=groups)
    own_gate, own_up, own_down = order_experts(layout_map, expert_gate, expert_up, expert_down)
    part_ids = (part * head_count + (head ^ turns))[:, None] * token_count + offsets[None, :]
    part_ids = part_ids.reshape(-1)
    if aligned:
        edge_ids = part * part_slots - stagger + jnp.arange(stagger, dtype=jnp.int32)
        part_ids = jnp.concatenate([part_ids, edge_ids])
    part_positions = prompt_split(part_ids, slot_len, stagger, prompt_count)[1]
    half_dim = HEAD // 2
    frequency = ROPE_BASE ** (-jnp.arange(half_dim, dtype=jnp.float32) / half_dim)
    angles = part_positions.astype(jnp.float32)[:, None] * frequency[None, :]
    cosine = jnp.cos(angles)
    sine_part = jnp.sin(angles)
    pieces = []
    for piece, masks in (
        (first_rows[:, :, : col_share // 2], group_masks[1:]),
        (first_rows[:, :, col_share // 2 :], group_masks[1:][::-1]),
    ):
        known = first_turns
        for mask in masks:
            if mask == masks[-1]:
                piece, own_gate, cosine, sine_part = lax.optimization_barrier(
                    (piece, own_gate, cosine, sine_part)
                )
            piece = jnp.concatenate([piece, swapped(piece, "seq", mask)], axis=0)
            known = known + [turn ^ mask for turn in known]
        pieces.append(jnp.concatenate([piece[known.index(m)] for m in range(head_count)], axis=0))
    part_rows = jnp.concatenate(pieces, axis=1)
    if aligned:
        for mask in group_masks:
            edge = edge + swapped(edge, "seq", mask)
        part_rows = jnp.concatenate([part_rows, edge], axis=0)

    def to_owner(blocks):
        taken = lax.all_to_all(blocks, "seq", split_axis=0, concat_axis=0, tiled=True)
        taken = taken.reshape(seq_count, local_experts, *blocks.shape[1:])
        return jnp.swapaxes(taken, 0, 1).reshape(local_experts, model_width, blocks.shape[2])

    own_gate, head_weights = lax.optimization_barrier((own_gate, head_weights))
    server_gate = to_owner(own_gate)

    def by_place(blocks):
        return jnp.stack(
            [
                lax.dynamic_index_in_dim(blocks, head ^ place, 0, keepdims=False)
                for place in range(head_count)
            ]
        )

    expert_ids = jnp.arange(expert_count, dtype=jnp.int32)
    block_rows = local_experts * capacity
    columns = jnp.arange(head_count * block_rows, dtype=jnp.int32)
    column_owner = part * head_count + columns // block_rows
    column_expert = column_owner * local_experts + columns // capacity % local_experts
    spread = (column_expert[None, :] == expert_ids[:, None]).astype(jnp.bfloat16)
    wanted = (columns % capacity).astype(jnp.float32)
    earlier = (offsets[:, None] > offsets[None, :]).astype(jnp.bfloat16)

    def routing(turn, own_routes):
        ids = (seq_place ^ turn) * token_count + offsets
        prompt, position = prompt_split(ids, slot_len, stagger, prompt_count)
        valid_token = position < length_of(prompt, real_lengths)
        chosen = jnp.any(own_routes[:, :, None] == expert_ids[None, None, :], axis=1)
        live = chosen & valid_token[:, None]
        rank = jnp.dot(earlier, live.astype(jnp.bfloat16), preferred_element_type=jnp.float32)
        rank = jnp.where(live, rank, -1.0).astype(jnp.bfloat16)
        placed = jnp.dot(rank, spread, preferred_element_type=jnp.float32) == wanted[None, :]
        return (chosen, valid_token, placed)

    routings = [routing(turn, all_routes[k]) for k, turn in enumerate(part_turns)]
    chosen, valid_token, _ = routings[0]

    starts = (tp_place + jnp.arange(tp_count, dtype=jnp.int32)) % tp_count * col_share
    rows = project(starts, tp_blocks(part_rows), head_weights, cosine, sine_part)
    sink = lax.dynamic_slice_in_dim(sink_logits, head, 1, 0)

    def start_state(row_count):
        return (
            jnp.broadcast_to(sink[:, None], (row_count, 1)),
            jnp.ones((row_count, 1), jnp.float32),
            jnp.zeros((row_count, HEAD), jnp.float32),
        )

    if aligned:
        row_prompt, row_position = prompt_split(part_ids, slot_len, stagger, prompt_count)
        row_live = (part_ids >= 0) & (row_position < length_of(row_prompt, real_lengths))
        mixed = attend_once(sink, row_prompt, jnp.where(row_live, row_prompt, -1), rows)
        mixed, server_gate = lax.optimization_barrier((mixed, server_gate))
        by_slot = by_place(mixed[:part_slots].reshape(head_count, token_count, HEAD))
        by_slot = jnp.concatenate([mixed[part_slots:], by_slot.reshape(part_slots, HEAD)], axis=0)
        by_slot = lax.dynamic_update_slice_in_dim(
            jnp.zeros((stagger + total_slots, HEAD), jnp.bfloat16), by_slot, part * part_slots, 0
        )[stagger:]
        taken = lax.all_to_all(
            by_slot.reshape(seq_count, token_count, HEAD),
            "seq",
            split_axis=0,
            concat_axis=0,
            tiled=True,
        )
        kept = lax.dynamic_slice_in_dim(taken, part * head_count, head_count, 0)
        next_part = jnp.minimum(part + 1, part_count - 1)
        moved = lax.dynamic_slice_in_dim(taken, next_part * head_count, head_count, 0)
        is_moved = (head == head_count - 1) & (offsets >= token_count - stagger)
        attention_result = jnp.where(is_moved[None, :, None], moved, kept)
    else:
        query_rows, key_rows, value_rows = (rows[:, k * HEAD : (k + 1) * HEAD] for k in range(3))
        softmax_state = attend(
            start_state(part_slots),
            query_rows,
            key_rows,
            value_rows,
            key_rules(part_ids, part_ids, slot_len, stagger, total_slots, real_lengths),
        )
        from_below = from_above = jnp.concatenate([key_rows, value_rows], axis=1)
        for turn in range(1, min(part_count - 1, -(-HALF_WIN // part_slots)) + 1):
            from_below = from_behind(from_below, "seq", head_count)
            from_above = from_behind(from_above, "seq", -head_count)
            reach = turn * part_slots
            key_ids = jnp.concatenate([part_ids - reach, part_ids + reach])
            pair = jnp.concatenate([from_below, from_above], axis=0)
            softmax_state = attend(
                softmax_state,
                query_rows,
                pair[:, :HEAD],
                pair[:, HEAD:],
                key_rules(part_ids, key_ids, slot_len, stagger, total_slots, real_lengths),
            )
        _, denominator, accumulated = softmax_state
        mixed = (accumulated / denominator).astype(jnp.bfloat16)
        mixed, server_gate = lax.optimization_barrier((mixed, server_gate))
        attention_result = lax.all_to_all(
            by_place(mixed.reshape(head_count, token_count, HEAD)),
            "seq",
            split_axis=0,
            concat_axis=0,
            tiled=True,
            axis_index_groups=groups,
        )
    attention_result, own_up = lax.optimization_barrier((attention_result, own_up))
    server_up = to_owner(own_up)

    proj_width = head_count * HEAD
    partial_out = jnp.dot(
        jnp.swapaxes(attention_result, 0, 1).reshape(token_count, proj_width),
        out_all[:proj_width],
        preferred_element_type=jnp.float32,
    )
    if tp_count == 2:
        out_pieces = [partial_out, from_turned(partial_out, "tp", 1)]
    else:
        out_pieces = [lax.psum(partial_out, "tp")]
    router_rows = out_all[proj_width:]
    slots = jnp.arange(seq_count, dtype=jnp.int32)
    turn = part ^ (slots // head_count)
    bits = len(part_masks)
    turn = sum(((turn >> k) & 1) << (bits - 1 - k) for k in range(bits))
    out_places = slots % head_count * part_count + turn
    width = w_out.shape[1]
    if width % 128:

        def in_order(value):
            blocks = [
                lax.dynamic_slice_in_dim(value, out_places[place] * width, width, 1)
                for place in range(seq_count)
            ]
            return jnp.concatenate(blocks, axis=1)

        out_pieces, router_rows = ([in_order(piece) for piece in out_pieces], in_order(router_rows))
        out_places, width = (jnp.zeros((1,), jnp.int32), model_width)
    full_rows, outgoing, logits = settle(
        out_places, out_pieces, tokens, mlp_gain, router_rows, width
    )
    residual = lax.dynamic_slice_in_dim(full_rows, tp_place * col_share, col_share, 1)
    outgoing_share = lax.dynamic_slice_in_dim(outgoing, tp_place * col_share, col_share, 1)


    route_logits = jnp.where(chosen, logits, -jnp.inf)
    route_exp = jnp.exp(route_logits - jnp.max(route_logits, axis=1, keepdims=True))
    route_weight = route_exp / jnp.sum(route_exp, axis=1, keepdims=True)
    route_weight = route_weight * valid_token[:, None]
    all_weights, _ = doubled(route_weight[None], part_masks, 0)
    all_rows, _ = doubled(outgoing_share[None], part_masks, 0)
    all_rows, all_weights, own_down = lax.optimization_barrier((all_rows, all_weights, own_down))
    server_down = to_owner(own_down)
    buffer = jnp.stack(
        [
            lax.dot_general(
                placed.astype(jnp.bfloat16),
                all_rows[k],
                (((0,), (0,)), ((), ())),
                preferred_element_type=jnp.float32,
            )
            .astype(jnp.bfloat16)
            .reshape(head_count, block_rows, col_share)
            for k, (_, _, placed) in enumerate(routings)
        ],
        axis=1,
    )
    def to_mate(m):
        block = lax.dynamic_index_in_dim(buffer, head ^ m, 0, keepdims=False)
        return swapped(block, "seq", m) if m else block

    received = by_place(jnp.stack([to_mate(m) for m in range(head_count)]))
    received = received.reshape(head_count, part_count, local_experts, capacity, col_share)
    turn_ids = jnp.arange(tp_count, dtype=jnp.int32)
    in_starts = (tp_place + turn_ids) % tp_count * col_share
    out_starts = (tp_place - turn_ids) % tp_count * col_share

    halves = [
        tp_blocks(jnp.moveaxis(rows, 2, 0).reshape(local_experts, -1, col_share))
        for rows in (received[:, 1:], received[:, :1])
    ]
    server = (server_gate, server_up, server_down)
    halves, server = lax.optimization_barrier((halves, server))

    def through_experts(row_blocks, parts):
        outs = experts(in_starts, out_starts, row_blocks, server)
        outs = [outs[0]] + [from_turned(outs[k], "tp", k) for k in range(1, tp_count)]
        summed = sum(piece.astype(jnp.float32) for piece in outs).astype(jnp.bfloat16)
        summed = summed.reshape(local_experts, head_count, parts, capacity, col_share)
        return jnp.moveaxis(summed, 0, 2).reshape(head_count, parts, block_rows, col_share)

    others = through_experts(halves[0], part_count - 1)
    own_rows = through_experts(halves[1], 1)

    def weighted(k, rows):
        placed = routings[k][2]
        stacked = jnp.concatenate(
            [
                jnp.where(
                    placed, jnp.dot(piece, spread, preferred_element_type=jnp.float32), 0.0
                ).astype(jnp.bfloat16)
                for piece in parts_of(all_weights[k], 3)
            ],
            axis=0,
        )
        mixes = jnp.dot(stacked, rows, preferred_element_type=jnp.float32)
        return sum(mixes[k * token_count : (k + 1) * token_count] for k in range(3))

    def back(blocks):
        return lax.all_to_all(
            blocks, "seq", split_axis=0, concat_axis=0, tiled=True, axis_index_groups=groups
        )

    others = back(others)
    mixes = [
        weighted(k, others[:, k - 1].reshape(-1, col_share)) for k in range(1, len(part_turns))
    ]
    mixes, own_rows = lax.optimization_barrier((mixes, own_rows))
    expert_mix = sum(
        swapped(mix.astype(jnp.bfloat16), "seq", turn).astype(jnp.float32)
        for mix, turn in zip(mixes, part_turns[1:])
    )
    own_mix = weighted(0, back(own_rows)[:, 0].reshape(-1, col_share))
    return (residual + (expert_mix + own_mix)).astype(jnp.bfloat16)


def solution(mesh):
    placed = (
        P("seq", None),
        P(),
        P(),
        P("seq", "tp"),
        P("seq", "tp"),
        P("seq", "tp"),
        P("tp", "seq"),
        P("tp"),
        P("seq", None),
        P(None, "seq", "tp"),
        P(None, "seq", "tp"),
        P(None, "seq", "tp"),
        P(),
        P(),
        P("seq", None),
    )
    return jax.shard_map(
        shards, mesh=mesh, in_specs=placed, out_specs=P("seq", "tp"), check_vma=False
    )
```

```python
import jax
import jax.numpy as jnp
from jax import lax
from jax.experimental import pallas as pl
from jax.experimental.pallas import tpu as pltpu
from jax.sharding import PartitionSpec as P

HEAD = 128
HALF_WIN = 2048


EPSILON = 1e-05
ROPE_BASE = 50000.0
MASKED = -1e30
SMALL = pl.CostEstimate(flops=1, bytes_accessed=1, transcendentals=1)


def from_behind(value, axis, steps):
    count = lax.axis_size(axis)
    first, last = (max(0, -steps), min(count, count - steps))
    return lax.ppermute(value, axis, [(source, source + steps) for source in range(first, last)])


def from_turned(value, axis, turn):
    count = lax.axis_size(axis)
    return lax.ppermute(value, axis, [((place + turn) % count, place) for place in range(count)])


def swapped(value, axis, mask):
    count = lax.axis_size(axis)
    return lax.ppermute(value, axis, [(place, place ^ mask) for place in range(count)])


def doubled(value, masks, axis):
    turns = [0]
    for mask in masks:
        value = jnp.concatenate([value, swapped(value, "seq", mask)], axis=axis)
        turns = turns + [turn ^ mask for turn in turns]
    return (value, turns)


def masks_below(count, least=1):
    masks = []
    while count > least:
        count //= 2
        masks.append(count)
    return masks


def rms_scale(row_values, gain_vector):
    mean_square = jnp.mean(row_values * row_values, axis=-1, keepdims=True)
    return row_values * lax.rsqrt(mean_square + EPSILON) * gain_vector


def rotate(rows, cosine, sine_part):
    half_dim = rows.shape[-1] // 2
    first_half = rows[:, :half_dim]
    second_half = rows[:, half_dim:]
    return jnp.concatenate(
        [
            first_half * cosine - second_half * sine_part,
            second_half * cosine + first_half * sine_part,
        ],
        axis=-1,
    )


def length_of(prompt, real_lengths):
    one_hot = prompt[:, None] == jnp.arange(real_lengths.shape[0], dtype=jnp.int32)[None, :]
    return jnp.sum(jnp.where(one_hot, real_lengths[None, :], 0), axis=1)


def prompt_split(slot_ids, slot_len, stagger, prompt_count):
    prompt = jnp.minimum((slot_ids + stagger) // slot_len, prompt_count - 1)
    start = jnp.maximum(prompt * slot_len - stagger, 0)
    return (prompt, slot_ids - start)


def key_rules(query_ids, key_ids, slot_len, stagger, total_slots, real_lengths):
    prompt_count = real_lengths.shape[0]
    key_prompt, key_pos = prompt_split(key_ids, slot_len, stagger, prompt_count)
    query_prompt = prompt_split(query_ids, slot_len, stagger, prompt_count)[0]
    inside = (key_ids >= 0) & (key_ids < total_slots)
    key_live = inside & (key_pos < length_of(key_prompt, real_lengths))
    same_prompt = query_prompt[:, None] == key_prompt[None, :]
    nearby = jnp.abs(query_ids[:, None] - key_ids[None, :]) < HALF_WIN
    return same_prompt & nearby & key_live[None, :]


def parts_of(values, count):
    rest = values
    pieces = []
    for _ in range(count):
        piece = lax.reduce_precision(rest, 8, 7)
        rest = rest - piece
        pieces.append(piece.astype(jnp.bfloat16))
    return pieces


def attend(softmax_state, query_rows, key_rows, value_rows, allowed):
    running_max, denominator, accumulated = softmax_state
    scores = lax.dot_general(
        query_rows, key_rows, (((1,), (1,)), ((), ())), preferred_element_type=jnp.float32
    ) * HEAD ** (-0.5)
    scores = jnp.where(allowed, scores, MASKED)
    new_max = jnp.maximum(running_max, jnp.max(scores, axis=1, keepdims=True))
    rescale = jnp.exp(running_max - new_max)
    weight_tensors = jnp.exp(scores - new_max)
    denominator = denominator * rescale + jnp.sum(weight_tensors, axis=1, keepdims=True)
    high, low = parts_of(weight_tensors, 2)
    accumulated = (
        accumulated * rescale
        + jnp.dot(high, value_rows, preferred_element_type=jnp.float32)
        + jnp.dot(low, value_rows, preferred_element_type=jnp.float32)
    )
    return (new_max, denominator, accumulated)


def order_body(order_ref, gate_ref, up_ref, down_ref, gate_out, up_out, down_out):
    gate_out[...] = gate_ref[...].astype(jnp.bfloat16)
    up_out[...] = up_ref[...].astype(jnp.bfloat16)
    down_out[...] = down_ref[...].astype(jnp.bfloat16)


def order_experts(layout_map, gate, up, down):
    count, rows, width = gate.shape
    source = pl.BlockSpec((1, rows, width), lambda place, order: (order[place], 0, 0))
    target = pl.BlockSpec((1, rows, width), lambda place, order: (place, 0, 0))
    return pl.pallas_call(
        order_body,
        grid_spec=pltpu.PrefetchScalarGridSpec(
            num_scalar_prefetch=1,
            grid=(count,),
            in_specs=[source, source, source],
            out_specs=[target, target, target],
        ),
        out_shape=[jax.ShapeDtypeStruct((count, rows, width), jnp.bfloat16)] * 3,
        cost_estimate=SMALL,
        name="order_experts",
    )(layout_map, gate, up, down)


def pack_body(query_ref, key_ref, value_ref, out_ref):
    heads = query_ref.shape[1] // HEAD
    for place in range(out_ref.shape[0]):
        head = place % heads
        for k, source in enumerate((query_ref, key_ref, value_ref)):
            out_ref[place, :, k * HEAD : (k + 1) * HEAD] = source[
                :, head * HEAD : (head + 1) * HEAD
            ].astype(jnp.bfloat16)


def pack_heads(w_query, w_key, w_value, copies):
    rows, width = w_query.shape
    places = copies * (width // HEAD)
    step = rows // 4 if rows % 64 == 0 else rows
    source = pl.BlockSpec((step, width), lambda place: (place, 0))
    return pl.pallas_call(
        pack_body,
        grid=(rows // step,),
        in_specs=[source, source, source],
        out_specs=pl.BlockSpec((places, step, 3 * HEAD), lambda place: (0, place, 0)),
        out_shape=jax.ShapeDtypeStruct((places, rows, 3 * HEAD), jnp.bfloat16),
        compiler_params=pltpu.CompilerParams(vmem_limit_bytes=32 * 2**20),
        cost_estimate=SMALL,
        name="pack_heads",
    )(w_query, w_key, w_value)


def project_body(turn_count, share, start_ref, *refs):
    rows, (weight_ref, cosine_ref, sine_ref, out_ref) = (refs[:turn_count], refs[turn_count:])
    product = 0.0
    for turn in range(turn_count):
        first = pl.multiple_of(start_ref[turn], share)
        product = product + jnp.dot(
            rows[turn][...], weight_ref[pl.ds(first, share), :], preferred_element_type=jnp.float32
        )
    cosine, sine_part = (cosine_ref[...], sine_ref[...])
    out_ref[:, :HEAD] = rotate(product[:, :HEAD], cosine, sine_part).astype(jnp.bfloat16)
    out_ref[:, HEAD : 2 * HEAD] = rotate(
        product[:, HEAD : 2 * HEAD], cosine, sine_part
    ).astype(jnp.bfloat16)
    out_ref[:, 2 * HEAD :] = product[:, 2 * HEAD :].astype(jnp.bfloat16)


def project(starts, row_blocks, weights, cosine, sine_part):
    row_count, share = row_blocks[0].shape
    step = row_count // 4
    whole = pl.BlockSpec(weights.shape, lambda place, starts: (0, 0))
    angle = pl.BlockSpec((step, cosine.shape[1]), lambda place, starts: (place, 0))
    return pl.pallas_call(
        lambda *refs: project_body(len(row_blocks), share, *refs),
        grid_spec=pltpu.PrefetchScalarGridSpec(
            num_scalar_prefetch=1,
            grid=(4,),
            in_specs=[pl.BlockSpec((step, share), lambda place, starts: (place, 0))]
            * len(row_blocks)
            + [whole, angle, angle],
            out_specs=pl.BlockSpec((step, weights.shape[1]), lambda place, starts: (place, 0)),
        ),
        out_shape=jax.ShapeDtypeStruct((row_count, weights.shape[1]), jnp.bfloat16),
        compiler_params=pltpu.CompilerParams(vmem_limit_bytes=32 * 2**20),
        cost_estimate=SMALL,
        name="project",
    )(starts, *row_blocks, weights, cosine, sine_part)


def attend_body(sink_ref, query_prompt_ref, key_prompt_ref, query_ref, key_ref, value_ref, out_ref):
    sink = sink_ref[0]
    scores = lax.dot_general(
        query_ref[...],
        key_ref[...],
        (((1,), (1,)), ((), ())),
        preferred_element_type=jnp.float32,
    ) * HEAD ** (-0.5)
    scores = jnp.where(query_prompt_ref[...] == key_prompt_ref[...], scores, MASKED)
    top = jnp.maximum(sink, jnp.max(scores, axis=1, keepdims=True))
    weights = jnp.exp(scores - top)
    denominator = jnp.exp(sink - top) + jnp.sum(weights, axis=1, keepdims=True)
    high = weights.astype(jnp.bfloat16)
    low = (weights - high.astype(jnp.float32)).astype(jnp.bfloat16)
    values = value_ref[...]
    mix = jnp.dot(high, values, preferred_element_type=jnp.float32) + jnp.dot(
        low, values, preferred_element_type=jnp.float32
    )
    out_ref[...] = (mix / denominator).astype(jnp.bfloat16)


def attend_once(sink, query_prompt, key_prompt, rows):
    row_count = rows.shape[0]
    steps = 4 if row_count % 64 == 0 else 1
    step = row_count // steps
    return pl.pallas_call(
        attend_body,
        grid=(steps,),
        in_specs=[
            pl.BlockSpec(memory_space=pltpu.SMEM),
            pl.BlockSpec((step, 1), lambda place: (place, 0)),
            pl.BlockSpec((1, row_count), lambda place: (0, 0)),
            pl.BlockSpec((step, HEAD), lambda place: (place, 0)),
            pl.BlockSpec((row_count, HEAD), lambda place: (0, 1)),
            pl.BlockSpec((row_count, HEAD), lambda place: (0, 2)),
        ],
        out_specs=pl.BlockSpec((step, HEAD), lambda place: (place, 0)),
        out_shape=jax.ShapeDtypeStruct((row_count, HEAD), jnp.bfloat16),
        compiler_params=pltpu.CompilerParams(vmem_limit_bytes=32 * 2**20),
        cost_estimate=SMALL,
        name="attend_once",
    )(sink, query_prompt[:, None], key_prompt[None, :], rows, rows, rows)


def settle_body(piece_count, width, place_ref, *refs):
    pieces = refs[:piece_count]
    token_ref, gain_ref, router_ref, full_ref, outgoing_ref, logit_ref, router_all = refs[
        piece_count:
    ]
    for place in range(full_ref.shape[1] // width):
        here = slice(place * width, (place + 1) * width)
        there = pl.ds(pl.multiple_of(place_ref[place] * width, width), width)
        block = sum(piece[:, there] for piece in pieces)
        full_ref[:, here] = token_ref[:, here].astype(jnp.float32) + block
        router_all[:, here] = router_ref[:, there]
    outgoing = rms_scale(full_ref[...], gain_ref[...]).astype(jnp.bfloat16)
    outgoing_ref[...] = outgoing
    logit_ref[...] = lax.dot_general(
        outgoing,
        router_all[...],
        (((1,), (1,)), ((), ())),
        preferred_element_type=jnp.float32,
    )


def settle(places, pieces, tokens, gain, router, width):
    rows, columns = tokens.shape
    vmem = pl.BlockSpec(memory_space=pltpu.VMEM)
    return pl.pallas_call(
        lambda *refs: settle_body(len(pieces), width, *refs),
        in_specs=[pl.BlockSpec(memory_space=pltpu.SMEM)] + [vmem] * (len(pieces) + 3),
        out_specs=[vmem] * 3,
        out_shape=[
            jax.ShapeDtypeStruct((rows, columns), jnp.float32),
            jax.ShapeDtypeStruct((rows, columns), jnp.bfloat16),
            jax.ShapeDtypeStruct((rows, router.shape[0]), jnp.float32),
        ],
        scratch_shapes=[pltpu.VMEM(router.shape, jnp.bfloat16)],
        compiler_params=pltpu.CompilerParams(vmem_limit_bytes=32 * 2**20),
        cost_estimate=SMALL,
        name="settle",
    )(places, *pieces, tokens, gain[None, :], router)


def hidden_body(turn_count, share, start_ref, *refs):
    rows, (gate_ref, up_ref, out_ref) = (refs[:turn_count], refs[turn_count:])
    gate = up = 0.0
    for turn in range(turn_count):
        here = pl.ds(pl.multiple_of(start_ref[turn], share), share)
        gate = gate + jnp.dot(
            rows[turn][0], gate_ref[0, here, :], preferred_element_type=jnp.float32
        )
        up = up + jnp.dot(rows[turn][0], up_ref[0, here, :], preferred_element_type=jnp.float32)
    out_ref[0] = (gate / (1.0 + jnp.exp(-gate)) * up).astype(jnp.bfloat16)


def hidden_units(starts, row_blocks, gate, up):
    local_experts, row_count, share = row_blocks[0].shape
    rows, width = gate.shape[1:]
    whole = pl.BlockSpec((1, rows, width), lambda e, a: (e, 0, 0))
    count = len(row_blocks)
    return pl.pallas_call(
        lambda *refs: hidden_body(count, share, *refs),
        grid_spec=pltpu.PrefetchScalarGridSpec(
            num_scalar_prefetch=1,
            grid=(local_experts,),
            in_specs=[pl.BlockSpec((1, row_count, share), lambda e, a: (e, 0, 0))] * count
            + [whole] * 2,
            out_specs=pl.BlockSpec((1, row_count, width), lambda e, a: (e, 0, 0)),
        ),
        out_shape=jax.ShapeDtypeStruct((local_experts, row_count, width), jnp.bfloat16),
        compiler_params=pltpu.CompilerParams(vmem_limit_bytes=52 * 2**20),
        cost_estimate=SMALL,
        name="hidden_units",
    )(starts, *row_blocks, gate, up)


def down_body(turn_count, share, start_ref, hidden_ref, down_ref, *outs):
    for turn in range(turn_count):
        here = pl.ds(pl.multiple_of(start_ref[turn], share), share)
        outs[turn][0] = lax.dot_general(
            hidden_ref[0],
            down_ref[0, here, :],
            (((1,), (1,)), ((), ())),
            preferred_element_type=jnp.float32,
        ).astype(jnp.bfloat16)


def down_rows(starts, hidden, down):
    local_experts, row_count, width = hidden.shape
    columns, count = (down.shape[1], starts.shape[0])
    share = columns // count
    block = pl.BlockSpec((1, row_count, share), lambda e, a: (e, 0, 0))
    return pl.pallas_call(
        lambda *refs: down_body(count, share, *refs),
        grid_spec=pltpu.PrefetchScalarGridSpec(
            num_scalar_prefetch=1,
            grid=(local_experts,),
            in_specs=[
                pl.BlockSpec((1, row_count, width), lambda e, a: (e, 0, 0)),
                pl.BlockSpec((1, columns, width), lambda e, a: (e, 0, 0)),
            ],
            out_specs=[block] * count,
        ),
        out_shape=[jax.ShapeDtypeStruct((local_experts, row_count, share), jnp.bfloat16)] * count,
        compiler_params=pltpu.CompilerParams(vmem_limit_bytes=52 * 2**20),
        cost_estimate=SMALL,
        name="down_rows",
    )(starts, hidden, down)


def shards(
    tokens,
    attn_gain,
    mlp_gain,
    w_query,
    w_key,
    w_value,
    w_out,
    sink_logits,
    router,
    expert_gate,
    expert_up,
    expert_down,
    layout_map,
    real_lengths,
    routes,
):
    token_count, model_width = tokens.shape
    seq_count = lax.axis_size("seq")
    tp_count = lax.axis_size("tp")
    expert_count = router.shape[1]
    route_count = routes.shape[1]
    head_count = sink_logits.shape[0]
    col_share = model_width // tp_count
    total_slots = token_count * seq_count
    prompt_count = real_lengths.shape[0]
    slot_len = total_slots // prompt_count
    stagger = token_count // 2
    capacity = max(2, min(token_count, 9 * token_count * route_count // (8 * expert_count)))
    part_count = seq_count // head_count
    part_slots = head_count * token_count
    local_experts = expert_count // seq_count
    seq_place = lax.axis_index("seq")
    tp_place = lax.axis_index("tp")
    part = seq_place // head_count
    head = seq_place % head_count

    def tp_blocks(value):
        return [value] + [from_turned(value, "tp", turn) for turn in range(1, tp_count)]

    offsets = jnp.arange(token_count, dtype=jnp.int32)
    turns = jnp.arange(head_count, dtype=jnp.int32)
    aligned = part_count == prompt_count and part_slots + stagger <= HALF_WIN
    group_masks = masks_below(head_count)
    groups = [[first + k for k in range(head_count)] for first in range(0, seq_count, head_count)]
    part_masks = masks_below(seq_count, head_count)

    head_weights = lax.all_to_all(
        pack_heads(w_query, w_key, w_value, part_count),
        "seq",
        split_axis=0,
        concat_axis=0,
        tiled=True,
    ).reshape(model_width, 3 * HEAD)

    normed = rms_scale(tokens.astype(jnp.float32), attn_gain).astype(jnp.bfloat16)
    share = lax.dynamic_slice_in_dim(normed, tp_place * col_share, col_share, 1)
    all_routes, part_turns = doubled(routes[None], part_masks, 0)
    out_all, _ = doubled(
        jnp.concatenate([w_out, router.T], axis=0).astype(jnp.bfloat16), part_masks, 1
    )
    first_rows, first_turns = doubled(share[None], group_masks[:1], 0)
    first_rows, all_routes, out_all, layout_map = lax.optimization_barrier(
        (first_rows, all_routes, out_all, layout_map)
    )
    own_gate, own_up, own_down = order_experts(layout_map, expert_gate, expert_up, expert_down)
    part_ids = (part * head_count + (head ^ turns))[:, None] * token_count + offsets[None, :]
    part_ids = part_ids.reshape(-1)
    part_positions = prompt_split(part_ids, slot_len, stagger, prompt_count)[1]
    half_dim = HEAD // 2
    frequency = ROPE_BASE ** (-jnp.arange(half_dim, dtype=jnp.float32) / half_dim)
    angles = part_positions.astype(jnp.float32)[:, None] * frequency[None, :]
    cosine = jnp.cos(angles)
    sine_part = jnp.sin(angles)
    pieces = []
    for piece, masks in (
        (first_rows[:, :, : col_share // 2], group_masks[1:]),
        (first_rows[:, :, col_share // 2 :], group_masks[1:][::-1]),
    ):
        known = first_turns
        for mask in masks:
            if mask == masks[-1]:
                piece, own_gate, cosine, sine_part = lax.optimization_barrier(
                    (piece, own_gate, cosine, sine_part)
                )
            piece = jnp.concatenate([piece, swapped(piece, "seq", mask)], axis=0)
            known = known + [turn ^ mask for turn in known]
        pieces.append(jnp.concatenate([piece[known.index(m)] for m in range(head_count)], axis=0))
    part_rows = jnp.concatenate(pieces, axis=1)

    def to_owner(blocks):
        taken = lax.all_to_all(blocks, "seq", split_axis=0, concat_axis=0, tiled=True)
        taken = taken.reshape(seq_count, local_experts, *blocks.shape[1:])
        return jnp.swapaxes(taken, 0, 1).reshape(local_experts, model_width, blocks.shape[2])

    out_all, _ = doubled(out_all, group_masks[:-2], 1)
    out_rows = out_all.shape[0] // 32 * 16
    out_halves = [
        (out_all[:out_rows], group_masks[-2:]),
        (out_all[out_rows:], group_masks[-2:][::-1]),
    ]
    halves, head_weights, part_rows = lax.optimization_barrier(
        ([half for half, _ in out_halves], head_weights, part_rows)
    )
    out_halves = [
        (doubled(half, masks[:1], 1)[0], masks[1:]) for half, (_, masks) in zip(halves, out_halves)
    ]

    def by_place(blocks):
        return jnp.stack(
            [
                lax.dynamic_index_in_dim(blocks, head ^ place, 0, keepdims=False)
                for place in range(head_count)
            ]
        )

    expert_ids = jnp.arange(expert_count, dtype=jnp.int32)
    block_rows = local_experts * capacity
    columns = jnp.arange(head_count * block_rows, dtype=jnp.int32)
    column_owner = part * head_count + columns // block_rows
    column_expert = column_owner * local_experts + columns // capacity % local_experts
    spread = (column_expert[None, :] == expert_ids[:, None]).astype(jnp.bfloat16)
    wanted = (columns % capacity).astype(jnp.float32)
    earlier = (offsets[:, None] > offsets[None, :]).astype(jnp.bfloat16)

    def routing(turn, own_routes):
        ids = (seq_place ^ turn) * token_count + offsets
        prompt, position = prompt_split(ids, slot_len, stagger, prompt_count)
        valid_token = position < length_of(prompt, real_lengths)
        chosen = jnp.any(own_routes[:, :, None] == expert_ids[None, None, :], axis=1)
        live = chosen & valid_token[:, None]
        rank = jnp.dot(earlier, live.astype(jnp.bfloat16), preferred_element_type=jnp.float32)
        rank = jnp.where(live, rank, -1.0).astype(jnp.bfloat16)
        placed = jnp.dot(rank, spread, preferred_element_type=jnp.float32) == wanted[None, :]
        return (chosen, valid_token, placed)

    routings = [routing(turn, all_routes[k]) for k, turn in enumerate(part_turns)]
    chosen, valid_token, _ = routings[0]

    starts = (tp_place + jnp.arange(tp_count, dtype=jnp.int32)) % tp_count * col_share
    rows = project(starts, tp_blocks(part_rows), head_weights, cosine, sine_part)
    sink = lax.dynamic_slice_in_dim(sink_logits, head, 1, 0)

    def start_state(row_count):
        return (
            jnp.broadcast_to(sink[:, None], (row_count, 1)),
            jnp.ones((row_count, 1), jnp.float32),
            jnp.zeros((row_count, HEAD), jnp.float32),
        )

    if aligned:
        edge_start = (head ^ (head_count - 1)) * token_count + token_count - stagger
        edge = from_behind(
            lax.dynamic_slice_in_dim(rows, edge_start, stagger, 0), "seq", head_count
        )
        edge_ids = part * part_slots - stagger + jnp.arange(stagger, dtype=jnp.int32)
        row_ids = jnp.concatenate([part_ids, edge_ids])
        row_prompt, row_position = prompt_split(row_ids, slot_len, stagger, prompt_count)
        row_live = (row_ids >= 0) & (row_position < length_of(row_prompt, real_lengths))
        halves, edge = lax.optimization_barrier(([half for half, _ in out_halves], edge))
        out_halves = [(half, masks) for half, (_, masks) in zip(halves, out_halves)]
        mixed = attend_once(
            sink,
            row_prompt,
            jnp.where(row_live, row_prompt, -1),
            jnp.concatenate([rows, edge], axis=0),
        )
        edge_back = from_behind(mixed[part_slots:], "seq", -head_count)
        mixed = mixed[:part_slots]
        kept = lax.dynamic_slice_in_dim(mixed, edge_start, stagger, 0)
        mixed = lax.dynamic_update_slice_in_dim(
            mixed, jnp.where(part < part_count - 1, edge_back, kept), edge_start, 0
        )
    else:
        query_rows, key_rows, value_rows = (rows[:, k * HEAD : (k + 1) * HEAD] for k in range(3))
        softmax_state = attend(
            start_state(part_slots),
            query_rows,
            key_rows,
            value_rows,
            key_rules(part_ids, part_ids, slot_len, stagger, total_slots, real_lengths),
        )
        from_below = from_above = jnp.concatenate([key_rows, value_rows], axis=1)
        for turn in range(1, min(part_count - 1, -(-HALF_WIN // part_slots)) + 1):
            from_below = from_behind(from_below, "seq", head_count)
            from_above = from_behind(from_above, "seq", -head_count)
            reach = turn * part_slots
            key_ids = jnp.concatenate([part_ids - reach, part_ids + reach])
            pair = jnp.concatenate([from_below, from_above], axis=0)
            softmax_state = attend(
                softmax_state,
                query_rows,
                pair[:, :HEAD],
                pair[:, HEAD:],
                key_rules(part_ids, key_ids, slot_len, stagger, total_slots, real_lengths),
            )
        _, denominator, accumulated = softmax_state
        mixed = (accumulated / denominator).astype(jnp.bfloat16)
    blocks = by_place(mixed.reshape(head_count, token_count, HEAD))
    out_halves = [(half, swapped(half, "seq", masks[0])) for half, masks in out_halves]
    blocks, out_halves = lax.optimization_barrier((blocks, out_halves))
    attention_result = lax.all_to_all(
        blocks, "seq", split_axis=0, concat_axis=0, tiled=True, axis_index_groups=groups
    )
    attention_result, own_gate = lax.optimization_barrier((attention_result, own_gate))
    server_gate = to_owner(own_gate)

    proj_width = head_count * HEAD
    attention_result = jnp.swapaxes(attention_result, 0, 1).reshape(token_count, proj_width)

    def joined(pieces, half):
        if half == 0:
            return jnp.concatenate(pieces, axis=1)
        span = pieces[0].shape[1] // 2
        low, high = ([piece[:, k * span : (k + 1) * span] for piece in pieces] for k in range(2))
        return jnp.concatenate([*low, *high], axis=1)

    partial_out = sum(
        joined([jnp.dot(rows, piece, preferred_element_type=jnp.float32) for piece in pieces], half)
        for half, (rows, pieces) in enumerate(
            (
                (attention_result[:, :out_rows], out_halves[0]),
                (
                    attention_result[:, out_rows:],
                    [piece[: proj_width - out_rows] for piece in out_halves[1]],
                ),
            )
        )
    )
    if tp_count == 2:
        out_pieces = [partial_out, from_turned(partial_out, "tp", 1)]
    else:
        out_pieces = [lax.psum(partial_out, "tp")]
    router_rows = joined([piece[proj_width - out_rows :] for piece in out_halves[1]], 1)
    slots = jnp.arange(seq_count, dtype=jnp.int32)
    turn = seq_place ^ slots
    bits = len(part_masks) + len(group_masks)
    out_places = sum(((turn >> k) & 1) << (bits - 1 - k) for k in range(bits))
    width = w_out.shape[1]
    if width % 128:

        def in_order(value):
            blocks = [
                lax.dynamic_slice_in_dim(value, out_places[place] * width, width, 1)
                for place in range(seq_count)
            ]
            return jnp.concatenate(blocks, axis=1)

        out_pieces, router_rows = ([in_order(piece) for piece in out_pieces], in_order(router_rows))
        out_places, width = (jnp.zeros((1,), jnp.int32), model_width)
    full_rows, outgoing, logits = settle(
        out_places, out_pieces, tokens, mlp_gain, router_rows, width
    )
    residual = lax.dynamic_slice_in_dim(full_rows, tp_place * col_share, col_share, 1)
    outgoing_share = lax.dynamic_slice_in_dim(outgoing, tp_place * col_share, col_share, 1)


    route_logits = jnp.where(chosen, logits, -jnp.inf)
    route_exp = jnp.exp(route_logits - jnp.max(route_logits, axis=1, keepdims=True))
    route_weight = route_exp / jnp.sum(route_exp, axis=1, keepdims=True)
    route_weight = route_weight * valid_token[:, None]
    all_weights, _ = doubled(route_weight[None], part_masks, 0)
    all_rows, _ = doubled(outgoing_share[None], part_masks, 0)
    all_rows, all_weights, server_gate, own_up = lax.optimization_barrier(
        (all_rows, all_weights, server_gate, own_up)
    )
    server_up = to_owner(own_up)
    buffer = jnp.stack(
        [
            lax.dot_general(
                placed.astype(jnp.bfloat16),
                all_rows[k],
                (((0,), (0,)), ((), ())),
                preferred_element_type=jnp.float32,
            )
            .astype(jnp.bfloat16)
            .reshape(head_count, block_rows, col_share)
            for k, (_, _, placed) in enumerate(routings)
        ],
        axis=1,
    )
    def to_mate(m):
        block = lax.dynamic_index_in_dim(buffer, head ^ m, 0, keepdims=False)
        return swapped(block, "seq", m) if m else block

    received = [to_mate(m) for m in range(head_count)]
    received[1], server_up, own_down = lax.optimization_barrier((received[1], server_up, own_down))
    server_down = to_owner(own_down)
    received = by_place(jnp.stack(received))
    received = received.reshape(head_count, part_count, local_experts, capacity, col_share)
    turn_ids = jnp.arange(tp_count, dtype=jnp.int32)
    in_starts = (tp_place + turn_ids) % tp_count * col_share
    out_starts = (tp_place - turn_ids) % tp_count * col_share

    halves = [
        tp_blocks(jnp.moveaxis(rows, 2, 0).reshape(local_experts, -1, col_share))
        for rows in (received[:, 1:], received[:, :1])
    ]
    hidden = [hidden_units(in_starts, rows, server_gate, server_up) for rows in halves]
    hidden, server_down = lax.optimization_barrier((hidden, server_down))

    def through_experts(rows, parts):
        outs = down_rows(out_starts, rows, server_down)
        outs = [outs[0]] + [from_turned(outs[k], "tp", k) for k in range(1, tp_count)]
        summed = sum(piece.astype(jnp.float32) for piece in outs).astype(jnp.bfloat16)
        summed = summed.reshape(local_experts, head_count, parts, capacity, col_share)
        return jnp.moveaxis(summed, 0, 2).reshape(head_count, parts, block_rows, col_share)

    others = through_experts(hidden[0], part_count - 1)
    own_rows = through_experts(hidden[1], 1)

    def weighted(k, rows):
        placed = routings[k][2]
        stacked = jnp.concatenate(
            [
                jnp.where(
                    placed, jnp.dot(piece, spread, preferred_element_type=jnp.float32), 0.0
                ).astype(jnp.bfloat16)
                for piece in parts_of(all_weights[k], 3)
            ],
            axis=0,
        )
        mixes = jnp.dot(stacked, rows, preferred_element_type=jnp.float32)
        return sum(mixes[k * token_count : (k + 1) * token_count] for k in range(3))

    def back(blocks):
        return lax.all_to_all(
            blocks, "seq", split_axis=0, concat_axis=0, tiled=True, axis_index_groups=groups
        )

    others = back(others)
    mixes = [
        weighted(k, others[:, k - 1].reshape(-1, col_share)) for k in range(1, len(part_turns))
    ]
    mixes, own_rows = lax.optimization_barrier((mixes, own_rows))
    expert_mix = sum(
        swapped(mix.astype(jnp.bfloat16), "seq", turn).astype(jnp.float32)
        for mix, turn in zip(mixes, part_turns[1:])
    )
    own_mix = weighted(0, back(own_rows)[:, 0].reshape(-1, col_share))
    return (residual + (expert_mix + own_mix)).astype(jnp.bfloat16)


def solution(mesh):
    placed = (
        P("seq", None),
        P(),
        P(),
        P("seq", "tp"),
        P("seq", "tp"),
        P("seq", "tp"),
        P("tp", "seq"),
        P("tp"),
        P("seq", None),
        P(None, "seq", "tp"),
        P(None, "seq", "tp"),
        P(None, "seq", "tp"),
        P(),
        P(),
        P("seq", None),
    )
    return jax.shard_map(
        shards, mesh=mesh, in_specs=placed, out_specs=P("seq", "tp"), check_vma=False
    )
```

```python
import jax
import jax.numpy as jnp
from jax import lax
from jax.experimental import pallas as pl
from jax.experimental.pallas import tpu as pltpu
from jax.sharding import PartitionSpec as P

HEAD = 128
HALF_WIN = 2048


EPSILON = 1e-05
ROPE_BASE = 50000.0
MASKED = -1e30
SMALL = pl.CostEstimate(flops=1, bytes_accessed=1, transcendentals=1)


def from_behind(value, axis, steps):
    count = lax.axis_size(axis)
    first, last = (max(0, -steps), min(count, count - steps))
    return lax.ppermute(value, axis, [(source, source + steps) for source in range(first, last)])


def from_turned(value, axis, turn):
    count = lax.axis_size(axis)
    return lax.ppermute(value, axis, [((place + turn) % count, place) for place in range(count)])


def swapped(value, axis, mask):
    count = lax.axis_size(axis)
    return lax.ppermute(value, axis, [(place, place ^ mask) for place in range(count)])


def doubled(value, masks, axis):
    turns = [0]
    for mask in masks:
        value = jnp.concatenate([value, swapped(value, "seq", mask)], axis=axis)
        turns = turns + [turn ^ mask for turn in turns]
    return (value, turns)


def masks_below(count, least=1):
    masks = []
    while count > least:
        count //= 2
        masks.append(count)
    return masks


def rms_scale(row_values, gain_vector):
    mean_square = jnp.mean(row_values * row_values, axis=-1, keepdims=True)
    return row_values * lax.rsqrt(mean_square + EPSILON) * gain_vector


def rotate(rows, cosine, sine_part):
    half_dim = rows.shape[-1] // 2
    first_half = rows[:, :half_dim]
    second_half = rows[:, half_dim:]
    return jnp.concatenate(
        [
            first_half * cosine - second_half * sine_part,
            second_half * cosine + first_half * sine_part,
        ],
        axis=-1,
    )


def length_of(prompt, real_lengths):
    one_hot = prompt[:, None] == jnp.arange(real_lengths.shape[0], dtype=jnp.int32)[None, :]
    return jnp.sum(jnp.where(one_hot, real_lengths[None, :], 0), axis=1)


def prompt_split(slot_ids, slot_len, stagger, prompt_count):
    prompt = jnp.minimum((slot_ids + stagger) // slot_len, prompt_count - 1)
    start = jnp.maximum(prompt * slot_len - stagger, 0)
    return (prompt, slot_ids - start)


def key_rules(query_ids, key_ids, slot_len, stagger, total_slots, real_lengths):
    prompt_count = real_lengths.shape[0]
    key_prompt, key_pos = prompt_split(key_ids, slot_len, stagger, prompt_count)
    query_prompt = prompt_split(query_ids, slot_len, stagger, prompt_count)[0]
    inside = (key_ids >= 0) & (key_ids < total_slots)
    key_live = inside & (key_pos < length_of(key_prompt, real_lengths))
    same_prompt = query_prompt[:, None] == key_prompt[None, :]
    nearby = jnp.abs(query_ids[:, None] - key_ids[None, :]) < HALF_WIN
    return same_prompt & nearby & key_live[None, :]


def parts_of(values, count):
    rest = values
    pieces = []
    for _ in range(count):
        piece = lax.reduce_precision(rest, 8, 7)
        rest = rest - piece
        pieces.append(piece.astype(jnp.bfloat16))
    return pieces


def attend(softmax_state, query_rows, key_rows, value_rows, allowed):
    running_max, denominator, accumulated = softmax_state
    scores = lax.dot_general(
        query_rows, key_rows, (((1,), (1,)), ((), ())), preferred_element_type=jnp.float32
    ) * HEAD ** (-0.5)
    scores = jnp.where(allowed, scores, MASKED)
    new_max = jnp.maximum(running_max, jnp.max(scores, axis=1, keepdims=True))
    rescale = jnp.exp(running_max - new_max)
    weight_tensors = jnp.exp(scores - new_max)
    denominator = denominator * rescale + jnp.sum(weight_tensors, axis=1, keepdims=True)
    high, low = parts_of(weight_tensors, 2)
    accumulated = (
        accumulated * rescale
        + jnp.dot(high, value_rows, preferred_element_type=jnp.float32)
        + jnp.dot(low, value_rows, preferred_element_type=jnp.float32)
    )
    return (new_max, denominator, accumulated)


def order_body(order_ref, gate_ref, up_ref, down_ref, *outs):
    half = gate_ref.shape[2] // 2
    outs[0][...] = gate_ref[:, :, :half].astype(jnp.bfloat16)
    outs[1][...] = gate_ref[:, :, half:].astype(jnp.bfloat16)
    outs[2][...] = up_ref[...].astype(jnp.bfloat16)
    outs[3][...] = down_ref[...].astype(jnp.bfloat16)


def order_experts(layout_map, gate, up, down):
    count, rows, width = gate.shape
    source = pl.BlockSpec((1, rows, width), lambda place, order: (order[place], 0, 0))
    widths = (width // 2, width - width // 2, width, width)
    return pl.pallas_call(
        order_body,
        grid_spec=pltpu.PrefetchScalarGridSpec(
            num_scalar_prefetch=1,
            grid=(count,),
            in_specs=[source, source, source],
            out_specs=[
                pl.BlockSpec((1, rows, some), lambda place, order: (place, 0, 0))
                for some in widths
            ],
        ),
        out_shape=[jax.ShapeDtypeStruct((count, rows, some), jnp.bfloat16) for some in widths],
        cost_estimate=SMALL,
        name="order_experts",
    )(layout_map, gate, up, down)


def pack_body(query_ref, key_ref, value_ref, out_ref):
    heads = query_ref.shape[1] // HEAD
    for place in range(out_ref.shape[0]):
        head = place % heads
        for k, source in enumerate((query_ref, key_ref, value_ref)):
            out_ref[place, :, k * HEAD : (k + 1) * HEAD] = source[
                :, head * HEAD : (head + 1) * HEAD
            ].astype(jnp.bfloat16)


def pack_heads(w_query, w_key, w_value, copies):
    rows, width = w_query.shape
    places = copies * (width // HEAD)
    step = rows // 4 if rows % 64 == 0 else rows
    source = pl.BlockSpec((step, width), lambda place: (place, 0))
    return pl.pallas_call(
        pack_body,
        grid=(rows // step,),
        in_specs=[source, source, source],
        out_specs=pl.BlockSpec((places, step, 3 * HEAD), lambda place: (0, place, 0)),
        out_shape=jax.ShapeDtypeStruct((places, rows, 3 * HEAD), jnp.bfloat16),
        compiler_params=pltpu.CompilerParams(vmem_limit_bytes=32 * 2**20),
        cost_estimate=SMALL,
        name="pack_heads",
    )(w_query, w_key, w_value)


def project_body(turn_count, share, start_ref, *refs):
    rows, (weight_ref, cosine_ref, sine_ref, out_ref) = (refs[:turn_count], refs[turn_count:])
    product = 0.0
    for turn in range(turn_count):
        first = pl.multiple_of(start_ref[turn], share)
        product = product + jnp.dot(
            rows[turn][...], weight_ref[pl.ds(first, share), :], preferred_element_type=jnp.float32
        )
    cosine, sine_part = (cosine_ref[...], sine_ref[...])
    out_ref[:, :HEAD] = rotate(product[:, :HEAD], cosine, sine_part).astype(jnp.bfloat16)
    out_ref[:, HEAD : 2 * HEAD] = rotate(
        product[:, HEAD : 2 * HEAD], cosine, sine_part
    ).astype(jnp.bfloat16)
    out_ref[:, 2 * HEAD :] = product[:, 2 * HEAD :].astype(jnp.bfloat16)


def project(starts, row_blocks, weights, cosine, sine_part):
    row_count, share = row_blocks[0].shape
    step = row_count // 4
    whole = pl.BlockSpec(weights.shape, lambda place, starts: (0, 0))
    angle = pl.BlockSpec((step, cosine.shape[1]), lambda place, starts: (place, 0))
    return pl.pallas_call(
        lambda *refs: project_body(len(row_blocks), share, *refs),
        grid_spec=pltpu.PrefetchScalarGridSpec(
            num_scalar_prefetch=1,
            grid=(4,),
            in_specs=[pl.BlockSpec((step, share), lambda place, starts: (place, 0))]
            * len(row_blocks)
            + [whole, angle, angle],
            out_specs=pl.BlockSpec((step, weights.shape[1]), lambda place, starts: (place, 0)),
        ),
        out_shape=jax.ShapeDtypeStruct((row_count, weights.shape[1]), jnp.bfloat16),
        compiler_params=pltpu.CompilerParams(vmem_limit_bytes=32 * 2**20),
        cost_estimate=SMALL,
        name="project",
    )(starts, *row_blocks, weights, cosine, sine_part)


def attend_body(sink_ref, query_prompt_ref, key_prompt_ref, query_ref, key_ref, value_ref, out_ref):
    sink = sink_ref[0]
    scores = lax.dot_general(
        query_ref[...],
        key_ref[...],
        (((1,), (1,)), ((), ())),
        preferred_element_type=jnp.float32,
    ) * HEAD ** (-0.5)
    scores = jnp.where(query_prompt_ref[...] == key_prompt_ref[...], scores, MASKED)
    top = jnp.maximum(sink, jnp.max(scores, axis=1, keepdims=True))
    weights = jnp.exp(scores - top)
    denominator = jnp.exp(sink - top) + jnp.sum(weights, axis=1, keepdims=True)
    high = weights.astype(jnp.bfloat16)
    low = (weights - high.astype(jnp.float32)).astype(jnp.bfloat16)
    values = value_ref[...]
    mix = jnp.dot(high, values, preferred_element_type=jnp.float32) + jnp.dot(
        low, values, preferred_element_type=jnp.float32
    )
    out_ref[...] = (mix / denominator).astype(jnp.bfloat16)


def attend_once(sink, query_prompt, key_prompt, rows):
    row_count = rows.shape[0]
    steps = 4 if row_count % 64 == 0 else 1
    step = row_count // steps
    return pl.pallas_call(
        attend_body,
        grid=(steps,),
        in_specs=[
            pl.BlockSpec(memory_space=pltpu.SMEM),
            pl.BlockSpec((step, 1), lambda place: (place, 0)),
            pl.BlockSpec((1, row_count), lambda place: (0, 0)),
            pl.BlockSpec((step, HEAD), lambda place: (place, 0)),
            pl.BlockSpec((row_count, HEAD), lambda place: (0, 1)),
            pl.BlockSpec((row_count, HEAD), lambda place: (0, 2)),
        ],
        out_specs=pl.BlockSpec((step, HEAD), lambda place: (place, 0)),
        out_shape=jax.ShapeDtypeStruct((row_count, HEAD), jnp.bfloat16),
        compiler_params=pltpu.CompilerParams(vmem_limit_bytes=32 * 2**20),
        cost_estimate=SMALL,
        name="attend_once",
    )(sink, query_prompt[:, None], key_prompt[None, :], rows, rows, rows)


def settle_body(piece_count, width, place_ref, *refs):
    pieces = refs[:piece_count]
    token_ref, gain_ref, router_ref, full_ref, outgoing_ref, logit_ref, router_all = refs[
        piece_count:
    ]
    for place in range(full_ref.shape[1] // width):
        here = slice(place * width, (place + 1) * width)
        there = pl.ds(pl.multiple_of(place_ref[place] * width, width), width)
        block = sum(piece[:, there] for piece in pieces)
        full_ref[:, here] = token_ref[:, here].astype(jnp.float32) + block
        router_all[:, here] = router_ref[:, there]
    outgoing = rms_scale(full_ref[...], gain_ref[...]).astype(jnp.bfloat16)
    outgoing_ref[...] = outgoing
    logit_ref[...] = lax.dot_general(
        outgoing,
        router_all[...],
        (((1,), (1,)), ((), ())),
        preferred_element_type=jnp.float32,
    )


def settle(places, pieces, tokens, gain, router, width):
    rows, columns = tokens.shape
    vmem = pl.BlockSpec(memory_space=pltpu.VMEM)
    return pl.pallas_call(
        lambda *refs: settle_body(len(pieces), width, *refs),
        in_specs=[pl.BlockSpec(memory_space=pltpu.SMEM)] + [vmem] * (len(pieces) + 3),
        out_specs=[vmem] * 3,
        out_shape=[
            jax.ShapeDtypeStruct((rows, columns), jnp.float32),
            jax.ShapeDtypeStruct((rows, columns), jnp.bfloat16),
            jax.ShapeDtypeStruct((rows, router.shape[0]), jnp.float32),
        ],
        scratch_shapes=[pltpu.VMEM(router.shape, jnp.bfloat16)],
        compiler_params=pltpu.CompilerParams(vmem_limit_bytes=32 * 2**20),
        cost_estimate=SMALL,
        name="settle",
    )(places, *pieces, tokens, gain[None, :], router)


def hidden_body(turn_count, share, start_ref, *refs):
    rows, (first_ref, second_ref, up_ref, out_ref) = (refs[:turn_count], refs[turn_count:])
    first = second = up = 0.0
    for turn in range(turn_count):
        here = pl.ds(pl.multiple_of(start_ref[turn], share), share)
        some = rows[turn][0]
        first = first + jnp.dot(some, first_ref[0, here, :], preferred_element_type=jnp.float32)
        second = second + jnp.dot(some, second_ref[0, here, :], preferred_element_type=jnp.float32)
        up = up + jnp.dot(some, up_ref[0, here, :], preferred_element_type=jnp.float32)
    gate = jnp.concatenate([first, second], axis=1)
    out_ref[0] = (gate / (1.0 + jnp.exp(-gate)) * up).astype(jnp.bfloat16)


def hidden_units(starts, row_blocks, weights):
    local_experts, row_count, share = row_blocks[0].shape
    width = weights[-1].shape[2]
    count = len(row_blocks)
    return pl.pallas_call(
        lambda *refs: hidden_body(count, share, *refs),
        grid_spec=pltpu.PrefetchScalarGridSpec(
            num_scalar_prefetch=1,
            grid=(local_experts,),
            in_specs=[pl.BlockSpec((1, row_count, share), lambda e, a: (e, 0, 0))] * count
            + [pl.BlockSpec((1, *w.shape[1:]), lambda e, a: (e, 0, 0)) for w in weights],
            out_specs=pl.BlockSpec((1, row_count, width), lambda e, a: (e, 0, 0)),
        ),
        out_shape=jax.ShapeDtypeStruct((local_experts, row_count, width), jnp.bfloat16),
        compiler_params=pltpu.CompilerParams(vmem_limit_bytes=52 * 2**20),
        cost_estimate=SMALL,
        name="hidden_units",
    )(starts, *row_blocks, *weights)


def down_body(turn_count, share, start_ref, hidden_ref, down_ref, *outs):
    for turn in range(turn_count):
        here = pl.ds(pl.multiple_of(start_ref[turn], share), share)
        outs[turn][0] = lax.dot_general(
            hidden_ref[0],
            down_ref[0, here, :],
            (((1,), (1,)), ((), ())),
            preferred_element_type=jnp.float32,
        ).astype(jnp.bfloat16)


def down_rows(starts, hidden, down):
    local_experts, row_count, width = hidden.shape
    columns, count = (down.shape[1], starts.shape[0])
    share = columns // count
    block = pl.BlockSpec((1, row_count, share), lambda e, a: (e, 0, 0))
    return pl.pallas_call(
        lambda *refs: down_body(count, share, *refs),
        grid_spec=pltpu.PrefetchScalarGridSpec(
            num_scalar_prefetch=1,
            grid=(local_experts,),
            in_specs=[
                pl.BlockSpec((1, row_count, width), lambda e, a: (e, 0, 0)),
                pl.BlockSpec((1, columns, width), lambda e, a: (e, 0, 0)),
            ],
            out_specs=[block] * count,
        ),
        out_shape=[jax.ShapeDtypeStruct((local_experts, row_count, share), jnp.bfloat16)] * count,
        compiler_params=pltpu.CompilerParams(vmem_limit_bytes=52 * 2**20),
        cost_estimate=SMALL,
        name="down_rows",
    )(starts, hidden, down)


def shards(
    tokens,
    attn_gain,
    mlp_gain,
    w_query,
    w_key,
    w_value,
    w_out,
    sink_logits,
    router,
    expert_gate,
    expert_up,
    expert_down,
    layout_map,
    real_lengths,
    routes,
):
    token_count, model_width = tokens.shape
    seq_count = lax.axis_size("seq")
    tp_count = lax.axis_size("tp")
    expert_count = router.shape[1]
    route_count = routes.shape[1]
    head_count = sink_logits.shape[0]
    col_share = model_width // tp_count
    total_slots = token_count * seq_count
    prompt_count = real_lengths.shape[0]
    slot_len = total_slots // prompt_count
    stagger = token_count // 2
    capacity = max(2, min(token_count, 9 * token_count * route_count // (8 * expert_count)))
    part_count = seq_count // head_count
    part_slots = head_count * token_count
    local_experts = expert_count // seq_count
    seq_place = lax.axis_index("seq")
    tp_place = lax.axis_index("tp")
    part = seq_place // head_count
    head = seq_place % head_count

    def tp_blocks(value):
        return [value] + [from_turned(value, "tp", turn) for turn in range(1, tp_count)]

    offsets = jnp.arange(token_count, dtype=jnp.int32)
    turns = jnp.arange(head_count, dtype=jnp.int32)
    aligned = part_count == prompt_count and part_slots + stagger <= HALF_WIN
    group_masks = masks_below(head_count)
    groups = [[first + k for k in range(head_count)] for first in range(0, seq_count, head_count)]
    part_masks = masks_below(seq_count, head_count)

    head_weights = lax.all_to_all(
        pack_heads(w_query, w_key, w_value, part_count),
        "seq",
        split_axis=0,
        concat_axis=0,
        tiled=True,
    ).reshape(model_width, 3 * HEAD)

    normed = rms_scale(tokens.astype(jnp.float32), attn_gain).astype(jnp.bfloat16)
    share = lax.dynamic_slice_in_dim(normed, tp_place * col_share, col_share, 1)
    all_routes, part_turns = doubled(routes[None], part_masks, 0)
    out_all, _ = doubled(
        jnp.concatenate([w_out, router.T], axis=0).astype(jnp.bfloat16), part_masks, 1
    )
    first_rows, first_turns = doubled(share[None], group_masks[:1], 0)
    first_rows, layout_map = lax.optimization_barrier((first_rows, layout_map))
    own_first, own_second, own_up, own_down = order_experts(
        layout_map, expert_gate, expert_up, expert_down
    )
    part_ids = (part * head_count + (head ^ turns))[:, None] * token_count + offsets[None, :]
    part_ids = part_ids.reshape(-1)
    part_positions = prompt_split(part_ids, slot_len, stagger, prompt_count)[1]
    half_dim = HEAD // 2
    frequency = ROPE_BASE ** (-jnp.arange(half_dim, dtype=jnp.float32) / half_dim)
    angles = part_positions.astype(jnp.float32)[:, None] * frequency[None, :]
    cosine = jnp.cos(angles)
    sine_part = jnp.sin(angles)
    pieces = []
    for piece, masks in (
        (first_rows[:, :, : col_share // 2], group_masks[1:]),
        (first_rows[:, :, col_share // 2 :], group_masks[1:][::-1]),
    ):
        known = first_turns
        for mask in masks:
            if mask == masks[-1]:
                piece, own_first, cosine, sine_part, all_routes = lax.optimization_barrier(
                    (piece, own_first, cosine, sine_part, all_routes)
                )
            piece = jnp.concatenate([piece, swapped(piece, "seq", mask)], axis=0)
            known = known + [turn ^ mask for turn in known]
        pieces.append(jnp.concatenate([piece[known.index(m)] for m in range(head_count)], axis=0))
    part_rows = jnp.concatenate(pieces, axis=1)

    def to_owner(blocks):
        taken = lax.all_to_all(blocks, "seq", split_axis=0, concat_axis=0, tiled=True)
        taken = taken.reshape(seq_count, local_experts, *blocks.shape[1:])
        return jnp.swapaxes(taken, 0, 1).reshape(local_experts, model_width, blocks.shape[2])

    out_all, _ = doubled(out_all, group_masks[:-2], 1)
    out_rows = out_all.shape[0] // 32 * 16
    out_halves = [
        (out_all[:out_rows], group_masks[-2:]),
        (out_all[out_rows:], group_masks[-2:][::-1]),
    ]
    halves, head_weights, part_rows, own_first = lax.optimization_barrier(
        ([half for half, _ in out_halves], head_weights, part_rows, own_first)
    )
    server_first = to_owner(own_first)
    out_halves = [
        (doubled(half, masks[:1], 1)[0], masks[1:]) for half, (_, masks) in zip(halves, out_halves)
    ]

    def by_place(blocks):
        return jnp.stack(
            [
                lax.dynamic_index_in_dim(blocks, head ^ place, 0, keepdims=False)
                for place in range(head_count)
            ]
        )

    expert_ids = jnp.arange(expert_count, dtype=jnp.int32)
    block_rows = local_experts * capacity
    columns = jnp.arange(head_count * block_rows, dtype=jnp.int32)
    column_owner = part * head_count + columns // block_rows
    column_expert = column_owner * local_experts + columns // capacity % local_experts
    spread = (column_expert[None, :] == expert_ids[:, None]).astype(jnp.bfloat16)
    wanted = (columns % capacity).astype(jnp.float32)
    earlier = (offsets[:, None] > offsets[None, :]).astype(jnp.bfloat16)

    def routing(turn, own_routes):
        ids = (seq_place ^ turn) * token_count + offsets
        prompt, position = prompt_split(ids, slot_len, stagger, prompt_count)
        valid_token = position < length_of(prompt, real_lengths)
        chosen = jnp.any(own_routes[:, :, None] == expert_ids[None, None, :], axis=1)
        live = chosen & valid_token[:, None]
        rank = jnp.dot(earlier, live.astype(jnp.bfloat16), preferred_element_type=jnp.float32)
        rank = jnp.where(live, rank, -1.0).astype(jnp.bfloat16)
        placed = jnp.dot(rank, spread, preferred_element_type=jnp.float32) == wanted[None, :]
        return (chosen, valid_token, placed)

    routings = [routing(turn, all_routes[k]) for k, turn in enumerate(part_turns)]
    chosen, valid_token, _ = routings[0]

    starts = (tp_place + jnp.arange(tp_count, dtype=jnp.int32)) % tp_count * col_share
    rows = project(starts, tp_blocks(part_rows), head_weights, cosine, sine_part)
    sink = lax.dynamic_slice_in_dim(sink_logits, head, 1, 0)

    def start_state(row_count):
        return (
            jnp.broadcast_to(sink[:, None], (row_count, 1)),
            jnp.ones((row_count, 1), jnp.float32),
            jnp.zeros((row_count, HEAD), jnp.float32),
        )

    if aligned:
        edge_start = (head ^ (head_count - 1)) * token_count + token_count - stagger
        edge = from_behind(
            lax.dynamic_slice_in_dim(rows, edge_start, stagger, 0), "seq", head_count
        )
        edge_ids = part * part_slots - stagger + jnp.arange(stagger, dtype=jnp.int32)
        row_ids = jnp.concatenate([part_ids, edge_ids])
        row_prompt, row_position = prompt_split(row_ids, slot_len, stagger, prompt_count)
        row_live = (row_ids >= 0) & (row_position < length_of(row_prompt, real_lengths))
        halves, edge = lax.optimization_barrier(([half for half, _ in out_halves], edge))
        out_halves = [(half, masks) for half, (_, masks) in zip(halves, out_halves)]
        mixed = attend_once(
            sink,
            row_prompt,
            jnp.where(row_live, row_prompt, -1),
            jnp.concatenate([rows, edge], axis=0),
        )
        edge_back = from_behind(mixed[part_slots:], "seq", -head_count)
        mixed = mixed[:part_slots]
        kept = lax.dynamic_slice_in_dim(mixed, edge_start, stagger, 0)
        mixed = lax.dynamic_update_slice_in_dim(
            mixed, jnp.where(part < part_count - 1, edge_back, kept), edge_start, 0
        )
    else:
        query_rows, key_rows, value_rows = (rows[:, k * HEAD : (k + 1) * HEAD] for k in range(3))
        softmax_state = attend(
            start_state(part_slots),
            query_rows,
            key_rows,
            value_rows,
            key_rules(part_ids, part_ids, slot_len, stagger, total_slots, real_lengths),
        )
        from_below = from_above = jnp.concatenate([key_rows, value_rows], axis=1)
        for turn in range(1, min(part_count - 1, -(-HALF_WIN // part_slots)) + 1):
            from_below = from_behind(from_below, "seq", head_count)
            from_above = from_behind(from_above, "seq", -head_count)
            reach = turn * part_slots
            key_ids = jnp.concatenate([part_ids - reach, part_ids + reach])
            pair = jnp.concatenate([from_below, from_above], axis=0)
            softmax_state = attend(
                softmax_state,
                query_rows,
                pair[:, :HEAD],
                pair[:, HEAD:],
                key_rules(part_ids, key_ids, slot_len, stagger, total_slots, real_lengths),
            )
        _, denominator, accumulated = softmax_state
        mixed = (accumulated / denominator).astype(jnp.bfloat16)
    blocks = by_place(mixed.reshape(head_count, token_count, HEAD))
    out_halves = [(half, swapped(half, "seq", masks[0])) for half, masks in out_halves]
    blocks, out_halves, server_first = lax.optimization_barrier((blocks, out_halves, server_first))
    attention_result = lax.all_to_all(
        blocks, "seq", split_axis=0, concat_axis=0, tiled=True, axis_index_groups=groups
    )
    attention_result, own_second = lax.optimization_barrier((attention_result, own_second))
    server_second = to_owner(own_second)

    proj_width = head_count * HEAD
    attention_result = jnp.swapaxes(attention_result, 0, 1).reshape(token_count, proj_width)

    def joined(pieces, half):
        if half == 0:
            return jnp.concatenate(pieces, axis=1)
        span = pieces[0].shape[1] // 2
        low, high = ([piece[:, k * span : (k + 1) * span] for piece in pieces] for k in range(2))
        return jnp.concatenate([*low, *high], axis=1)

    partial_out = sum(
        joined([jnp.dot(rows, piece, preferred_element_type=jnp.float32) for piece in pieces], half)
        for half, (rows, pieces) in enumerate(
            (
                (attention_result[:, :out_rows], out_halves[0]),
                (
                    attention_result[:, out_rows:],
                    [piece[: proj_width - out_rows] for piece in out_halves[1]],
                ),
            )
        )
    )
    if tp_count == 2:
        out_pieces = [partial_out, from_turned(partial_out, "tp", 1)]
    else:
        out_pieces = [lax.psum(partial_out, "tp")]
    router_rows = joined([piece[proj_width - out_rows :] for piece in out_halves[1]], 1)
    slots = jnp.arange(seq_count, dtype=jnp.int32)
    turn = seq_place ^ slots
    bits = len(part_masks) + len(group_masks)
    out_places = sum(((turn >> k) & 1) << (bits - 1 - k) for k in range(bits))
    width = w_out.shape[1]
    if width % 128:

        def in_order(value):
            blocks = [
                lax.dynamic_slice_in_dim(value, out_places[place] * width, width, 1)
                for place in range(seq_count)
            ]
            return jnp.concatenate(blocks, axis=1)

        out_pieces, router_rows = ([in_order(piece) for piece in out_pieces], in_order(router_rows))
        out_places, width = (jnp.zeros((1,), jnp.int32), model_width)
    full_rows, outgoing, logits = settle(
        out_places, out_pieces, tokens, mlp_gain, router_rows, width
    )
    residual = lax.dynamic_slice_in_dim(full_rows, tp_place * col_share, col_share, 1)
    outgoing_share = lax.dynamic_slice_in_dim(outgoing, tp_place * col_share, col_share, 1)


    route_logits = jnp.where(chosen, logits, -jnp.inf)
    route_exp = jnp.exp(route_logits - jnp.max(route_logits, axis=1, keepdims=True))
    route_weight = route_exp / jnp.sum(route_exp, axis=1, keepdims=True)
    route_weight = route_weight * valid_token[:, None]
    all_weights, _ = doubled(route_weight[None], part_masks, 0)
    all_rows, _ = doubled(outgoing_share[None], part_masks, 0)
    all_rows, all_weights, server_second, own_up = lax.optimization_barrier(
        (all_rows, all_weights, server_second, own_up)
    )
    server_up = to_owner(own_up)
    buffer = jnp.stack(
        [
            lax.dot_general(
                placed.astype(jnp.bfloat16),
                all_rows[k],
                (((0,), (0,)), ((), ())),
                preferred_element_type=jnp.float32,
            )
            .astype(jnp.bfloat16)
            .reshape(head_count, block_rows, col_share)
            for k, (_, _, placed) in enumerate(routings)
        ],
        axis=1,
    )
    def to_mate(m):
        block = lax.dynamic_index_in_dim(buffer, head ^ m, 0, keepdims=False)
        return swapped(block, "seq", m) if m else block

    received = [to_mate(m) for m in range(head_count)]
    received[1:4], server_up, own_down = lax.optimization_barrier(
        (received[1:4], server_up, own_down)
    )
    server_down = to_owner(own_down)
    received = by_place(jnp.stack(received))
    received = received.reshape(head_count, part_count, local_experts, capacity, col_share)
    turn_ids = jnp.arange(tp_count, dtype=jnp.int32)
    in_starts = (tp_place + turn_ids) % tp_count * col_share
    out_starts = (tp_place - turn_ids) % tp_count * col_share

    halves = [
        tp_blocks(jnp.moveaxis(rows, 2, 0).reshape(local_experts, -1, col_share))
        for rows in (received[:, 1:], received[:, :1])
    ]
    hidden = [hidden_units(in_starts, rows, (server_first, server_second, server_up)) for rows in halves]
    hidden, server_down = lax.optimization_barrier((hidden, server_down))

    def through_experts(rows, parts):
        outs = down_rows(out_starts, rows, server_down)
        outs = [outs[0]] + [from_turned(outs[k], "tp", k) for k in range(1, tp_count)]
        summed = sum(piece.astype(jnp.float32) for piece in outs).astype(jnp.bfloat16)
        summed = summed.reshape(local_experts, head_count, parts, capacity, col_share)
        return jnp.moveaxis(summed, 0, 2).reshape(head_count, parts, block_rows, col_share)

    others = through_experts(hidden[0], part_count - 1)
    own_rows = through_experts(hidden[1], 1)

    def weighted(k, rows):
        placed = routings[k][2]
        stacked = jnp.concatenate(
            [
                jnp.where(
                    placed, jnp.dot(piece, spread, preferred_element_type=jnp.float32), 0.0
                ).astype(jnp.bfloat16)
                for piece in parts_of(all_weights[k], 3)
            ],
            axis=0,
        )
        mixes = jnp.dot(stacked, rows, preferred_element_type=jnp.float32)
        return sum(mixes[k * token_count : (k + 1) * token_count] for k in range(3))

    def back(blocks):
        return lax.all_to_all(
            blocks, "seq", split_axis=0, concat_axis=0, tiled=True, axis_index_groups=groups
        )

    others = back(others)
    mixes = [
        weighted(k, others[:, k - 1].reshape(-1, col_share)) for k in range(1, len(part_turns))
    ]
    mixes, own_rows = lax.optimization_barrier((mixes, own_rows))
    expert_mix = sum(
        swapped(mix.astype(jnp.bfloat16), "seq", turn).astype(jnp.float32)
        for mix, turn in zip(mixes, part_turns[1:])
    )
    own_mix = weighted(0, back(own_rows)[:, 0].reshape(-1, col_share))
    return (residual + (expert_mix + own_mix)).astype(jnp.bfloat16)


def solution(mesh):
    placed = (
        P("seq", None),
        P(),
        P(),
        P("seq", "tp"),
        P("seq", "tp"),
        P("seq", "tp"),
        P("tp", "seq"),
        P("tp"),
        P("seq", None),
        P(None, "seq", "tp"),
        P(None, "seq", "tp"),
        P(None, "seq", "tp"),
        P(),
        P(),
        P("seq", None),
    )
    return jax.shard_map(
        shards, mesh=mesh, in_specs=placed, out_specs=P("seq", "tp"), check_vma=False
    )
```

```python
import jax
import jax.numpy as jnp
from jax import lax
from jax.experimental import pallas as pl
from jax.experimental.pallas import tpu as pltpu
from jax.sharding import PartitionSpec as P

HEAD = 128
HALF_WIN = 2048


EPSILON = 1e-05
ROPE_BASE = 50000.0
MASKED = -1e30
SMALL = pl.CostEstimate(flops=1, bytes_accessed=1, transcendentals=1)


def from_behind(value, axis, steps):
    count = lax.axis_size(axis)
    first, last = (max(0, -steps), min(count, count - steps))
    return lax.ppermute(value, axis, [(source, source + steps) for source in range(first, last)])


def from_turned(value, axis, turn):
    count = lax.axis_size(axis)
    return lax.ppermute(value, axis, [((place + turn) % count, place) for place in range(count)])


def swapped(value, axis, mask):
    count = lax.axis_size(axis)
    return lax.ppermute(value, axis, [(place, place ^ mask) for place in range(count)])


def doubled(value, masks, axis):
    turns = [0]
    for mask in masks:
        value = jnp.concatenate([value, swapped(value, "seq", mask)], axis=axis)
        turns = turns + [turn ^ mask for turn in turns]
    return (value, turns)


def masks_below(count, least=1):
    masks = []
    while count > least:
        count //= 2
        masks.append(count)
    return masks


def rms_scale(row_values, gain_vector):
    mean_square = jnp.mean(row_values * row_values, axis=-1, keepdims=True)
    return row_values * lax.rsqrt(mean_square + EPSILON) * gain_vector


def rotate(rows, cosine, sine_part):
    half_dim = rows.shape[-1] // 2
    first_half = rows[:, :half_dim]
    second_half = rows[:, half_dim:]
    return jnp.concatenate(
        [
            first_half * cosine - second_half * sine_part,
            second_half * cosine + first_half * sine_part,
        ],
        axis=-1,
    )


def length_of(prompt, real_lengths):
    one_hot = prompt[:, None] == jnp.arange(real_lengths.shape[0], dtype=jnp.int32)[None, :]
    return jnp.sum(jnp.where(one_hot, real_lengths[None, :], 0), axis=1)


def prompt_split(slot_ids, slot_len, stagger, prompt_count):
    prompt = jnp.minimum((slot_ids + stagger) // slot_len, prompt_count - 1)
    start = jnp.maximum(prompt * slot_len - stagger, 0)
    return (prompt, slot_ids - start)


def key_rules(query_ids, key_ids, slot_len, stagger, total_slots, real_lengths):
    prompt_count = real_lengths.shape[0]
    key_prompt, key_pos = prompt_split(key_ids, slot_len, stagger, prompt_count)
    query_prompt = prompt_split(query_ids, slot_len, stagger, prompt_count)[0]
    inside = (key_ids >= 0) & (key_ids < total_slots)
    key_live = inside & (key_pos < length_of(key_prompt, real_lengths))
    same_prompt = query_prompt[:, None] == key_prompt[None, :]
    nearby = jnp.abs(query_ids[:, None] - key_ids[None, :]) < HALF_WIN
    return same_prompt & nearby & key_live[None, :]


def parts_of(values, count):
    rest = values
    pieces = []
    for _ in range(count):
        piece = lax.reduce_precision(rest, 8, 7)
        rest = rest - piece
        pieces.append(piece.astype(jnp.bfloat16))
    return pieces


def attend(softmax_state, query_rows, key_rows, value_rows, allowed):
    running_max, denominator, accumulated = softmax_state
    scores = lax.dot_general(
        query_rows, key_rows, (((1,), (1,)), ((), ())), preferred_element_type=jnp.float32
    ) * HEAD ** (-0.5)
    scores = jnp.where(allowed, scores, MASKED)
    new_max = jnp.maximum(running_max, jnp.max(scores, axis=1, keepdims=True))
    rescale = jnp.exp(running_max - new_max)
    weight_tensors = jnp.exp(scores - new_max)
    denominator = denominator * rescale + jnp.sum(weight_tensors, axis=1, keepdims=True)
    high, low = parts_of(weight_tensors, 2)
    accumulated = (
        accumulated * rescale
        + jnp.dot(high, value_rows, preferred_element_type=jnp.float32)
        + jnp.dot(low, value_rows, preferred_element_type=jnp.float32)
    )
    return (new_max, denominator, accumulated)


def order_body(order_ref, gate_ref, up_ref, down_ref, *outs):
    half = gate_ref.shape[2] // 2
    outs[0][...] = gate_ref[:, :, :half].astype(jnp.bfloat16)
    outs[1][...] = gate_ref[:, :, half:].astype(jnp.bfloat16)
    outs[2][...] = up_ref[:, :, :half].astype(jnp.bfloat16)
    outs[3][...] = up_ref[:, :, half:].astype(jnp.bfloat16)
    outs[4][...] = down_ref[...].astype(jnp.bfloat16)


def order_experts(layout_map, gate, up, down):
    count, rows, width = gate.shape
    source = pl.BlockSpec((1, rows, width), lambda place, order: (order[place], 0, 0))
    widths = (width // 2, width // 2, width // 2, width // 2, width)
    return pl.pallas_call(
        order_body,
        grid_spec=pltpu.PrefetchScalarGridSpec(
            num_scalar_prefetch=1,
            grid=(count,),
            in_specs=[source, source, source],
            out_specs=[
                pl.BlockSpec((1, rows, some), lambda place, order: (place, 0, 0))
                for some in widths
            ],
        ),
        out_shape=[jax.ShapeDtypeStruct((count, rows, some), jnp.bfloat16) for some in widths],
        cost_estimate=SMALL,
        name="order_experts",
    )(layout_map, gate, up, down)


def pack_body(query_ref, key_ref, value_ref, out_ref):
    heads = query_ref.shape[1] // HEAD
    for place in range(out_ref.shape[0]):
        head = place % heads
        for k, source in enumerate((query_ref, key_ref, value_ref)):
            out_ref[place, :, k * HEAD : (k + 1) * HEAD] = source[
                :, head * HEAD : (head + 1) * HEAD
            ].astype(jnp.bfloat16)


def pack_heads(w_query, w_key, w_value, copies):
    rows, width = w_query.shape
    places = copies * (width // HEAD)
    step = rows // 4 if rows % 64 == 0 else rows
    source = pl.BlockSpec((step, width), lambda place: (place, 0))
    return pl.pallas_call(
        pack_body,
        grid=(rows // step,),
        in_specs=[source, source, source],
        out_specs=pl.BlockSpec((places, step, 3 * HEAD), lambda place: (0, place, 0)),
        out_shape=jax.ShapeDtypeStruct((places, rows, 3 * HEAD), jnp.bfloat16),
        compiler_params=pltpu.CompilerParams(vmem_limit_bytes=32 * 2**20),
        cost_estimate=SMALL,
        name="pack_heads",
    )(w_query, w_key, w_value)


def project_body(turn_count, share, start_ref, *refs):
    rows, (weight_ref, cosine_ref, sine_ref, out_ref) = (refs[:turn_count], refs[turn_count:])
    product = 0.0
    for turn in range(turn_count):
        first = pl.multiple_of(start_ref[turn], share)
        product = product + jnp.dot(
            rows[turn][...], weight_ref[pl.ds(first, share), :], preferred_element_type=jnp.float32
        )
    cosine, sine_part = (cosine_ref[...], sine_ref[...])
    out_ref[:, :HEAD] = rotate(product[:, :HEAD], cosine, sine_part).astype(jnp.bfloat16)
    out_ref[:, HEAD : 2 * HEAD] = rotate(
        product[:, HEAD : 2 * HEAD], cosine, sine_part
    ).astype(jnp.bfloat16)
    out_ref[:, 2 * HEAD :] = product[:, 2 * HEAD :].astype(jnp.bfloat16)


def project(starts, row_blocks, weights, cosine, sine_part):
    row_count, share = row_blocks[0].shape
    step = row_count // 4
    whole = pl.BlockSpec(weights.shape, lambda place, starts: (0, 0))
    angle = pl.BlockSpec((step, cosine.shape[1]), lambda place, starts: (place, 0))
    return pl.pallas_call(
        lambda *refs: project_body(len(row_blocks), share, *refs),
        grid_spec=pltpu.PrefetchScalarGridSpec(
            num_scalar_prefetch=1,
            grid=(4,),
            in_specs=[pl.BlockSpec((step, share), lambda place, starts: (place, 0))]
            * len(row_blocks)
            + [whole, angle, angle],
            out_specs=pl.BlockSpec((step, weights.shape[1]), lambda place, starts: (place, 0)),
        ),
        out_shape=jax.ShapeDtypeStruct((row_count, weights.shape[1]), jnp.bfloat16),
        compiler_params=pltpu.CompilerParams(vmem_limit_bytes=32 * 2**20),
        cost_estimate=SMALL,
        name="project",
    )(starts, *row_blocks, weights, cosine, sine_part)


def attend_body(sink_ref, query_prompt_ref, key_prompt_ref, query_ref, key_ref, value_ref, out_ref):
    sink = sink_ref[0]
    scores = lax.dot_general(
        query_ref[...],
        key_ref[...],
        (((1,), (1,)), ((), ())),
        preferred_element_type=jnp.float32,
    ) * HEAD ** (-0.5)
    scores = jnp.where(query_prompt_ref[...] == key_prompt_ref[...], scores, MASKED)
    top = jnp.maximum(sink, jnp.max(scores, axis=1, keepdims=True))
    weights = jnp.exp(scores - top)
    denominator = jnp.exp(sink - top) + jnp.sum(weights, axis=1, keepdims=True)
    high = weights.astype(jnp.bfloat16)
    low = (weights - high.astype(jnp.float32)).astype(jnp.bfloat16)
    values = value_ref[...]
    mix = jnp.dot(high, values, preferred_element_type=jnp.float32) + jnp.dot(
        low, values, preferred_element_type=jnp.float32
    )
    out_ref[...] = (mix / denominator).astype(jnp.bfloat16)


def attend_once(sink, query_prompt, key_prompt, rows):
    row_count = rows.shape[0]
    steps = 4 if row_count % 64 == 0 else 1
    step = row_count // steps
    return pl.pallas_call(
        attend_body,
        grid=(steps,),
        in_specs=[
            pl.BlockSpec(memory_space=pltpu.SMEM),
            pl.BlockSpec((step, 1), lambda place: (place, 0)),
            pl.BlockSpec((1, row_count), lambda place: (0, 0)),
            pl.BlockSpec((step, HEAD), lambda place: (place, 0)),
            pl.BlockSpec((row_count, HEAD), lambda place: (0, 1)),
            pl.BlockSpec((row_count, HEAD), lambda place: (0, 2)),
        ],
        out_specs=pl.BlockSpec((step, HEAD), lambda place: (place, 0)),
        out_shape=jax.ShapeDtypeStruct((row_count, HEAD), jnp.bfloat16),
        compiler_params=pltpu.CompilerParams(vmem_limit_bytes=32 * 2**20),
        cost_estimate=SMALL,
        name="attend_once",
    )(sink, query_prompt[:, None], key_prompt[None, :], rows, rows, rows)


def settle_body(piece_count, width, place_ref, *refs):
    pieces = refs[:piece_count]
    token_ref, gain_ref, router_ref, full_ref, outgoing_ref, logit_ref, router_all = refs[
        piece_count:
    ]
    for place in range(full_ref.shape[1] // width):
        here = slice(place * width, (place + 1) * width)
        there = pl.ds(pl.multiple_of(place_ref[place] * width, width), width)
        block = sum(piece[:, there] for piece in pieces)
        full_ref[:, here] = token_ref[:, here].astype(jnp.float32) + block
        router_all[:, here] = router_ref[:, there]
    outgoing = rms_scale(full_ref[...], gain_ref[...]).astype(jnp.bfloat16)
    outgoing_ref[...] = outgoing
    logit_ref[...] = lax.dot_general(
        outgoing,
        router_all[...],
        (((1,), (1,)), ((), ())),
        preferred_element_type=jnp.float32,
    )


def settle(places, pieces, tokens, gain, router, width):
    rows, columns = tokens.shape
    vmem = pl.BlockSpec(memory_space=pltpu.VMEM)
    return pl.pallas_call(
        lambda *refs: settle_body(len(pieces), width, *refs),
        in_specs=[pl.BlockSpec(memory_space=pltpu.SMEM)] + [vmem] * (len(pieces) + 3),
        out_specs=[vmem] * 3,
        out_shape=[
            jax.ShapeDtypeStruct((rows, columns), jnp.float32),
            jax.ShapeDtypeStruct((rows, columns), jnp.bfloat16),
            jax.ShapeDtypeStruct((rows, router.shape[0]), jnp.float32),
        ],
        scratch_shapes=[pltpu.VMEM(router.shape, jnp.bfloat16)],
        compiler_params=pltpu.CompilerParams(vmem_limit_bytes=32 * 2**20),
        cost_estimate=SMALL,
        name="settle",
    )(places, *pieces, tokens, gain[None, :], router)


def hidden_body(turn_count, share, start_ref, *refs):
    rows, weights, out_ref = (refs[:turn_count], refs[turn_count:-1], refs[-1])
    products = []
    for weight in weights:
        product = 0.0
        for turn in range(turn_count):
            here = pl.ds(pl.multiple_of(start_ref[turn], share), share)
            product = product + jnp.dot(
                rows[turn][0], weight[0, here, :], preferred_element_type=jnp.float32
            )
        products.append(product)
    count = len(products) // 2
    width = out_ref.shape[2] // count
    for k in range(count):
        gate, up = (products[k], products[count + k])
        out_ref[0, :, k * width : (k + 1) * width] = (
            gate / (1.0 + jnp.exp(-gate)) * up
        ).astype(jnp.bfloat16)


def hidden_units(starts, row_blocks, weights):
    local_experts, row_count, share = row_blocks[0].shape
    width = sum(w.shape[2] for w in weights) // 2
    count = len(row_blocks)
    return pl.pallas_call(
        lambda *refs: hidden_body(count, share, *refs),
        grid_spec=pltpu.PrefetchScalarGridSpec(
            num_scalar_prefetch=1,
            grid=(local_experts,),
            in_specs=[pl.BlockSpec((1, row_count, share), lambda e, a: (e, 0, 0))] * count
            + [pl.BlockSpec((1, *w.shape[1:]), lambda e, a: (e, 0, 0)) for w in weights],
            out_specs=pl.BlockSpec((1, row_count, width), lambda e, a: (e, 0, 0)),
        ),
        out_shape=jax.ShapeDtypeStruct((local_experts, row_count, width), jnp.bfloat16),
        compiler_params=pltpu.CompilerParams(vmem_limit_bytes=52 * 2**20),
        cost_estimate=SMALL,
        name="hidden_units",
    )(starts, *row_blocks, *weights)


def down_body(turn_count, share, start_ref, hidden_ref, down_ref, *outs):
    for turn in range(turn_count):
        here = pl.ds(pl.multiple_of(start_ref[turn], share), share)
        outs[turn][0] = lax.dot_general(
            hidden_ref[0],
            down_ref[0, here, :],
            (((1,), (1,)), ((), ())),
            preferred_element_type=jnp.float32,
        ).astype(jnp.bfloat16)


def down_rows(starts, hidden, down):
    local_experts, row_count, width = hidden.shape
    columns, count = (down.shape[1], starts.shape[0])
    share = columns // count
    block = pl.BlockSpec((1, row_count, share), lambda e, a: (e, 0, 0))
    return pl.pallas_call(
        lambda *refs: down_body(count, share, *refs),
        grid_spec=pltpu.PrefetchScalarGridSpec(
            num_scalar_prefetch=1,
            grid=(local_experts,),
            in_specs=[
                pl.BlockSpec((1, row_count, width), lambda e, a: (e, 0, 0)),
                pl.BlockSpec((1, columns, width), lambda e, a: (e, 0, 0)),
            ],
            out_specs=[block] * count,
        ),
        out_shape=[jax.ShapeDtypeStruct((local_experts, row_count, share), jnp.bfloat16)] * count,
        compiler_params=pltpu.CompilerParams(vmem_limit_bytes=52 * 2**20),
        cost_estimate=SMALL,
        name="down_rows",
    )(starts, hidden, down)


def shards(
    tokens,
    attn_gain,
    mlp_gain,
    w_query,
    w_key,
    w_value,
    w_out,
    sink_logits,
    router,
    expert_gate,
    expert_up,
    expert_down,
    layout_map,
    real_lengths,
    routes,
):
    token_count, model_width = tokens.shape
    seq_count = lax.axis_size("seq")
    tp_count = lax.axis_size("tp")
    expert_count = router.shape[1]
    route_count = routes.shape[1]
    head_count = sink_logits.shape[0]
    col_share = model_width // tp_count
    total_slots = token_count * seq_count
    prompt_count = real_lengths.shape[0]
    slot_len = total_slots // prompt_count
    stagger = token_count // 2
    capacity = max(2, min(token_count, 9 * token_count * route_count // (8 * expert_count)))
    part_count = seq_count // head_count
    part_slots = head_count * token_count
    local_experts = expert_count // seq_count
    seq_place = lax.axis_index("seq")
    tp_place = lax.axis_index("tp")
    part = seq_place // head_count
    head = seq_place % head_count

    def tp_blocks(value):
        return [value] + [from_turned(value, "tp", turn) for turn in range(1, tp_count)]

    offsets = jnp.arange(token_count, dtype=jnp.int32)
    turns = jnp.arange(head_count, dtype=jnp.int32)
    aligned = part_count == prompt_count and part_slots + stagger <= HALF_WIN
    group_masks = masks_below(head_count)
    groups = [[first + k for k in range(head_count)] for first in range(0, seq_count, head_count)]
    part_masks = masks_below(seq_count, head_count)

    head_weights = lax.all_to_all(
        pack_heads(w_query, w_key, w_value, part_count),
        "seq",
        split_axis=0,
        concat_axis=0,
        tiled=True,
    ).reshape(model_width, 3 * HEAD)

    normed = rms_scale(tokens.astype(jnp.float32), attn_gain).astype(jnp.bfloat16)
    share = lax.dynamic_slice_in_dim(normed, tp_place * col_share, col_share, 1)
    all_routes, part_turns = doubled(routes[None], part_masks, 0)
    out_all, _ = doubled(
        jnp.concatenate([w_out, router.T], axis=0).astype(jnp.bfloat16), part_masks, 1
    )
    first_rows, first_turns = doubled(share[None], group_masks[:1], 0)
    first_rows, layout_map = lax.optimization_barrier((first_rows, layout_map))
    own_first, own_second, own_third, own_fourth, own_down = order_experts(
        layout_map, expert_gate, expert_up, expert_down
    )
    part_ids = (part * head_count + (head ^ turns))[:, None] * token_count + offsets[None, :]
    part_ids = part_ids.reshape(-1)
    part_positions = prompt_split(part_ids, slot_len, stagger, prompt_count)[1]
    half_dim = HEAD // 2
    frequency = ROPE_BASE ** (-jnp.arange(half_dim, dtype=jnp.float32) / half_dim)
    angles = part_positions.astype(jnp.float32)[:, None] * frequency[None, :]
    cosine = jnp.cos(angles)
    sine_part = jnp.sin(angles)
    pieces = []
    for piece, masks in (
        (first_rows[:, :, : col_share // 2], group_masks[1:]),
        (first_rows[:, :, col_share // 2 :], group_masks[1:][::-1]),
    ):
        known = first_turns
        for mask in masks:
            if mask == masks[-1]:
                piece, own_first, cosine, sine_part, all_routes = lax.optimization_barrier(
                    (piece, own_first, cosine, sine_part, all_routes)
                )
            piece = jnp.concatenate([piece, swapped(piece, "seq", mask)], axis=0)
            known = known + [turn ^ mask for turn in known]
        pieces.append(jnp.concatenate([piece[known.index(m)] for m in range(head_count)], axis=0))
    part_rows = jnp.concatenate(pieces, axis=1)

    def to_owner(blocks):
        taken = lax.all_to_all(blocks, "seq", split_axis=0, concat_axis=0, tiled=True)
        taken = taken.reshape(seq_count, local_experts, *blocks.shape[1:])
        return jnp.swapaxes(taken, 0, 1).reshape(local_experts, model_width, blocks.shape[2])

    out_all, _ = doubled(out_all, group_masks[:-2], 1)
    out_rows = out_all.shape[0] // 32 * 16
    out_halves = [
        (out_all[:out_rows], group_masks[-2:]),
        (out_all[out_rows:], group_masks[-2:][::-1]),
    ]
    halves, head_weights, part_rows, own_first = lax.optimization_barrier(
        ([half for half, _ in out_halves], head_weights, part_rows, own_first)
    )
    server_first = to_owner(own_first)
    out_halves = [
        (doubled(half, masks[:1], 1)[0], masks[1:]) for half, (_, masks) in zip(halves, out_halves)
    ]

    def by_place(blocks):
        return jnp.stack(
            [
                lax.dynamic_index_in_dim(blocks, head ^ place, 0, keepdims=False)
                for place in range(head_count)
            ]
        )

    expert_ids = jnp.arange(expert_count, dtype=jnp.int32)
    block_rows = local_experts * capacity
    columns = jnp.arange(head_count * block_rows, dtype=jnp.int32)
    column_owner = part * head_count + columns // block_rows
    column_expert = column_owner * local_experts + columns // capacity % local_experts
    spread = (column_expert[None, :] == expert_ids[:, None]).astype(jnp.bfloat16)
    wanted = (columns % capacity).astype(jnp.float32)
    earlier = (offsets[:, None] > offsets[None, :]).astype(jnp.bfloat16)

    def routing(turn, own_routes):
        ids = (seq_place ^ turn) * token_count + offsets
        prompt, position = prompt_split(ids, slot_len, stagger, prompt_count)
        valid_token = position < length_of(prompt, real_lengths)
        chosen = jnp.any(own_routes[:, :, None] == expert_ids[None, None, :], axis=1)
        live = chosen & valid_token[:, None]
        rank = jnp.dot(earlier, live.astype(jnp.bfloat16), preferred_element_type=jnp.float32)
        rank = jnp.where(live, rank, -1.0).astype(jnp.bfloat16)
        placed = jnp.dot(rank, spread, preferred_element_type=jnp.float32) == wanted[None, :]
        return (chosen, valid_token, placed)

    routings = [routing(turn, all_routes[k]) for k, turn in enumerate(part_turns)]
    chosen, valid_token, _ = routings[0]

    starts = (tp_place + jnp.arange(tp_count, dtype=jnp.int32)) % tp_count * col_share
    rows = project(starts, tp_blocks(part_rows), head_weights, cosine, sine_part)
    sink = lax.dynamic_slice_in_dim(sink_logits, head, 1, 0)

    def start_state(row_count):
        return (
            jnp.broadcast_to(sink[:, None], (row_count, 1)),
            jnp.ones((row_count, 1), jnp.float32),
            jnp.zeros((row_count, HEAD), jnp.float32),
        )

    if aligned:
        edge_start = (head ^ (head_count - 1)) * token_count + token_count - stagger
        edge = from_behind(
            lax.dynamic_slice_in_dim(rows, edge_start, stagger, 0), "seq", head_count
        )
        edge_ids = part * part_slots - stagger + jnp.arange(stagger, dtype=jnp.int32)
        row_ids = jnp.concatenate([part_ids, edge_ids])
        row_prompt, row_position = prompt_split(row_ids, slot_len, stagger, prompt_count)
        row_live = (row_ids >= 0) & (row_position < length_of(row_prompt, real_lengths))
        halves, edge = lax.optimization_barrier(([half for half, _ in out_halves], edge))
        out_halves = [(half, masks) for half, (_, masks) in zip(halves, out_halves)]
        mixed = attend_once(
            sink,
            row_prompt,
            jnp.where(row_live, row_prompt, -1),
            jnp.concatenate([rows, edge], axis=0),
        )
        edge_back = from_behind(mixed[part_slots:], "seq", -head_count)
        mixed = mixed[:part_slots]
        kept = lax.dynamic_slice_in_dim(mixed, edge_start, stagger, 0)
        mixed = lax.dynamic_update_slice_in_dim(
            mixed, jnp.where(part < part_count - 1, edge_back, kept), edge_start, 0
        )
    else:
        query_rows, key_rows, value_rows = (rows[:, k * HEAD : (k + 1) * HEAD] for k in range(3))
        softmax_state = attend(
            start_state(part_slots),
            query_rows,
            key_rows,
            value_rows,
            key_rules(part_ids, part_ids, slot_len, stagger, total_slots, real_lengths),
        )
        from_below = from_above = jnp.concatenate([key_rows, value_rows], axis=1)
        for turn in range(1, min(part_count - 1, -(-HALF_WIN // part_slots)) + 1):
            from_below = from_behind(from_below, "seq", head_count)
            from_above = from_behind(from_above, "seq", -head_count)
            reach = turn * part_slots
            key_ids = jnp.concatenate([part_ids - reach, part_ids + reach])
            pair = jnp.concatenate([from_below, from_above], axis=0)
            softmax_state = attend(
                softmax_state,
                query_rows,
                pair[:, :HEAD],
                pair[:, HEAD:],
                key_rules(part_ids, key_ids, slot_len, stagger, total_slots, real_lengths),
            )
        _, denominator, accumulated = softmax_state
        mixed = (accumulated / denominator).astype(jnp.bfloat16)
    mixed, own_second, server_first = lax.optimization_barrier((mixed, own_second, server_first))
    server_second = to_owner(own_second)
    blocks = by_place(mixed.reshape(head_count, token_count, HEAD))
    out_halves = [(half, swapped(half, "seq", masks[0])) for half, masks in out_halves]
    blocks, out_halves, server_second = lax.optimization_barrier(
        (blocks, out_halves, server_second)
    )
    attention_result = lax.all_to_all(
        blocks, "seq", split_axis=0, concat_axis=0, tiled=True, axis_index_groups=groups
    )
    attention_result, own_third = lax.optimization_barrier((attention_result, own_third))
    server_third = to_owner(own_third)

    proj_width = head_count * HEAD
    attention_result = jnp.swapaxes(attention_result, 0, 1).reshape(token_count, proj_width)

    def joined(pieces, half):
        if half == 0:
            return jnp.concatenate(pieces, axis=1)
        span = pieces[0].shape[1] // 2
        low, high = ([piece[:, k * span : (k + 1) * span] for piece in pieces] for k in range(2))
        return jnp.concatenate([*low, *high], axis=1)

    partial_out = sum(
        joined([jnp.dot(rows, piece, preferred_element_type=jnp.float32) for piece in pieces], half)
        for half, (rows, pieces) in enumerate(
            (
                (attention_result[:, :out_rows], out_halves[0]),
                (
                    attention_result[:, out_rows:],
                    [piece[: proj_width - out_rows] for piece in out_halves[1]],
                ),
            )
        )
    )
    if tp_count == 2:
        out_pieces = [partial_out, from_turned(partial_out, "tp", 1)]
    else:
        out_pieces = [lax.psum(partial_out, "tp")]
    router_rows = joined([piece[proj_width - out_rows :] for piece in out_halves[1]], 1)
    slots = jnp.arange(seq_count, dtype=jnp.int32)
    turn = seq_place ^ slots
    bits = len(part_masks) + len(group_masks)
    out_places = sum(((turn >> k) & 1) << (bits - 1 - k) for k in range(bits))
    width = w_out.shape[1]
    if width % 128:

        def in_order(value):
            blocks = [
                lax.dynamic_slice_in_dim(value, out_places[place] * width, width, 1)
                for place in range(seq_count)
            ]
            return jnp.concatenate(blocks, axis=1)

        out_pieces, router_rows = ([in_order(piece) for piece in out_pieces], in_order(router_rows))
        out_places, width = (jnp.zeros((1,), jnp.int32), model_width)
    full_rows, outgoing, logits = settle(
        out_places, out_pieces, tokens, mlp_gain, router_rows, width
    )
    residual = lax.dynamic_slice_in_dim(full_rows, tp_place * col_share, col_share, 1)
    outgoing_share = lax.dynamic_slice_in_dim(outgoing, tp_place * col_share, col_share, 1)


    route_logits = jnp.where(chosen, logits, -jnp.inf)
    route_exp = jnp.exp(route_logits - jnp.max(route_logits, axis=1, keepdims=True))
    route_weight = route_exp / jnp.sum(route_exp, axis=1, keepdims=True)
    route_weight = route_weight * valid_token[:, None]
    all_weights, _ = doubled(route_weight[None], part_masks, 0)
    all_rows, _ = doubled(outgoing_share[None], part_masks, 0)
    all_rows, all_weights, server_third, own_fourth = lax.optimization_barrier(
        (all_rows, all_weights, server_third, own_fourth)
    )
    server_fourth = to_owner(own_fourth)
    buffer = jnp.stack(
        [
            lax.dot_general(
                placed.astype(jnp.bfloat16),
                all_rows[k],
                (((0,), (0,)), ((), ())),
                preferred_element_type=jnp.float32,
            )
            .astype(jnp.bfloat16)
            .reshape(head_count, block_rows, col_share)
            for k, (_, _, placed) in enumerate(routings)
        ],
        axis=1,
    )
    def to_mate(m):
        block = lax.dynamic_index_in_dim(buffer, head ^ m, 0, keepdims=False)
        return swapped(block, "seq", m) if m else block

    received = [to_mate(m) for m in range(head_count)]
    received[1:3], server_fourth, own_down = lax.optimization_barrier(
        (received[1:3], server_fourth, own_down)
    )
    server_down = to_owner(own_down)
    received = by_place(jnp.stack(received))
    received = received.reshape(head_count, part_count, local_experts, capacity, col_share)
    turn_ids = jnp.arange(tp_count, dtype=jnp.int32)
    in_starts = (tp_place + turn_ids) % tp_count * col_share
    out_starts = (tp_place - turn_ids) % tp_count * col_share

    halves = [
        tp_blocks(jnp.moveaxis(rows, 2, 0).reshape(local_experts, -1, col_share))
        for rows in (received[:, 1:], received[:, :1])
    ]
    server = (server_first, server_second, server_third, server_fourth)
    hidden = [hidden_units(in_starts, rows, server) for rows in halves]
    hidden[0], halves[1], server_down = lax.optimization_barrier(
        (hidden[0], halves[1], server_down)
    )

    def through_experts(rows, parts):
        outs = down_rows(out_starts, rows, server_down)
        outs = [outs[0]] + [from_turned(outs[k], "tp", k) for k in range(1, tp_count)]
        summed = sum(piece.astype(jnp.float32) for piece in outs).astype(jnp.bfloat16)
        summed = summed.reshape(local_experts, head_count, parts, capacity, col_share)
        return jnp.moveaxis(summed, 0, 2).reshape(head_count, parts, block_rows, col_share)

    others = through_experts(hidden[0], part_count - 1)
    own_rows = through_experts(hidden[1], 1)

    def weighted(k, rows):
        placed = routings[k][2]
        stacked = jnp.concatenate(
            [
                jnp.where(
                    placed, jnp.dot(piece, spread, preferred_element_type=jnp.float32), 0.0
                ).astype(jnp.bfloat16)
                for piece in parts_of(all_weights[k], 3)
            ],
            axis=0,
        )
        mixes = jnp.dot(stacked, rows, preferred_element_type=jnp.float32)
        return sum(mixes[k * token_count : (k + 1) * token_count] for k in range(3))

    def back(blocks):
        return lax.all_to_all(
            blocks, "seq", split_axis=0, concat_axis=0, tiled=True, axis_index_groups=groups
        )

    others = back(others)
    mixes = [
        weighted(k, others[:, k - 1].reshape(-1, col_share)) for k in range(1, len(part_turns))
    ]
    mixes, own_rows = lax.optimization_barrier((mixes, own_rows))
    expert_mix = sum(
        swapped(mix.astype(jnp.bfloat16), "seq", turn).astype(jnp.float32)
        for mix, turn in zip(mixes, part_turns[1:])
    )
    own_mix = weighted(0, back(own_rows)[:, 0].reshape(-1, col_share))
    return (residual + (expert_mix + own_mix)).astype(jnp.bfloat16)


def solution(mesh):
    placed = (
        P("seq", None),
        P(),
        P(),
        P("seq", "tp"),
        P("seq", "tp"),
        P("seq", "tp"),
        P("tp", "seq"),
        P("tp"),
        P("seq", None),
        P(None, "seq", "tp"),
        P(None, "seq", "tp"),
        P(None, "seq", "tp"),
        P(),
        P(),
        P("seq", None),
    )
    return jax.shard_map(
        shards, mesh=mesh, in_specs=placed, out_specs=P("seq", "tp"), check_vma=False
    )
```

```python
import jax
import jax.numpy as jnp
from jax import lax
from jax.experimental import pallas as pl
from jax.experimental.pallas import tpu as pltpu
from jax.sharding import PartitionSpec as P

HEAD = 128
HALF_WIN = 2048


EPSILON = 1e-05
ROPE_BASE = 50000.0
MASKED = -1e30
SMALL = pl.CostEstimate(flops=1, bytes_accessed=1, transcendentals=1)


def from_behind(value, axis, steps):
    count = lax.axis_size(axis)
    first, last = (max(0, -steps), min(count, count - steps))
    return lax.ppermute(value, axis, [(source, source + steps) for source in range(first, last)])


def from_turned(value, axis, turn):
    count = lax.axis_size(axis)
    return lax.ppermute(value, axis, [((place + turn) % count, place) for place in range(count)])


def swapped(value, axis, mask):
    count = lax.axis_size(axis)
    return lax.ppermute(value, axis, [(place, place ^ mask) for place in range(count)])


def doubled(value, masks, axis):
    turns = [0]
    for mask in masks:
        value = jnp.concatenate([value, swapped(value, "seq", mask)], axis=axis)
        turns = turns + [turn ^ mask for turn in turns]
    return (value, turns)


def masks_below(count, least=1):
    masks = []
    while count > least:
        count //= 2
        masks.append(count)
    return masks


def rms_scale(row_values, gain_vector):
    mean_square = jnp.mean(row_values * row_values, axis=-1, keepdims=True)
    return row_values * lax.rsqrt(mean_square + EPSILON) * gain_vector


def rotate(rows, cosine, sine_part):
    half_dim = rows.shape[-1] // 2
    first_half = rows[:, :half_dim]
    second_half = rows[:, half_dim:]
    return jnp.concatenate(
        [
            first_half * cosine - second_half * sine_part,
            second_half * cosine + first_half * sine_part,
        ],
        axis=-1,
    )


def length_of(prompt, real_lengths):
    one_hot = prompt[:, None] == jnp.arange(real_lengths.shape[0], dtype=jnp.int32)[None, :]
    return jnp.sum(jnp.where(one_hot, real_lengths[None, :], 0), axis=1)


def prompt_split(slot_ids, slot_len, stagger, prompt_count):
    prompt = jnp.minimum((slot_ids + stagger) // slot_len, prompt_count - 1)
    start = jnp.maximum(prompt * slot_len - stagger, 0)
    return (prompt, slot_ids - start)


def key_rules(query_ids, key_ids, slot_len, stagger, total_slots, real_lengths):
    prompt_count = real_lengths.shape[0]
    key_prompt, key_pos = prompt_split(key_ids, slot_len, stagger, prompt_count)
    query_prompt = prompt_split(query_ids, slot_len, stagger, prompt_count)[0]
    inside = (key_ids >= 0) & (key_ids < total_slots)
    key_live = inside & (key_pos < length_of(key_prompt, real_lengths))
    same_prompt = query_prompt[:, None] == key_prompt[None, :]
    nearby = jnp.abs(query_ids[:, None] - key_ids[None, :]) < HALF_WIN
    return same_prompt & nearby & key_live[None, :]


def parts_of(values, count):
    rest = values
    pieces = []
    for _ in range(count):
        piece = lax.reduce_precision(rest, 8, 7)
        rest = rest - piece
        pieces.append(piece.astype(jnp.bfloat16))
    return pieces


def attend(softmax_state, query_rows, key_rows, value_rows, allowed):
    running_max, denominator, accumulated = softmax_state
    scores = lax.dot_general(
        query_rows, key_rows, (((1,), (1,)), ((), ())), preferred_element_type=jnp.float32
    ) * HEAD ** (-0.5)
    scores = jnp.where(allowed, scores, MASKED)
    new_max = jnp.maximum(running_max, jnp.max(scores, axis=1, keepdims=True))
    rescale = jnp.exp(running_max - new_max)
    weight_tensors = jnp.exp(scores - new_max)
    denominator = denominator * rescale + jnp.sum(weight_tensors, axis=1, keepdims=True)
    high, low = parts_of(weight_tensors, 2)
    accumulated = (
        accumulated * rescale
        + jnp.dot(high, value_rows, preferred_element_type=jnp.float32)
        + jnp.dot(low, value_rows, preferred_element_type=jnp.float32)
    )
    return (new_max, denominator, accumulated)


def order_body(order_ref, gate_ref, up_ref, down_ref, *outs):
    half = gate_ref.shape[2] // 2
    outs[0][...] = gate_ref[:, :, :half].astype(jnp.bfloat16)
    outs[1][...] = gate_ref[:, :, half:].astype(jnp.bfloat16)
    outs[2][...] = up_ref[...].astype(jnp.bfloat16)
    outs[3][...] = down_ref[...].astype(jnp.bfloat16)


def order_experts(layout_map, gate, up, down):
    count, rows, width = gate.shape
    source = pl.BlockSpec((1, rows, width), lambda place, order: (order[place], 0, 0))
    widths = (width // 2, width - width // 2, width, width)
    return pl.pallas_call(
        order_body,
        grid_spec=pltpu.PrefetchScalarGridSpec(
            num_scalar_prefetch=1,
            grid=(count,),
            in_specs=[source, source, source],
            out_specs=[
                pl.BlockSpec((1, rows, some), lambda place, order: (place, 0, 0))
                for some in widths
            ],
        ),
        out_shape=[jax.ShapeDtypeStruct((count, rows, some), jnp.bfloat16) for some in widths],
        cost_estimate=SMALL,
        name="order_experts",
    )(layout_map, gate, up, down)


def pack_body(query_ref, key_ref, value_ref, out_ref):
    heads = query_ref.shape[1] // HEAD
    for place in range(out_ref.shape[0]):
        head = place % heads
        for k, source in enumerate((query_ref, key_ref, value_ref)):
            out_ref[place, :, k * HEAD : (k + 1) * HEAD] = source[
                :, head * HEAD : (head + 1) * HEAD
            ].astype(jnp.bfloat16)


def pack_heads(w_query, w_key, w_value, copies):
    rows, width = w_query.shape
    places = copies * (width // HEAD)
    step = rows // 4 if rows % 64 == 0 else rows
    source = pl.BlockSpec((step, width), lambda place: (place, 0))
    return pl.pallas_call(
        pack_body,
        grid=(rows // step,),
        in_specs=[source, source, source],
        out_specs=pl.BlockSpec((places, step, 3 * HEAD), lambda place: (0, place, 0)),
        out_shape=jax.ShapeDtypeStruct((places, rows, 3 * HEAD), jnp.bfloat16),
        compiler_params=pltpu.CompilerParams(vmem_limit_bytes=32 * 2**20),
        cost_estimate=SMALL,
        name="pack_heads",
    )(w_query, w_key, w_value)


def project_body(turn_count, share, start_ref, *refs):
    rows, (weight_ref, cosine_ref, sine_ref, out_ref) = (refs[:turn_count], refs[turn_count:])
    product = 0.0
    for turn in range(turn_count):
        first = pl.multiple_of(start_ref[turn], share)
        product = product + jnp.dot(
            rows[turn][...], weight_ref[pl.ds(first, share), :], preferred_element_type=jnp.float32
        )
    cosine, sine_part = (cosine_ref[...], sine_ref[...])
    out_ref[:, :HEAD] = rotate(product[:, :HEAD], cosine, sine_part).astype(jnp.bfloat16)
    out_ref[:, HEAD : 2 * HEAD] = rotate(
        product[:, HEAD : 2 * HEAD], cosine, sine_part
    ).astype(jnp.bfloat16)
    out_ref[:, 2 * HEAD :] = product[:, 2 * HEAD :].astype(jnp.bfloat16)


def project(starts, row_blocks, weights, cosine, sine_part):
    row_count, share = row_blocks[0].shape
    step = row_count // 4
    whole = pl.BlockSpec(weights.shape, lambda place, starts: (0, 0))
    angle = pl.BlockSpec((step, cosine.shape[1]), lambda place, starts: (place, 0))
    return pl.pallas_call(
        lambda *refs: project_body(len(row_blocks), share, *refs),
        grid_spec=pltpu.PrefetchScalarGridSpec(
            num_scalar_prefetch=1,
            grid=(4,),
            in_specs=[pl.BlockSpec((step, share), lambda place, starts: (place, 0))]
            * len(row_blocks)
            + [whole, angle, angle],
            out_specs=pl.BlockSpec((step, weights.shape[1]), lambda place, starts: (place, 0)),
        ),
        out_shape=jax.ShapeDtypeStruct((row_count, weights.shape[1]), jnp.bfloat16),
        compiler_params=pltpu.CompilerParams(vmem_limit_bytes=32 * 2**20),
        cost_estimate=SMALL,
        name="project",
    )(starts, *row_blocks, weights, cosine, sine_part)


def attend_body(sink_ref, query_prompt_ref, key_prompt_ref, query_ref, key_ref, value_ref, out_ref):
    sink = sink_ref[0]
    scores = lax.dot_general(
        query_ref[...],
        key_ref[...],
        (((1,), (1,)), ((), ())),
        preferred_element_type=jnp.float32,
    ) * HEAD ** (-0.5)
    scores = jnp.where(query_prompt_ref[...] == key_prompt_ref[...], scores, MASKED)
    top = jnp.maximum(sink, jnp.max(scores, axis=1, keepdims=True))
    weights = jnp.exp(scores - top)
    denominator = jnp.exp(sink - top) + jnp.sum(weights, axis=1, keepdims=True)
    high = weights.astype(jnp.bfloat16)
    low = (weights - high.astype(jnp.float32)).astype(jnp.bfloat16)
    values = value_ref[...]
    mix = jnp.dot(high, values, preferred_element_type=jnp.float32) + jnp.dot(
        low, values, preferred_element_type=jnp.float32
    )
    out_ref[...] = (mix / denominator).astype(jnp.bfloat16)


def attend_once(sink, query_prompt, key_prompt, rows):
    row_count = rows.shape[0]
    steps = 4 if row_count % 64 == 0 else 1
    step = row_count // steps
    return pl.pallas_call(
        attend_body,
        grid=(steps,),
        in_specs=[
            pl.BlockSpec(memory_space=pltpu.SMEM),
            pl.BlockSpec((step, 1), lambda place: (place, 0)),
            pl.BlockSpec((1, row_count), lambda place: (0, 0)),
            pl.BlockSpec((step, HEAD), lambda place: (place, 0)),
            pl.BlockSpec((row_count, HEAD), lambda place: (0, 1)),
            pl.BlockSpec((row_count, HEAD), lambda place: (0, 2)),
        ],
        out_specs=pl.BlockSpec((step, HEAD), lambda place: (place, 0)),
        out_shape=jax.ShapeDtypeStruct((row_count, HEAD), jnp.bfloat16),
        compiler_params=pltpu.CompilerParams(vmem_limit_bytes=32 * 2**20),
        cost_estimate=SMALL,
        name="attend_once",
    )(sink, query_prompt[:, None], key_prompt[None, :], rows, rows, rows)


def out_body(head_ref, first_ref, first_other_ref, second_ref, second_other_ref, out_ref):
    heads = first_ref.shape[0] // HEAD
    first, second = (
        jnp.concatenate([head_ref[h] for h in place], axis=1)
        for place in (range(heads), range(heads, head_ref.shape[0]))
    )
    rows = second.shape[1]
    half = first_ref.shape[1]
    span = half // 2
    for k, (one, two) in enumerate(
        ((first_ref, second_ref), (first_other_ref, second_other_ref))
    ):
        own = jnp.dot(first, one[...], preferred_element_type=jnp.float32)
        other = jnp.dot(second, two[:rows, :], preferred_element_type=jnp.float32)
        if k == 0:
            low, high = (other[:, :span], other[:, span:])
            out_ref[:, :span] = own[:, :span] + low
            out_ref[:, span:half] = own[:, span:]
            out_ref[:, half : half + span] = high
        else:
            out_ref[:, span:half] = out_ref[:, span:half] + other[:, :span]
            out_ref[:, half : half + span] = out_ref[:, half : half + span] + own[:, :span]
            out_ref[:, half + span :] = own[:, span:] + other[:, span:]


def out_project(heads, pieces):
    vmem = pl.BlockSpec(memory_space=pltpu.VMEM)
    return pl.pallas_call(
        out_body,
        in_specs=[vmem] * 5,
        out_specs=vmem,
        out_shape=jax.ShapeDtypeStruct((heads.shape[1], 2 * pieces[0].shape[1]), jnp.float32),
        compiler_params=pltpu.CompilerParams(vmem_limit_bytes=40 * 2**20),
        cost_estimate=SMALL,
        name="out_project",
    )(heads, *pieces)


def settle_body(piece_count, width, place_ref, *refs):
    pieces = refs[:piece_count]
    token_ref, gain_ref, router_ref, full_ref, outgoing_ref, logit_ref, router_all = refs[
        piece_count:
    ]
    for place in range(full_ref.shape[1] // width):
        here = slice(place * width, (place + 1) * width)
        there = pl.ds(pl.multiple_of(place_ref[place] * width, width), width)
        block = sum(piece[:, there] for piece in pieces)
        full_ref[:, here] = token_ref[:, here].astype(jnp.float32) + block
        router_all[:, here] = router_ref[:, there]
    outgoing = rms_scale(full_ref[...], gain_ref[...]).astype(jnp.bfloat16)
    outgoing_ref[...] = outgoing
    logit_ref[...] = lax.dot_general(
        outgoing,
        router_all[...],
        (((1,), (1,)), ((), ())),
        preferred_element_type=jnp.float32,
    )


def settle(places, pieces, tokens, gain, router, width):
    rows, columns = tokens.shape
    vmem = pl.BlockSpec(memory_space=pltpu.VMEM)
    return pl.pallas_call(
        lambda *refs: settle_body(len(pieces), width, *refs),
        in_specs=[pl.BlockSpec(memory_space=pltpu.SMEM)] + [vmem] * (len(pieces) + 3),
        out_specs=[vmem] * 3,
        out_shape=[
            jax.ShapeDtypeStruct((rows, columns), jnp.float32),
            jax.ShapeDtypeStruct((rows, columns), jnp.bfloat16),
            jax.ShapeDtypeStruct((rows, router.shape[0]), jnp.float32),
        ],
        scratch_shapes=[pltpu.VMEM(router.shape, jnp.bfloat16)],
        compiler_params=pltpu.CompilerParams(vmem_limit_bytes=32 * 2**20),
        cost_estimate=SMALL,
        name="settle",
    )(places, *pieces, tokens, gain[None, :], router)


def hidden_body(turn_count, share, start_ref, *refs):
    rows, (first_ref, second_ref, up_ref, out_ref) = (refs[:turn_count], refs[turn_count:])
    first = second = up = 0.0
    for turn in range(turn_count):
        here = pl.ds(pl.multiple_of(start_ref[turn], share), share)
        some = rows[turn][0]
        first = first + jnp.dot(some, first_ref[0, here, :], preferred_element_type=jnp.float32)
        second = second + jnp.dot(some, second_ref[0, here, :], preferred_element_type=jnp.float32)
        up = up + jnp.dot(some, up_ref[0, here, :], preferred_element_type=jnp.float32)
    gate = jnp.concatenate([first, second], axis=1)
    out_ref[0] = (gate / (1.0 + jnp.exp(-gate)) * up).astype(jnp.bfloat16)


def hidden_units(starts, row_blocks, weights):
    local_experts, row_count, share = row_blocks[0].shape
    width = weights[-1].shape[2]
    count = len(row_blocks)
    return pl.pallas_call(
        lambda *refs: hidden_body(count, share, *refs),
        grid_spec=pltpu.PrefetchScalarGridSpec(
            num_scalar_prefetch=1,
            grid=(local_experts,),
            in_specs=[pl.BlockSpec((1, row_count, share), lambda e, a: (e, 0, 0))] * count
            + [pl.BlockSpec((1, *w.shape[1:]), lambda e, a: (e, 0, 0)) for w in weights],
            out_specs=pl.BlockSpec((1, row_count, width), lambda e, a: (e, 0, 0)),
        ),
        out_shape=jax.ShapeDtypeStruct((local_experts, row_count, width), jnp.bfloat16),
        compiler_params=pltpu.CompilerParams(vmem_limit_bytes=52 * 2**20),
        cost_estimate=SMALL,
        name="hidden_units",
    )(starts, *row_blocks, *weights)


def down_body(turn_count, share, start_ref, hidden_ref, down_ref, *outs):
    for turn in range(turn_count):
        here = pl.ds(pl.multiple_of(start_ref[turn], share), share)
        outs[turn][0] = lax.dot_general(
            hidden_ref[0],
            down_ref[0, here, :],
            (((1,), (1,)), ((), ())),
            preferred_element_type=jnp.float32,
        ).astype(jnp.bfloat16)


def down_rows(starts, hidden, down):
    local_experts, row_count, width = hidden.shape
    columns, count = (down.shape[1], starts.shape[0])
    share = columns // count
    block = pl.BlockSpec((1, row_count, share), lambda e, a: (e, 0, 0))
    return pl.pallas_call(
        lambda *refs: down_body(count, share, *refs),
        grid_spec=pltpu.PrefetchScalarGridSpec(
            num_scalar_prefetch=1,
            grid=(local_experts,),
            in_specs=[
                pl.BlockSpec((1, row_count, width), lambda e, a: (e, 0, 0)),
                pl.BlockSpec((1, columns, width), lambda e, a: (e, 0, 0)),
            ],
            out_specs=[block] * count,
        ),
        out_shape=[jax.ShapeDtypeStruct((local_experts, row_count, share), jnp.bfloat16)] * count,
        compiler_params=pltpu.CompilerParams(vmem_limit_bytes=52 * 2**20),
        cost_estimate=SMALL,
        name="down_rows",
    )(starts, hidden, down)


def shards(
    tokens,
    attn_gain,
    mlp_gain,
    w_query,
    w_key,
    w_value,
    w_out,
    sink_logits,
    router,
    expert_gate,
    expert_up,
    expert_down,
    layout_map,
    real_lengths,
    routes,
):
    token_count, model_width = tokens.shape
    seq_count = lax.axis_size("seq")
    tp_count = lax.axis_size("tp")
    expert_count = router.shape[1]
    route_count = routes.shape[1]
    head_count = sink_logits.shape[0]
    col_share = model_width // tp_count
    total_slots = token_count * seq_count
    prompt_count = real_lengths.shape[0]
    slot_len = total_slots // prompt_count
    stagger = token_count // 2
    capacity = max(2, min(token_count, 9 * token_count * route_count // (8 * expert_count)))
    part_count = seq_count // head_count
    part_slots = head_count * token_count
    local_experts = expert_count // seq_count
    seq_place = lax.axis_index("seq")
    tp_place = lax.axis_index("tp")
    part = seq_place // head_count
    head = seq_place % head_count

    def tp_blocks(value):
        return [value] + [from_turned(value, "tp", turn) for turn in range(1, tp_count)]

    offsets = jnp.arange(token_count, dtype=jnp.int32)
    turns = jnp.arange(head_count, dtype=jnp.int32)
    aligned = part_count == prompt_count and part_slots + stagger <= HALF_WIN
    group_masks = masks_below(head_count)
    groups = [[first + k for k in range(head_count)] for first in range(0, seq_count, head_count)]
    part_masks = masks_below(seq_count, head_count)

    packed = pack_heads(w_query, w_key, w_value, part_count)
    packed, tokens = lax.optimization_barrier((packed, tokens))
    head_weights = lax.all_to_all(
        packed,
        "seq",
        split_axis=0,
        concat_axis=0,
        tiled=True,
    ).reshape(model_width, 3 * HEAD)

    normed = rms_scale(tokens.astype(jnp.float32), attn_gain).astype(jnp.bfloat16)
    share = lax.dynamic_slice_in_dim(normed, tp_place * col_share, col_share, 1)
    all_routes, part_turns = doubled(routes[None], part_masks, 0)
    out_all, _ = doubled(
        jnp.concatenate([w_out, router.T], axis=0).astype(jnp.bfloat16), part_masks, 1
    )
    first_rows, first_turns = doubled(share[None], group_masks[:1], 0)
    first_rows, layout_map = lax.optimization_barrier((first_rows, layout_map))
    own_first, own_second, own_up, own_down = order_experts(
        layout_map, expert_gate, expert_up, expert_down
    )
    part_ids = (part * head_count + (head ^ turns))[:, None] * token_count + offsets[None, :]
    part_ids = part_ids.reshape(-1)
    part_positions = prompt_split(part_ids, slot_len, stagger, prompt_count)[1]
    half_dim = HEAD // 2
    frequency = ROPE_BASE ** (-jnp.arange(half_dim, dtype=jnp.float32) / half_dim)
    angles = part_positions.astype(jnp.float32)[:, None] * frequency[None, :]
    cosine = jnp.cos(angles)
    sine_part = jnp.sin(angles)
    pieces = []
    for piece, masks in (
        (first_rows[:, :, : col_share // 2], group_masks[1:]),
        (first_rows[:, :, col_share // 2 :], group_masks[1:][::-1]),
    ):
        known = first_turns
        for mask in masks:
            if mask == masks[-1]:
                piece, own_first, cosine, sine_part, all_routes = lax.optimization_barrier(
                    (piece, own_first, cosine, sine_part, all_routes)
                )
            piece = jnp.concatenate([piece, swapped(piece, "seq", mask)], axis=0)
            known = known + [turn ^ mask for turn in known]
        pieces.append(jnp.concatenate([piece[known.index(m)] for m in range(head_count)], axis=0))
    part_rows = jnp.concatenate(pieces, axis=1)

    def to_owner(blocks):
        taken = lax.all_to_all(blocks, "seq", split_axis=0, concat_axis=0, tiled=True)
        taken = taken.reshape(seq_count, local_experts, *blocks.shape[1:])
        return jnp.swapaxes(taken, 0, 1).reshape(local_experts, model_width, blocks.shape[2])

    out_all, _ = doubled(out_all, group_masks[:-2], 1)
    out_rows = out_all.shape[0] // 32 * 16
    out_halves = [
        (out_all[:out_rows], group_masks[-2:]),
        (out_all[out_rows:], group_masks[-2:][::-1]),
    ]
    halves, head_weights, part_rows, own_first = lax.optimization_barrier(
        ([half for half, _ in out_halves], head_weights, part_rows, own_first)
    )
    server_first = to_owner(own_first)
    out_halves = [
        (doubled(half, masks[:1], 1)[0], masks[1:]) for half, (_, masks) in zip(halves, out_halves)
    ]

    def by_place(blocks):
        return jnp.stack(
            [
                lax.dynamic_index_in_dim(blocks, head ^ place, 0, keepdims=False)
                for place in range(head_count)
            ]
        )

    expert_ids = jnp.arange(expert_count, dtype=jnp.int32)
    block_rows = local_experts * capacity
    columns = jnp.arange(head_count * block_rows, dtype=jnp.int32)
    column_owner = part * head_count + columns // block_rows
    column_expert = column_owner * local_experts + columns // capacity % local_experts
    spread = (column_expert[None, :] == expert_ids[:, None]).astype(jnp.bfloat16)
    wanted = (columns % capacity).astype(jnp.float32)
    earlier = (offsets[:, None] > offsets[None, :]).astype(jnp.bfloat16)

    def routing(turn, own_routes):
        ids = (seq_place ^ turn) * token_count + offsets
        prompt, position = prompt_split(ids, slot_len, stagger, prompt_count)
        valid_token = position < length_of(prompt, real_lengths)
        chosen = jnp.any(own_routes[:, :, None] == expert_ids[None, None, :], axis=1)
        live = chosen & valid_token[:, None]
        rank = jnp.dot(earlier, live.astype(jnp.bfloat16), preferred_element_type=jnp.float32)
        rank = jnp.where(live, rank, -1.0).astype(jnp.bfloat16)
        placed = jnp.dot(rank, spread, preferred_element_type=jnp.float32) == wanted[None, :]
        return (chosen, valid_token, placed)

    routings = [routing(turn, all_routes[k]) for k, turn in enumerate(part_turns)]
    chosen, valid_token, _ = routings[0]

    starts = (tp_place + jnp.arange(tp_count, dtype=jnp.int32)) % tp_count * col_share
    rows = project(starts, tp_blocks(part_rows), head_weights, cosine, sine_part)
    sink = lax.dynamic_slice_in_dim(sink_logits, head, 1, 0)

    def start_state(row_count):
        return (
            jnp.broadcast_to(sink[:, None], (row_count, 1)),
            jnp.ones((row_count, 1), jnp.float32),
            jnp.zeros((row_count, HEAD), jnp.float32),
        )

    if aligned:
        edge_start = (head ^ (head_count - 1)) * token_count + token_count - stagger
        edge = from_behind(
            lax.dynamic_slice_in_dim(rows, edge_start, stagger, 0), "seq", head_count
        )
        edge_ids = part * part_slots - stagger + jnp.arange(stagger, dtype=jnp.int32)
        row_ids = jnp.concatenate([part_ids, edge_ids])
        row_prompt, row_position = prompt_split(row_ids, slot_len, stagger, prompt_count)
        row_live = (row_ids >= 0) & (row_position < length_of(row_prompt, real_lengths))
        halves, edge = lax.optimization_barrier(([half for half, _ in out_halves], edge))
        out_halves = [(half, masks) for half, (_, masks) in zip(halves, out_halves)]
        mixed = attend_once(
            sink,
            row_prompt,
            jnp.where(row_live, row_prompt, -1),
            jnp.concatenate([rows, edge], axis=0),
        )
        edge_back = from_behind(mixed[part_slots:], "seq", -head_count)
        mixed = mixed[:part_slots]
        kept = lax.dynamic_slice_in_dim(mixed, edge_start, stagger, 0)
        mixed = lax.dynamic_update_slice_in_dim(
            mixed, jnp.where(part < part_count - 1, edge_back, kept), edge_start, 0
        )
    else:
        query_rows, key_rows, value_rows = (rows[:, k * HEAD : (k + 1) * HEAD] for k in range(3))
        softmax_state = attend(
            start_state(part_slots),
            query_rows,
            key_rows,
            value_rows,
            key_rules(part_ids, part_ids, slot_len, stagger, total_slots, real_lengths),
        )
        from_below = from_above = jnp.concatenate([key_rows, value_rows], axis=1)
        for turn in range(1, min(part_count - 1, -(-HALF_WIN // part_slots)) + 1):
            from_below = from_behind(from_below, "seq", head_count)
            from_above = from_behind(from_above, "seq", -head_count)
            reach = turn * part_slots
            key_ids = jnp.concatenate([part_ids - reach, part_ids + reach])
            pair = jnp.concatenate([from_below, from_above], axis=0)
            softmax_state = attend(
                softmax_state,
                query_rows,
                pair[:, :HEAD],
                pair[:, HEAD:],
                key_rules(part_ids, key_ids, slot_len, stagger, total_slots, real_lengths),
            )
        _, denominator, accumulated = softmax_state
        mixed = (accumulated / denominator).astype(jnp.bfloat16)
    blocks = by_place(mixed.reshape(head_count, token_count, HEAD))
    out_halves = [(half, swapped(half, "seq", masks[0])) for half, masks in out_halves]
    blocks, out_halves, server_first = lax.optimization_barrier((blocks, out_halves, server_first))
    attention_result = lax.all_to_all(
        blocks, "seq", split_axis=0, concat_axis=0, tiled=True, axis_index_groups=groups
    )
    attention_result, own_second = lax.optimization_barrier((attention_result, own_second))
    server_second = to_owner(own_second)

    proj_width = head_count * HEAD
    def joined(pieces, half):
        if half == 0:
            return jnp.concatenate(pieces, axis=1)
        span = pieces[0].shape[1] // 2
        low, high = ([piece[:, k * span : (k + 1) * span] for piece in pieces] for k in range(2))
        return jnp.concatenate([*low, *high], axis=1)

    if out_rows % HEAD == 0 and out_rows < proj_width:
        partial_out = out_project(attention_result, [*out_halves[0], *out_halves[1]])
    else:
        attention_result = jnp.swapaxes(attention_result, 0, 1).reshape(token_count, proj_width)
        partial_out = sum(
            joined([jnp.dot(rows, piece, preferred_element_type=jnp.float32) for piece in pieces], half)
            for half, (rows, pieces) in enumerate(
                (
                    (attention_result[:, :out_rows], out_halves[0]),
                    (
                        attention_result[:, out_rows:],
                        [piece[: proj_width - out_rows] for piece in out_halves[1]],
                    ),
                )
            )
        )
    if tp_count == 2:
        out_pieces = [partial_out, from_turned(partial_out, "tp", 1)]
    else:
        out_pieces = [lax.psum(partial_out, "tp")]
    router_rows = joined([piece[proj_width - out_rows :] for piece in out_halves[1]], 1)
    slots = jnp.arange(seq_count, dtype=jnp.int32)
    turn = seq_place ^ slots
    bits = len(part_masks) + len(group_masks)
    out_places = sum(((turn >> k) & 1) << (bits - 1 - k) for k in range(bits))
    width = w_out.shape[1]
    if width % 128:

        def in_order(value):
            blocks = [
                lax.dynamic_slice_in_dim(value, out_places[place] * width, width, 1)
                for place in range(seq_count)
            ]
            return jnp.concatenate(blocks, axis=1)

        out_pieces, router_rows = ([in_order(piece) for piece in out_pieces], in_order(router_rows))
        out_places, width = (jnp.zeros((1,), jnp.int32), model_width)
    full_rows, outgoing, logits = settle(
        out_places, out_pieces, tokens, mlp_gain, router_rows, width
    )
    residual = lax.dynamic_slice_in_dim(full_rows, tp_place * col_share, col_share, 1)
    outgoing_share = lax.dynamic_slice_in_dim(outgoing, tp_place * col_share, col_share, 1)


    route_logits = jnp.where(chosen, logits, -jnp.inf)
    route_exp = jnp.exp(route_logits - jnp.max(route_logits, axis=1, keepdims=True))
    route_weight = route_exp / jnp.sum(route_exp, axis=1, keepdims=True)
    route_weight = route_weight * valid_token[:, None]
    all_weights, _ = doubled(route_weight[None], part_masks, 0)
    all_rows, _ = doubled(outgoing_share[None], part_masks, 0)
    all_rows, all_weights, server_second, own_up = lax.optimization_barrier(
        (all_rows, all_weights, server_second, own_up)
    )
    server_up = to_owner(own_up)
    buffer = jnp.stack(
        [
            lax.dot_general(
                placed.astype(jnp.bfloat16),
                all_rows[k],
                (((0,), (0,)), ((), ())),
                preferred_element_type=jnp.float32,
            )
            .astype(jnp.bfloat16)
            .reshape(head_count, block_rows, col_share)
            for k, (_, _, placed) in enumerate(routings)
        ],
        axis=1,
    )
    def to_mate(m):
        block = lax.dynamic_index_in_dim(buffer, head ^ m, 0, keepdims=False)
        return swapped(block, "seq", m) if m else block

    received = [to_mate(m) for m in range(head_count)]
    received[1:3], server_up, own_down = lax.optimization_barrier(
        (received[1:3], server_up, own_down)
    )
    server_down = to_owner(own_down)
    received = by_place(jnp.stack(received))
    received = received.reshape(head_count, part_count, local_experts, capacity, col_share)
    turn_ids = jnp.arange(tp_count, dtype=jnp.int32)
    in_starts = (tp_place + turn_ids) % tp_count * col_share
    out_starts = (tp_place - turn_ids) % tp_count * col_share

    halves = [
        tp_blocks(jnp.moveaxis(rows, 2, 0).reshape(local_experts, -1, col_share))
        for rows in (received[:, 1:], received[:, :1])
    ]
    server = (server_first, server_second, server_up)
    hidden = hidden_units(in_starts, halves[0], server)
    hidden, own_half, server_down = lax.optimization_barrier((hidden, halves[1], server_down))
    hidden = [hidden, hidden_units(in_starts, own_half, server)]

    def through_experts(rows, parts):
        outs = down_rows(out_starts, rows, server_down)
        outs = [outs[0]] + [from_turned(outs[k], "tp", k) for k in range(1, tp_count)]
        summed = sum(piece.astype(jnp.float32) for piece in outs).astype(jnp.bfloat16)
        summed = summed.reshape(local_experts, head_count, parts, capacity, col_share)
        return jnp.moveaxis(summed, 0, 2).reshape(head_count, parts, block_rows, col_share)

    others = through_experts(hidden[0], part_count - 1)
    own_rows = through_experts(hidden[1], 1)

    def weighted(k, rows):
        placed = routings[k][2]
        stacked = jnp.concatenate(
            [
                jnp.where(
                    placed, jnp.dot(piece, spread, preferred_element_type=jnp.float32), 0.0
                ).astype(jnp.bfloat16)
                for piece in parts_of(all_weights[k], 3)
            ],
            axis=0,
        )
        mixes = jnp.dot(stacked, rows, preferred_element_type=jnp.float32)
        return sum(mixes[k * token_count : (k + 1) * token_count] for k in range(3))

    def back(blocks):
        return lax.all_to_all(
            blocks, "seq", split_axis=0, concat_axis=0, tiled=True, axis_index_groups=groups
        )

    others = back(others)
    mixes = [
        weighted(k, others[:, k - 1].reshape(-1, col_share)) for k in range(1, len(part_turns))
    ]
    mixes, own_rows = lax.optimization_barrier((mixes, own_rows))
    expert_mix = sum(
        swapped(mix.astype(jnp.bfloat16), "seq", turn).astype(jnp.float32)
        for mix, turn in zip(mixes, part_turns[1:])
    )
    own_mix = weighted(0, back(own_rows)[:, 0].reshape(-1, col_share))
    return (residual + (expert_mix + own_mix)).astype(jnp.bfloat16)


def solution(mesh):
    placed = (
        P("seq", None),
        P(),
        P(),
        P("seq", "tp"),
        P("seq", "tp"),
        P("seq", "tp"),
        P("tp", "seq"),
        P("tp"),
        P("seq", None),
        P(None, "seq", "tp"),
        P(None, "seq", "tp"),
        P(None, "seq", "tp"),
        P(),
        P(),
        P("seq", None),
    )
    return jax.shard_map(
        shards, mesh=mesh, in_specs=placed, out_specs=P("seq", "tp"), check_vma=False
    )
```

```python
import jax
import jax.numpy as jnp
from jax import lax
from jax.experimental import pallas as pl
from jax.experimental.pallas import tpu as pltpu
from jax.sharding import PartitionSpec as P

HEAD = 128
HALF_WIN = 2048


EPSILON = 1e-05
ROPE_BASE = 50000.0
MASKED = -1e30
SMALL = pl.CostEstimate(flops=1, bytes_accessed=1, transcendentals=1)


def from_behind(value, axis, steps):
    count = lax.axis_size(axis)
    first, last = (max(0, -steps), min(count, count - steps))
    return lax.ppermute(value, axis, [(source, source + steps) for source in range(first, last)])


def from_turned(value, axis, turn):
    count = lax.axis_size(axis)
    return lax.ppermute(value, axis, [((place + turn) % count, place) for place in range(count)])


def swapped(value, axis, mask):
    count = lax.axis_size(axis)
    return lax.ppermute(value, axis, [(place, place ^ mask) for place in range(count)])


def doubled(value, masks, axis):
    turns = [0]
    for mask in masks:
        value = jnp.concatenate([value, swapped(value, "seq", mask)], axis=axis)
        turns = turns + [turn ^ mask for turn in turns]
    return (value, turns)


def masks_below(count, least=1):
    masks = []
    while count > least:
        count //= 2
        masks.append(count)
    return masks


def rms_scale(row_values, gain_vector):
    mean_square = jnp.mean(row_values * row_values, axis=-1, keepdims=True)
    return row_values * lax.rsqrt(mean_square + EPSILON) * gain_vector


def rotate(rows, cosine, sine_part):
    half_dim = rows.shape[-1] // 2
    first_half = rows[:, :half_dim]
    second_half = rows[:, half_dim:]
    return jnp.concatenate(
        [
            first_half * cosine - second_half * sine_part,
            second_half * cosine + first_half * sine_part,
        ],
        axis=-1,
    )


def length_of(prompt, real_lengths):
    one_hot = prompt[:, None] == jnp.arange(real_lengths.shape[0], dtype=jnp.int32)[None, :]
    return jnp.sum(jnp.where(one_hot, real_lengths[None, :], 0), axis=1)


def prompt_split(slot_ids, slot_len, stagger, prompt_count):
    prompt = jnp.minimum((slot_ids + stagger) // slot_len, prompt_count - 1)
    start = jnp.maximum(prompt * slot_len - stagger, 0)
    return (prompt, slot_ids - start)


def key_rules(query_ids, key_ids, slot_len, stagger, total_slots, real_lengths):
    prompt_count = real_lengths.shape[0]
    key_prompt, key_pos = prompt_split(key_ids, slot_len, stagger, prompt_count)
    query_prompt = prompt_split(query_ids, slot_len, stagger, prompt_count)[0]
    inside = (key_ids >= 0) & (key_ids < total_slots)
    key_live = inside & (key_pos < length_of(key_prompt, real_lengths))
    same_prompt = query_prompt[:, None] == key_prompt[None, :]
    nearby = jnp.abs(query_ids[:, None] - key_ids[None, :]) < HALF_WIN
    return same_prompt & nearby & key_live[None, :]


def parts_of(values, count):
    rest = values
    pieces = []
    for _ in range(count):
        piece = lax.reduce_precision(rest, 8, 7)
        rest = rest - piece
        pieces.append(piece.astype(jnp.bfloat16))
    return pieces


def attend(softmax_state, query_rows, key_rows, value_rows, allowed):
    running_max, denominator, accumulated = softmax_state
    scores = lax.dot_general(
        query_rows, key_rows, (((1,), (1,)), ((), ())), preferred_element_type=jnp.float32
    ) * HEAD ** (-0.5)
    scores = jnp.where(allowed, scores, MASKED)
    new_max = jnp.maximum(running_max, jnp.max(scores, axis=1, keepdims=True))
    rescale = jnp.exp(running_max - new_max)
    weight_tensors = jnp.exp(scores - new_max)
    denominator = denominator * rescale + jnp.sum(weight_tensors, axis=1, keepdims=True)
    high, low = parts_of(weight_tensors, 2)
    accumulated = (
        accumulated * rescale
        + jnp.dot(high, value_rows, preferred_element_type=jnp.float32)
        + jnp.dot(low, value_rows, preferred_element_type=jnp.float32)
    )
    return (new_max, denominator, accumulated)


def order_body(order_ref, gate_ref, up_ref, down_ref, *outs):
    half = gate_ref.shape[2] // 2
    outs[0][...] = gate_ref[:, :, :half].astype(jnp.bfloat16)
    outs[1][...] = gate_ref[:, :, half:].astype(jnp.bfloat16)
    outs[2][...] = up_ref[...].astype(jnp.bfloat16)
    outs[3][...] = down_ref[...].astype(jnp.bfloat16)


def order_experts(layout_map, gate, up, down):
    count, rows, width = gate.shape
    source = pl.BlockSpec((1, rows, width), lambda place, order: (order[place], 0, 0))
    widths = (width // 2, width - width // 2, width, width)
    return pl.pallas_call(
        order_body,
        grid_spec=pltpu.PrefetchScalarGridSpec(
            num_scalar_prefetch=1,
            grid=(count,),
            in_specs=[source, source, source],
            out_specs=[
                pl.BlockSpec((1, rows, some), lambda place, order: (place, 0, 0))
                for some in widths
            ],
        ),
        out_shape=[jax.ShapeDtypeStruct((count, rows, some), jnp.bfloat16) for some in widths],
        cost_estimate=SMALL,
        name="order_experts",
    )(layout_map, gate, up, down)


def pack_body(query_ref, key_ref, value_ref, out_ref):
    heads = query_ref.shape[1] // HEAD
    for place in range(out_ref.shape[0]):
        head = place % heads
        for k, source in enumerate((query_ref, key_ref, value_ref)):
            out_ref[place, :, k * HEAD : (k + 1) * HEAD] = source[
                :, head * HEAD : (head + 1) * HEAD
            ].astype(jnp.bfloat16)


def pack_heads(w_query, w_key, w_value, copies):
    rows, width = w_query.shape
    places = copies * (width // HEAD)
    step = rows // 4 if rows % 64 == 0 else rows
    source = pl.BlockSpec((step, width), lambda place: (place, 0))
    return pl.pallas_call(
        pack_body,
        grid=(rows // step,),
        in_specs=[source, source, source],
        out_specs=pl.BlockSpec((places, step, 3 * HEAD), lambda place: (0, place, 0)),
        out_shape=jax.ShapeDtypeStruct((places, rows, 3 * HEAD), jnp.bfloat16),
        compiler_params=pltpu.CompilerParams(vmem_limit_bytes=32 * 2**20),
        cost_estimate=SMALL,
        name="pack_heads",
    )(w_query, w_key, w_value)


def project_body(turn_count, share, start_ref, *refs):
    rows, (weight_ref, cosine_ref, sine_ref, out_ref) = (refs[:turn_count], refs[turn_count:])
    product = 0.0
    for turn in range(turn_count):
        first = pl.multiple_of(start_ref[turn], share)
        product = product + jnp.dot(
            rows[turn][...], weight_ref[pl.ds(first, share), :], preferred_element_type=jnp.float32
        )
    cosine, sine_part = (cosine_ref[...], sine_ref[...])
    out_ref[:, :HEAD] = rotate(product[:, :HEAD], cosine, sine_part).astype(jnp.bfloat16)
    out_ref[:, HEAD : 2 * HEAD] = rotate(
        product[:, HEAD : 2 * HEAD], cosine, sine_part
    ).astype(jnp.bfloat16)
    out_ref[:, 2 * HEAD :] = product[:, 2 * HEAD :].astype(jnp.bfloat16)


def project(starts, row_blocks, weights, cosine, sine_part):
    row_count, share = row_blocks[0].shape
    step = row_count // 4
    whole = pl.BlockSpec(weights.shape, lambda place, starts: (0, 0))
    angle = pl.BlockSpec((step, cosine.shape[1]), lambda place, starts: (place, 0))
    return pl.pallas_call(
        lambda *refs: project_body(len(row_blocks), share, *refs),
        grid_spec=pltpu.PrefetchScalarGridSpec(
            num_scalar_prefetch=1,
            grid=(4,),
            in_specs=[pl.BlockSpec((step, share), lambda place, starts: (place, 0))]
            * len(row_blocks)
            + [whole, angle, angle],
            out_specs=pl.BlockSpec((step, weights.shape[1]), lambda place, starts: (place, 0)),
        ),
        out_shape=jax.ShapeDtypeStruct((row_count, weights.shape[1]), jnp.bfloat16),
        compiler_params=pltpu.CompilerParams(vmem_limit_bytes=32 * 2**20),
        cost_estimate=SMALL,
        name="project",
    )(starts, *row_blocks, weights, cosine, sine_part)


def attend_body(sink_ref, query_prompt_ref, key_prompt_ref, query_ref, key_ref, value_ref, out_ref):
    sink = sink_ref[0]
    scores = lax.dot_general(
        query_ref[...],
        key_ref[...],
        (((1,), (1,)), ((), ())),
        preferred_element_type=jnp.float32,
    ) * HEAD ** (-0.5)
    scores = jnp.where(query_prompt_ref[...] == key_prompt_ref[...], scores, MASKED)
    top = jnp.maximum(sink, jnp.max(scores, axis=1, keepdims=True))
    weights = jnp.exp(scores - top)
    denominator = jnp.exp(sink - top) + jnp.sum(weights, axis=1, keepdims=True)
    high = weights.astype(jnp.bfloat16)
    low = (weights - high.astype(jnp.float32)).astype(jnp.bfloat16)
    values = value_ref[...]
    mix = jnp.dot(high, values, preferred_element_type=jnp.float32) + jnp.dot(
        low, values, preferred_element_type=jnp.float32
    )
    out_ref[...] = (mix / denominator).astype(jnp.bfloat16)


def attend_once(sink, query_prompt, key_prompt, rows):
    row_count = rows.shape[0]
    steps = 4 if row_count % 64 == 0 else 1
    step = row_count // steps
    return pl.pallas_call(
        attend_body,
        grid=(steps,),
        in_specs=[
            pl.BlockSpec(memory_space=pltpu.SMEM),
            pl.BlockSpec((step, 1), lambda place: (place, 0)),
            pl.BlockSpec((1, row_count), lambda place: (0, 0)),
            pl.BlockSpec((step, HEAD), lambda place: (place, 0)),
            pl.BlockSpec((row_count, HEAD), lambda place: (0, 1)),
            pl.BlockSpec((row_count, HEAD), lambda place: (0, 2)),
        ],
        out_specs=pl.BlockSpec((step, HEAD), lambda place: (place, 0)),
        out_shape=jax.ShapeDtypeStruct((row_count, HEAD), jnp.bfloat16),
        compiler_params=pltpu.CompilerParams(vmem_limit_bytes=32 * 2**20),
        cost_estimate=SMALL,
        name="attend_once",
    )(sink, query_prompt[:, None], key_prompt[None, :], rows, rows, rows)


def out_body(head_ref, first_ref, first_other_ref, second_ref, second_other_ref, out_ref):
    heads = first_ref.shape[0] // HEAD
    first, second = (
        jnp.concatenate([head_ref[h] for h in place], axis=1)
        for place in (range(heads), range(heads, head_ref.shape[0]))
    )
    rows = second.shape[1]
    half = first_ref.shape[1]
    span = half // 2
    for k, (one, two) in enumerate(
        ((first_ref, second_ref), (first_other_ref, second_other_ref))
    ):
        own = jnp.dot(first, one[...], preferred_element_type=jnp.float32)
        other = jnp.dot(second, two[:rows, :], preferred_element_type=jnp.float32)
        if k == 0:
            low, high = (other[:, :span], other[:, span:])
            out_ref[:, :span] = own[:, :span] + low
            out_ref[:, span:half] = own[:, span:]
            out_ref[:, half : half + span] = high
        else:
            out_ref[:, span:half] = out_ref[:, span:half] + other[:, :span]
            out_ref[:, half : half + span] = out_ref[:, half : half + span] + own[:, :span]
            out_ref[:, half + span :] = own[:, span:] + other[:, span:]


def out_project(heads, pieces):
    vmem = pl.BlockSpec(memory_space=pltpu.VMEM)
    return pl.pallas_call(
        out_body,
        in_specs=[vmem] * 5,
        out_specs=vmem,
        out_shape=jax.ShapeDtypeStruct((heads.shape[1], 2 * pieces[0].shape[1]), jnp.float32),
        compiler_params=pltpu.CompilerParams(vmem_limit_bytes=40 * 2**20),
        cost_estimate=SMALL,
        name="out_project",
    )(heads, *pieces)


def settle_body(piece_count, width, place_ref, *refs):
    pieces = refs[:piece_count]
    token_ref, gain_ref, router_ref, full_ref, outgoing_ref, logit_ref, router_all = refs[
        piece_count:
    ]
    for place in range(full_ref.shape[1] // width):
        here = slice(place * width, (place + 1) * width)
        there = pl.ds(pl.multiple_of(place_ref[place] * width, width), width)
        block = sum(piece[:, there] for piece in pieces)
        full_ref[:, here] = token_ref[:, here].astype(jnp.float32) + block
        router_all[:, here] = router_ref[:, there]
    outgoing = rms_scale(full_ref[...], gain_ref[...]).astype(jnp.bfloat16)
    outgoing_ref[...] = outgoing
    logit_ref[...] = lax.dot_general(
        outgoing,
        router_all[...],
        (((1,), (1,)), ((), ())),
        preferred_element_type=jnp.float32,
    )


def settle(places, pieces, tokens, gain, router, width):
    rows, columns = tokens.shape
    vmem = pl.BlockSpec(memory_space=pltpu.VMEM)
    return pl.pallas_call(
        lambda *refs: settle_body(len(pieces), width, *refs),
        in_specs=[pl.BlockSpec(memory_space=pltpu.SMEM)] + [vmem] * (len(pieces) + 3),
        out_specs=[vmem] * 3,
        out_shape=[
            jax.ShapeDtypeStruct((rows, columns), jnp.float32),
            jax.ShapeDtypeStruct((rows, columns), jnp.bfloat16),
            jax.ShapeDtypeStruct((rows, router.shape[0]), jnp.float32),
        ],
        scratch_shapes=[pltpu.VMEM(router.shape, jnp.bfloat16)],
        compiler_params=pltpu.CompilerParams(vmem_limit_bytes=32 * 2**20),
        cost_estimate=SMALL,
        name="settle",
    )(places, *pieces, tokens, gain[None, :], router)


def hidden_body(turn_count, share, start_ref, *refs):
    rows, (first_ref, second_ref, up_ref, out_ref) = (refs[:turn_count], refs[turn_count:])
    first = second = up = 0.0
    for turn in range(turn_count):
        here = pl.ds(pl.multiple_of(start_ref[turn], share), share)
        some = rows[turn][0]
        first = first + jnp.dot(some, first_ref[0, here, :], preferred_element_type=jnp.float32)
        second = second + jnp.dot(some, second_ref[0, here, :], preferred_element_type=jnp.float32)
        up = up + jnp.dot(some, up_ref[0, here, :], preferred_element_type=jnp.float32)
    gate = jnp.concatenate([first, second], axis=1)
    out_ref[0] = (gate / (1.0 + jnp.exp(-gate)) * up).astype(jnp.bfloat16)


def hidden_units(starts, row_blocks, weights):
    local_experts, row_count, share = row_blocks[0].shape
    width = weights[-1].shape[2]
    count = len(row_blocks)
    return pl.pallas_call(
        lambda *refs: hidden_body(count, share, *refs),
        grid_spec=pltpu.PrefetchScalarGridSpec(
            num_scalar_prefetch=1,
            grid=(local_experts,),
            in_specs=[pl.BlockSpec((1, row_count, share), lambda e, a: (e, 0, 0))] * count
            + [pl.BlockSpec((1, *w.shape[1:]), lambda e, a: (e, 0, 0)) for w in weights],
            out_specs=pl.BlockSpec((1, row_count, width), lambda e, a: (e, 0, 0)),
        ),
        out_shape=jax.ShapeDtypeStruct((local_experts, row_count, width), jnp.bfloat16),
        compiler_params=pltpu.CompilerParams(vmem_limit_bytes=52 * 2**20),
        cost_estimate=SMALL,
        name="hidden_units",
    )(starts, *row_blocks, *weights)


def down_body(turn_count, share, start_ref, hidden_ref, down_ref, *outs):
    for turn in range(turn_count):
        here = pl.ds(pl.multiple_of(start_ref[turn], share), share)
        outs[turn][0] = lax.dot_general(
            hidden_ref[0],
            down_ref[0, here, :],
            (((1,), (1,)), ((), ())),
            preferred_element_type=jnp.float32,
        ).astype(jnp.bfloat16)


def down_rows(starts, hidden, down):
    local_experts, row_count, width = hidden.shape
    columns, count = (down.shape[1], starts.shape[0])
    share = columns // count
    block = pl.BlockSpec((1, row_count, share), lambda e, a: (e, 0, 0))
    return pl.pallas_call(
        lambda *refs: down_body(count, share, *refs),
        grid_spec=pltpu.PrefetchScalarGridSpec(
            num_scalar_prefetch=1,
            grid=(local_experts,),
            in_specs=[
                pl.BlockSpec((1, row_count, width), lambda e, a: (e, 0, 0)),
                pl.BlockSpec((1, columns, width), lambda e, a: (e, 0, 0)),
            ],
            out_specs=[block] * count,
        ),
        out_shape=[jax.ShapeDtypeStruct((local_experts, row_count, share), jnp.bfloat16)] * count,
        compiler_params=pltpu.CompilerParams(vmem_limit_bytes=52 * 2**20),
        cost_estimate=SMALL,
        name="down_rows",
    )(starts, hidden, down)


def shards(
    tokens,
    attn_gain,
    mlp_gain,
    w_query,
    w_key,
    w_value,
    w_out,
    sink_logits,
    router,
    expert_gate,
    expert_up,
    expert_down,
    layout_map,
    real_lengths,
    routes,
):
    token_count, model_width = tokens.shape
    seq_count = lax.axis_size("seq")
    tp_count = lax.axis_size("tp")
    expert_count = router.shape[1]
    route_count = routes.shape[1]
    head_count = sink_logits.shape[0]
    col_share = model_width // tp_count
    total_slots = token_count * seq_count
    prompt_count = real_lengths.shape[0]
    slot_len = total_slots // prompt_count
    stagger = token_count // 2
    capacity = max(2, min(token_count, 9 * token_count * route_count // (8 * expert_count)))
    part_count = seq_count // head_count
    part_slots = head_count * token_count
    local_experts = expert_count // seq_count
    seq_place = lax.axis_index("seq")
    tp_place = lax.axis_index("tp")
    part = seq_place // head_count
    head = seq_place % head_count

    def tp_blocks(value):
        return [value] + [from_turned(value, "tp", turn) for turn in range(1, tp_count)]

    offsets = jnp.arange(token_count, dtype=jnp.int32)
    turns = jnp.arange(head_count, dtype=jnp.int32)
    aligned = part_count == prompt_count and part_slots + stagger <= HALF_WIN
    group_masks = masks_below(head_count)
    groups = [[first + k for k in range(head_count)] for first in range(0, seq_count, head_count)]
    part_masks = masks_below(seq_count, head_count)

    packed = pack_heads(w_query, w_key, w_value, part_count)
    packed, tokens = lax.optimization_barrier((packed, tokens))
    head_weights = lax.all_to_all(
        packed,
        "seq",
        split_axis=0,
        concat_axis=0,
        tiled=True,
    ).reshape(model_width, 3 * HEAD)

    normed = rms_scale(tokens.astype(jnp.float32), attn_gain).astype(jnp.bfloat16)
    share = lax.dynamic_slice_in_dim(normed, tp_place * col_share, col_share, 1)
    out_all, _ = doubled(
        jnp.concatenate([w_out, router.T], axis=0).astype(jnp.bfloat16), part_masks, 1
    )
    first_rows, first_turns = doubled(share[None], group_masks[:1], 0)
    first_rows, layout_map = lax.optimization_barrier((first_rows, layout_map))
    own_first, own_second, own_up, own_down = order_experts(
        layout_map, expert_gate, expert_up, expert_down
    )
    part_ids = (part * head_count + (head ^ turns))[:, None] * token_count + offsets[None, :]
    part_ids = part_ids.reshape(-1)
    part_positions = prompt_split(part_ids, slot_len, stagger, prompt_count)[1]
    half_dim = HEAD // 2
    frequency = ROPE_BASE ** (-jnp.arange(half_dim, dtype=jnp.float32) / half_dim)
    angles = part_positions.astype(jnp.float32)[:, None] * frequency[None, :]
    cosine = jnp.cos(angles)
    sine_part = jnp.sin(angles)
    pieces = []
    for piece, masks in (
        (first_rows[:, :, : col_share // 2], group_masks[1:]),
        (first_rows[:, :, col_share // 2 :], group_masks[1:][::-1]),
    ):
        known = first_turns
        for mask in masks:
            if mask == masks[-1]:
                piece, own_first, cosine, sine_part = lax.optimization_barrier(
                    (piece, own_first, cosine, sine_part)
                )
            piece = jnp.concatenate([piece, swapped(piece, "seq", mask)], axis=0)
            known = known + [turn ^ mask for turn in known]
        pieces.append(jnp.concatenate([piece[known.index(m)] for m in range(head_count)], axis=0))
    part_rows = jnp.concatenate(pieces, axis=1)

    def to_owner(blocks):
        taken = lax.all_to_all(blocks, "seq", split_axis=0, concat_axis=0, tiled=True)
        taken = taken.reshape(seq_count, local_experts, *blocks.shape[1:])
        return jnp.swapaxes(taken, 0, 1).reshape(local_experts, model_width, blocks.shape[2])

    out_all, _ = doubled(out_all, group_masks[:-2], 1)
    out_rows = out_all.shape[0] // 32 * 16
    out_halves = [
        (out_all[:out_rows], group_masks[-2:]),
        (out_all[out_rows:], group_masks[-2:][::-1]),
    ]
    halves, head_weights, part_rows, own_first = lax.optimization_barrier(
        ([half for half, _ in out_halves], head_weights, part_rows, own_first)
    )
    server_first = to_owner(own_first)
    out_halves = [
        (doubled(half, masks[:1], 1)[0], masks[1:]) for half, (_, masks) in zip(halves, out_halves)
    ]

    def by_place(blocks):
        return jnp.stack(
            [
                lax.dynamic_index_in_dim(blocks, head ^ place, 0, keepdims=False)
                for place in range(head_count)
            ]
        )

    expert_ids = jnp.arange(expert_count, dtype=jnp.int32)
    block_rows = local_experts * capacity
    columns = jnp.arange(head_count * block_rows, dtype=jnp.int32)
    column_owner = part * head_count + columns // block_rows
    column_expert = column_owner * local_experts + columns // capacity % local_experts
    spread = (column_expert[None, :] == expert_ids[:, None]).astype(jnp.bfloat16)
    wanted = (columns % capacity).astype(jnp.float32)
    earlier = (offsets[:, None] > offsets[None, :]).astype(jnp.bfloat16)

    def routing(turn, own_routes):
        ids = (seq_place ^ turn) * token_count + offsets
        prompt, position = prompt_split(ids, slot_len, stagger, prompt_count)
        valid_token = position < length_of(prompt, real_lengths)
        chosen = jnp.any(own_routes[:, :, None] == expert_ids[None, None, :], axis=1)
        live = chosen & valid_token[:, None]
        rank = jnp.dot(earlier, live.astype(jnp.bfloat16), preferred_element_type=jnp.float32)
        rank = jnp.where(live, rank, -1.0).astype(jnp.bfloat16)
        placed = jnp.dot(rank, spread, preferred_element_type=jnp.float32) == wanted[None, :]
        return (chosen, valid_token, placed)


    starts = (tp_place + jnp.arange(tp_count, dtype=jnp.int32)) % tp_count * col_share
    rows = project(starts, tp_blocks(part_rows), head_weights, cosine, sine_part)
    rows, routes = lax.optimization_barrier((rows, routes))
    all_routes, part_turns = doubled(routes[None], part_masks, 0)
    sink = lax.dynamic_slice_in_dim(sink_logits, head, 1, 0)

    def start_state(row_count):
        return (
            jnp.broadcast_to(sink[:, None], (row_count, 1)),
            jnp.ones((row_count, 1), jnp.float32),
            jnp.zeros((row_count, HEAD), jnp.float32),
        )

    if aligned:
        edge_start = (head ^ (head_count - 1)) * token_count + token_count - stagger
        edge = from_behind(
            lax.dynamic_slice_in_dim(rows, edge_start, stagger, 0), "seq", head_count
        )
        edge_ids = part * part_slots - stagger + jnp.arange(stagger, dtype=jnp.int32)
        row_ids = jnp.concatenate([part_ids, edge_ids])
        row_prompt, row_position = prompt_split(row_ids, slot_len, stagger, prompt_count)
        row_live = (row_ids >= 0) & (row_position < length_of(row_prompt, real_lengths))
        halves, edge, all_routes = lax.optimization_barrier(
            ([half for half, _ in out_halves], edge, all_routes)
        )
        out_halves = [(half, masks) for half, (_, masks) in zip(halves, out_halves)]
        mixed = attend_once(
            sink,
            row_prompt,
            jnp.where(row_live, row_prompt, -1),
            jnp.concatenate([rows, edge], axis=0),
        )
        edge_back = from_behind(mixed[part_slots:], "seq", -head_count)
        mixed = mixed[:part_slots]
        kept = lax.dynamic_slice_in_dim(mixed, edge_start, stagger, 0)
        mixed = lax.dynamic_update_slice_in_dim(
            mixed, jnp.where(part < part_count - 1, edge_back, kept), edge_start, 0
        )
    else:
        query_rows, key_rows, value_rows = (rows[:, k * HEAD : (k + 1) * HEAD] for k in range(3))
        softmax_state = attend(
            start_state(part_slots),
            query_rows,
            key_rows,
            value_rows,
            key_rules(part_ids, part_ids, slot_len, stagger, total_slots, real_lengths),
        )
        from_below = from_above = jnp.concatenate([key_rows, value_rows], axis=1)
        for turn in range(1, min(part_count - 1, -(-HALF_WIN // part_slots)) + 1):
            from_below = from_behind(from_below, "seq", head_count)
            from_above = from_behind(from_above, "seq", -head_count)
            reach = turn * part_slots
            key_ids = jnp.concatenate([part_ids - reach, part_ids + reach])
            pair = jnp.concatenate([from_below, from_above], axis=0)
            softmax_state = attend(
                softmax_state,
                query_rows,
                pair[:, :HEAD],
                pair[:, HEAD:],
                key_rules(part_ids, key_ids, slot_len, stagger, total_slots, real_lengths),
            )
        _, denominator, accumulated = softmax_state
        mixed = (accumulated / denominator).astype(jnp.bfloat16)
    routings = [routing(turn, all_routes[k]) for k, turn in enumerate(part_turns)]
    chosen, valid_token, _ = routings[0]
    blocks = by_place(mixed.reshape(head_count, token_count, HEAD))
    out_halves = [(half, swapped(half, "seq", masks[0])) for half, masks in out_halves]
    blocks, out_halves, server_first = lax.optimization_barrier((blocks, out_halves, server_first))
    attention_result = lax.all_to_all(
        blocks, "seq", split_axis=0, concat_axis=0, tiled=True, axis_index_groups=groups
    )
    attention_result, own_second = lax.optimization_barrier((attention_result, own_second))
    server_second = to_owner(own_second)

    proj_width = head_count * HEAD
    def joined(pieces, half):
        if half == 0:
            return jnp.concatenate(pieces, axis=1)
        span = pieces[0].shape[1] // 2
        low, high = ([piece[:, k * span : (k + 1) * span] for piece in pieces] for k in range(2))
        return jnp.concatenate([*low, *high], axis=1)

    if out_rows % HEAD == 0 and out_rows < proj_width:
        partial_out = out_project(attention_result, [*out_halves[0], *out_halves[1]])
    else:
        attention_result = jnp.swapaxes(attention_result, 0, 1).reshape(token_count, proj_width)
        partial_out = sum(
            joined([jnp.dot(rows, piece, preferred_element_type=jnp.float32) for piece in pieces], half)
            for half, (rows, pieces) in enumerate(
                (
                    (attention_result[:, :out_rows], out_halves[0]),
                    (
                        attention_result[:, out_rows:],
                        [piece[: proj_width - out_rows] for piece in out_halves[1]],
                    ),
                )
            )
        )
    if tp_count == 2:
        out_pieces = [partial_out, from_turned(partial_out, "tp", 1)]
    else:
        out_pieces = [lax.psum(partial_out, "tp")]
    router_rows = joined([piece[proj_width - out_rows :] for piece in out_halves[1]], 1)
    slots = jnp.arange(seq_count, dtype=jnp.int32)
    turn = seq_place ^ slots
    bits = len(part_masks) + len(group_masks)
    out_places = sum(((turn >> k) & 1) << (bits - 1 - k) for k in range(bits))
    width = w_out.shape[1]
    if width % 128:

        def in_order(value):
            blocks = [
                lax.dynamic_slice_in_dim(value, out_places[place] * width, width, 1)
                for place in range(seq_count)
            ]
            return jnp.concatenate(blocks, axis=1)

        out_pieces, router_rows = ([in_order(piece) for piece in out_pieces], in_order(router_rows))
        out_places, width = (jnp.zeros((1,), jnp.int32), model_width)
    full_rows, outgoing, logits = settle(
        out_places, out_pieces, tokens, mlp_gain, router_rows, width
    )
    residual = lax.dynamic_slice_in_dim(full_rows, tp_place * col_share, col_share, 1)
    outgoing_share = lax.dynamic_slice_in_dim(outgoing, tp_place * col_share, col_share, 1)


    route_logits = jnp.where(chosen, logits, -jnp.inf)
    route_exp = jnp.exp(route_logits - jnp.max(route_logits, axis=1, keepdims=True))
    route_weight = route_exp / jnp.sum(route_exp, axis=1, keepdims=True)
    route_weight = route_weight * valid_token[:, None]
    all_weights, _ = doubled(route_weight[None], part_masks, 0)
    all_rows, _ = doubled(outgoing_share[None], part_masks, 0)
    all_rows, all_weights, server_second, own_up = lax.optimization_barrier(
        (all_rows, all_weights, server_second, own_up)
    )
    server_up = to_owner(own_up)
    buffer = jnp.stack(
        [
            lax.dot_general(
                placed.astype(jnp.bfloat16),
                all_rows[k],
                (((0,), (0,)), ((), ())),
                preferred_element_type=jnp.float32,
            )
            .astype(jnp.bfloat16)
            .reshape(head_count, block_rows, col_share)
            for k, (_, _, placed) in enumerate(routings)
        ],
        axis=1,
    )
    def to_mate(m):
        block = lax.dynamic_index_in_dim(buffer, head ^ m, 0, keepdims=False)
        return swapped(block, "seq", m) if m else block

    received = [to_mate(m) for m in range(head_count)]
    received[1:3], server_up, own_down = lax.optimization_barrier(
        (received[1:3], server_up, own_down)
    )
    server_down = to_owner(own_down)
    received = by_place(jnp.stack(received))
    received = received.reshape(head_count, part_count, local_experts, capacity, col_share)
    turn_ids = jnp.arange(tp_count, dtype=jnp.int32)
    in_starts = (tp_place + turn_ids) % tp_count * col_share
    out_starts = (tp_place - turn_ids) % tp_count * col_share

    halves = [
        tp_blocks(jnp.moveaxis(rows, 2, 0).reshape(local_experts, -1, col_share))
        for rows in (received[:, 1:], received[:, :1])
    ]
    server = (server_first, server_second, server_up)
    hidden = hidden_units(in_starts, halves[0], server)
    hidden, own_half, server_down = lax.optimization_barrier((hidden, halves[1], server_down))
    hidden = [hidden, hidden_units(in_starts, own_half, server)]

    def through_experts(rows, parts):
        outs = down_rows(out_starts, rows, server_down)
        outs = [outs[0]] + [from_turned(outs[k], "tp", k) for k in range(1, tp_count)]
        summed = sum(piece.astype(jnp.float32) for piece in outs).astype(jnp.bfloat16)
        summed = summed.reshape(local_experts, head_count, parts, capacity, col_share)
        return jnp.moveaxis(summed, 0, 2).reshape(head_count, parts, block_rows, col_share)

    others = through_experts(hidden[0], part_count - 1)
    own_rows = through_experts(hidden[1], 1)

    def weighted(k, rows):
        placed = routings[k][2]
        stacked = jnp.concatenate(
            [
                jnp.where(
                    placed, jnp.dot(piece, spread, preferred_element_type=jnp.float32), 0.0
                ).astype(jnp.bfloat16)
                for piece in parts_of(all_weights[k], 3)
            ],
            axis=0,
        )
        mixes = jnp.dot(stacked, rows, preferred_element_type=jnp.float32)
        return sum(mixes[k * token_count : (k + 1) * token_count] for k in range(3))

    def back(blocks):
        return lax.all_to_all(
            blocks, "seq", split_axis=0, concat_axis=0, tiled=True, axis_index_groups=groups
        )

    others = back(others)
    mixes = [
        weighted(k, others[:, k - 1].reshape(-1, col_share)) for k in range(1, len(part_turns))
    ]
    mixes, own_rows = lax.optimization_barrier((mixes, own_rows))
    expert_mix = sum(
        swapped(mix.astype(jnp.bfloat16), "seq", turn).astype(jnp.float32)
        for mix, turn in zip(mixes, part_turns[1:])
    )
    own_mix = weighted(0, back(own_rows)[:, 0].reshape(-1, col_share))
    return (residual + (expert_mix + own_mix)).astype(jnp.bfloat16)


def solution(mesh):
    placed = (
        P("seq", None),
        P(),
        P(),
        P("seq", "tp"),
        P("seq", "tp"),
        P("seq", "tp"),
        P("tp", "seq"),
        P("tp"),
        P("seq", None),
        P(None, "seq", "tp"),
        P(None, "seq", "tp"),
        P(None, "seq", "tp"),
        P(),
        P(),
        P("seq", None),
    )
    return jax.shard_map(
        shards, mesh=mesh, in_specs=placed, out_specs=P("seq", "tp"), check_vma=False
    )
```

```python
import jax
import jax.numpy as jnp
from jax import lax
from jax.experimental import pallas as pl
from jax.experimental.pallas import tpu as pltpu
from jax.sharding import PartitionSpec as P

HEAD = 128
HALF_WIN = 2048


EPSILON = 1e-05
ROPE_BASE = 50000.0
MASKED = -1e30
SMALL = pl.CostEstimate(flops=1, bytes_accessed=1, transcendentals=1)


def from_behind(value, axis, steps):
    count = lax.axis_size(axis)
    first, last = (max(0, -steps), min(count, count - steps))
    return lax.ppermute(value, axis, [(source, source + steps) for source in range(first, last)])


def from_turned(value, axis, turn):
    count = lax.axis_size(axis)
    return lax.ppermute(value, axis, [((place + turn) % count, place) for place in range(count)])


def swapped(value, axis, mask):
    count = lax.axis_size(axis)
    return lax.ppermute(value, axis, [(place, place ^ mask) for place in range(count)])


def doubled(value, masks, axis):
    turns = [0]
    for mask in masks:
        value = jnp.concatenate([value, swapped(value, "seq", mask)], axis=axis)
        turns = turns + [turn ^ mask for turn in turns]
    return (value, turns)


def masks_below(count, least=1):
    masks = []
    while count > least:
        count //= 2
        masks.append(count)
    return masks


def rms_scale(row_values, gain_vector):
    mean_square = jnp.mean(row_values * row_values, axis=-1, keepdims=True)
    return row_values * lax.rsqrt(mean_square + EPSILON) * gain_vector


def rotate(rows, cosine, sine_part):
    half_dim = rows.shape[-1] // 2
    first_half = rows[:, :half_dim]
    second_half = rows[:, half_dim:]
    return jnp.concatenate(
        [
            first_half * cosine - second_half * sine_part,
            second_half * cosine + first_half * sine_part,
        ],
        axis=-1,
    )


def length_of(prompt, real_lengths):
    one_hot = prompt[:, None] == jnp.arange(real_lengths.shape[0], dtype=jnp.int32)[None, :]
    return jnp.sum(jnp.where(one_hot, real_lengths[None, :], 0), axis=1)


def prompt_split(slot_ids, slot_len, stagger, prompt_count):
    prompt = jnp.minimum((slot_ids + stagger) // slot_len, prompt_count - 1)
    start = jnp.maximum(prompt * slot_len - stagger, 0)
    return (prompt, slot_ids - start)


def key_rules(query_ids, key_ids, slot_len, stagger, total_slots, real_lengths):
    prompt_count = real_lengths.shape[0]
    key_prompt, key_pos = prompt_split(key_ids, slot_len, stagger, prompt_count)
    query_prompt = prompt_split(query_ids, slot_len, stagger, prompt_count)[0]
    inside = (key_ids >= 0) & (key_ids < total_slots)
    key_live = inside & (key_pos < length_of(key_prompt, real_lengths))
    same_prompt = query_prompt[:, None] == key_prompt[None, :]
    nearby = jnp.abs(query_ids[:, None] - key_ids[None, :]) < HALF_WIN
    return same_prompt & nearby & key_live[None, :]


def parts_of(values, count):
    rest = values
    pieces = []
    for _ in range(count):
        piece = lax.reduce_precision(rest, 8, 7)
        rest = rest - piece
        pieces.append(piece.astype(jnp.bfloat16))
    return pieces


def attend(softmax_state, query_rows, key_rows, value_rows, allowed):
    running_max, denominator, accumulated = softmax_state
    scores = lax.dot_general(
        query_rows, key_rows, (((1,), (1,)), ((), ())), preferred_element_type=jnp.float32
    ) * HEAD ** (-0.5)
    scores = jnp.where(allowed, scores, MASKED)
    new_max = jnp.maximum(running_max, jnp.max(scores, axis=1, keepdims=True))
    rescale = jnp.exp(running_max - new_max)
    weight_tensors = jnp.exp(scores - new_max)
    denominator = denominator * rescale + jnp.sum(weight_tensors, axis=1, keepdims=True)
    high, low = parts_of(weight_tensors, 2)
    accumulated = (
        accumulated * rescale
        + jnp.dot(high, value_rows, preferred_element_type=jnp.float32)
        + jnp.dot(low, value_rows, preferred_element_type=jnp.float32)
    )
    return (new_max, denominator, accumulated)


def order_body(order_ref, gate_ref, up_ref, down_ref, *outs):
    half = gate_ref.shape[2] // 2
    outs[0][...] = gate_ref[:, :, :half].astype(jnp.bfloat16)
    outs[1][...] = gate_ref[:, :, half:].astype(jnp.bfloat16)
    outs[2][...] = up_ref[...].astype(jnp.bfloat16)
    outs[3][...] = down_ref[...].astype(jnp.bfloat16)


def order_experts(layout_map, gate, up, down):
    count, rows, width = gate.shape
    source = pl.BlockSpec((1, rows, width), lambda place, order: (order[place], 0, 0))
    widths = (width // 2, width - width // 2, width, width)
    return pl.pallas_call(
        order_body,
        grid_spec=pltpu.PrefetchScalarGridSpec(
            num_scalar_prefetch=1,
            grid=(count,),
            in_specs=[source, source, source],
            out_specs=[
                pl.BlockSpec((1, rows, some), lambda place, order: (place, 0, 0))
                for some in widths
            ],
        ),
        out_shape=[jax.ShapeDtypeStruct((count, rows, some), jnp.bfloat16) for some in widths],
        cost_estimate=SMALL,
        name="order_experts",
    )(layout_map, gate, up, down)


def pack_body(query_ref, key_ref, value_ref, out_ref):
    heads = query_ref.shape[1] // HEAD
    for place in range(out_ref.shape[0]):
        head = place % heads
        for k, source in enumerate((query_ref, key_ref, value_ref)):
            out_ref[place, :, k * HEAD : (k + 1) * HEAD] = source[
                :, head * HEAD : (head + 1) * HEAD
            ].astype(jnp.bfloat16)


def pack_heads(w_query, w_key, w_value, copies):
    rows, width = w_query.shape
    places = copies * (width // HEAD)
    step = rows // 4 if rows % 64 == 0 else rows
    source = pl.BlockSpec((step, width), lambda place: (place, 0))
    return pl.pallas_call(
        pack_body,
        grid=(rows // step,),
        in_specs=[source, source, source],
        out_specs=pl.BlockSpec((places, step, 3 * HEAD), lambda place: (0, place, 0)),
        out_shape=jax.ShapeDtypeStruct((places, rows, 3 * HEAD), jnp.bfloat16),
        compiler_params=pltpu.CompilerParams(vmem_limit_bytes=32 * 2**20),
        cost_estimate=SMALL,
        name="pack_heads",
    )(w_query, w_key, w_value)


def project_body(turn_count, share, start_ref, *refs):
    rows, (weight_ref, cosine_ref, sine_ref, out_ref) = (refs[:turn_count], refs[turn_count:])
    product = 0.0
    for turn in range(turn_count):
        first = pl.multiple_of(start_ref[turn], share)
        product = product + jnp.dot(
            rows[turn][...], weight_ref[pl.ds(first, share), :], preferred_element_type=jnp.float32
        )
    cosine, sine_part = (cosine_ref[...], sine_ref[...])
    out_ref[:, :HEAD] = rotate(product[:, :HEAD], cosine, sine_part).astype(jnp.bfloat16)
    out_ref[:, HEAD : 2 * HEAD] = rotate(
        product[:, HEAD : 2 * HEAD], cosine, sine_part
    ).astype(jnp.bfloat16)
    out_ref[:, 2 * HEAD :] = product[:, 2 * HEAD :].astype(jnp.bfloat16)


def project(starts, row_blocks, weights, cosine, sine_part):
    row_count, share = row_blocks[0].shape
    step = row_count // 4
    whole = pl.BlockSpec(weights.shape, lambda place, starts: (0, 0))
    angle = pl.BlockSpec((step, cosine.shape[1]), lambda place, starts: (place, 0))
    return pl.pallas_call(
        lambda *refs: project_body(len(row_blocks), share, *refs),
        grid_spec=pltpu.PrefetchScalarGridSpec(
            num_scalar_prefetch=1,
            grid=(4,),
            in_specs=[pl.BlockSpec((step, share), lambda place, starts: (place, 0))]
            * len(row_blocks)
            + [whole, angle, angle],
            out_specs=pl.BlockSpec((step, weights.shape[1]), lambda place, starts: (place, 0)),
        ),
        out_shape=jax.ShapeDtypeStruct((row_count, weights.shape[1]), jnp.bfloat16),
        compiler_params=pltpu.CompilerParams(vmem_limit_bytes=32 * 2**20),
        cost_estimate=SMALL,
        name="project",
    )(starts, *row_blocks, weights, cosine, sine_part)


def attend_body(sink_ref, query_prompt_ref, key_prompt_ref, query_ref, key_ref, value_ref, out_ref):
    sink = sink_ref[0]
    scores = lax.dot_general(
        query_ref[...],
        key_ref[...],
        (((1,), (1,)), ((), ())),
        preferred_element_type=jnp.float32,
    ) * HEAD ** (-0.5)
    scores = jnp.where(query_prompt_ref[...] == key_prompt_ref[...], scores, MASKED)
    top = jnp.maximum(sink, jnp.max(scores, axis=1, keepdims=True))
    weights = jnp.exp(scores - top)
    denominator = jnp.exp(sink - top) + jnp.sum(weights, axis=1, keepdims=True)
    high = weights.astype(jnp.bfloat16)
    low = (weights - high.astype(jnp.float32)).astype(jnp.bfloat16)
    values = value_ref[...]
    mix = jnp.dot(high, values, preferred_element_type=jnp.float32) + jnp.dot(
        low, values, preferred_element_type=jnp.float32
    )
    out_ref[...] = (mix / denominator).astype(jnp.bfloat16)


def attend_once(sink, query_prompt, key_prompt, rows):
    row_count = rows.shape[0]
    steps = 4 if row_count % 64 == 0 else 1
    step = row_count // steps
    return pl.pallas_call(
        attend_body,
        grid=(steps,),
        in_specs=[
            pl.BlockSpec(memory_space=pltpu.SMEM),
            pl.BlockSpec((step, 1), lambda place: (place, 0)),
            pl.BlockSpec((1, row_count), lambda place: (0, 0)),
            pl.BlockSpec((step, HEAD), lambda place: (place, 0)),
            pl.BlockSpec((row_count, HEAD), lambda place: (0, 1)),
            pl.BlockSpec((row_count, HEAD), lambda place: (0, 2)),
        ],
        out_specs=pl.BlockSpec((step, HEAD), lambda place: (place, 0)),
        out_shape=jax.ShapeDtypeStruct((row_count, HEAD), jnp.bfloat16),
        compiler_params=pltpu.CompilerParams(vmem_limit_bytes=32 * 2**20),
        cost_estimate=SMALL,
        name="attend_once",
    )(sink, query_prompt[:, None], key_prompt[None, :], rows, rows, rows)


def out_body(head_ref, first_ref, first_other_ref, second_ref, second_other_ref, out_ref):
    heads = first_ref.shape[0] // HEAD
    first, second = (
        jnp.concatenate([head_ref[h] for h in place], axis=1)
        for place in (range(heads), range(heads, head_ref.shape[0]))
    )
    rows = second.shape[1]
    half = first_ref.shape[1]
    span = half // 2
    for k, (one, two) in enumerate(
        ((first_ref, second_ref), (first_other_ref, second_other_ref))
    ):
        own = jnp.dot(first, one[...], preferred_element_type=jnp.float32)
        other = jnp.dot(second, two[:rows, :], preferred_element_type=jnp.float32)
        if k == 0:
            low, high = (other[:, :span], other[:, span:])
            out_ref[:, :span] = own[:, :span] + low
            out_ref[:, span:half] = own[:, span:]
            out_ref[:, half : half + span] = high
        else:
            out_ref[:, span:half] = out_ref[:, span:half] + other[:, :span]
            out_ref[:, half : half + span] = out_ref[:, half : half + span] + own[:, :span]
            out_ref[:, half + span :] = own[:, span:] + other[:, span:]


def out_project(heads, pieces):
    vmem = pl.BlockSpec(memory_space=pltpu.VMEM)
    return pl.pallas_call(
        out_body,
        in_specs=[vmem] * 5,
        out_specs=vmem,
        out_shape=jax.ShapeDtypeStruct((heads.shape[1], 2 * pieces[0].shape[1]), jnp.float32),
        compiler_params=pltpu.CompilerParams(vmem_limit_bytes=40 * 2**20),
        cost_estimate=SMALL,
        name="out_project",
    )(heads, *pieces)


def settle_body(piece_count, width, place_ref, *refs):
    pieces = refs[:piece_count]
    token_ref, gain_ref, router_ref, full_ref, outgoing_ref, logit_ref, router_all = refs[
        piece_count:
    ]
    for place in range(full_ref.shape[1] // width):
        here = slice(place * width, (place + 1) * width)
        there = pl.ds(pl.multiple_of(place_ref[place] * width, width), width)
        block = sum(piece[:, there] for piece in pieces)
        full_ref[:, here] = token_ref[:, here].astype(jnp.float32) + block
        router_all[:, here] = router_ref[:, there]
    outgoing = rms_scale(full_ref[...], gain_ref[...]).astype(jnp.bfloat16)
    outgoing_ref[...] = outgoing
    logit_ref[...] = lax.dot_general(
        outgoing,
        router_all[...],
        (((1,), (1,)), ((), ())),
        preferred_element_type=jnp.float32,
    )


def settle(places, pieces, tokens, gain, router, width):
    rows, columns = tokens.shape
    vmem = pl.BlockSpec(memory_space=pltpu.VMEM)
    return pl.pallas_call(
        lambda *refs: settle_body(len(pieces), width, *refs),
        in_specs=[pl.BlockSpec(memory_space=pltpu.SMEM)] + [vmem] * (len(pieces) + 3),
        out_specs=[vmem] * 3,
        out_shape=[
            jax.ShapeDtypeStruct((rows, columns), jnp.float32),
            jax.ShapeDtypeStruct((rows, columns), jnp.bfloat16),
            jax.ShapeDtypeStruct((rows, router.shape[0]), jnp.float32),
        ],
        scratch_shapes=[pltpu.VMEM(router.shape, jnp.bfloat16)],
        compiler_params=pltpu.CompilerParams(vmem_limit_bytes=32 * 2**20),
        cost_estimate=SMALL,
        name="settle",
    )(places, *pieces, tokens, gain[None, :], router)


def hidden_body(turn_count, share, start_ref, *refs):
    rows, (first_ref, second_ref, up_ref, out_ref) = (refs[:turn_count], refs[turn_count:])
    first = second = up = 0.0
    for turn in range(turn_count):
        here = pl.ds(pl.multiple_of(start_ref[turn], share), share)
        some = rows[turn][0]
        first = first + jnp.dot(some, first_ref[0, here, :], preferred_element_type=jnp.float32)
        second = second + jnp.dot(some, second_ref[0, here, :], preferred_element_type=jnp.float32)
        up = up + jnp.dot(some, up_ref[0, here, :], preferred_element_type=jnp.float32)
    gate = jnp.concatenate([first, second], axis=1)
    out_ref[0] = (gate / (1.0 + jnp.exp(-gate)) * up).astype(jnp.bfloat16)


def hidden_units(starts, row_blocks, weights):
    local_experts, row_count, share = row_blocks[0].shape
    width = weights[-1].shape[2]
    count = len(row_blocks)
    return pl.pallas_call(
        lambda *refs: hidden_body(count, share, *refs),
        grid_spec=pltpu.PrefetchScalarGridSpec(
            num_scalar_prefetch=1,
            grid=(local_experts,),
            in_specs=[pl.BlockSpec((1, row_count, share), lambda e, a: (e, 0, 0))] * count
            + [pl.BlockSpec((1, *w.shape[1:]), lambda e, a: (e, 0, 0)) for w in weights],
            out_specs=pl.BlockSpec((1, row_count, width), lambda e, a: (e, 0, 0)),
        ),
        out_shape=jax.ShapeDtypeStruct((local_experts, row_count, width), jnp.bfloat16),
        compiler_params=pltpu.CompilerParams(vmem_limit_bytes=52 * 2**20),
        cost_estimate=SMALL,
        name="hidden_units",
    )(starts, *row_blocks, *weights)


def down_body(turn_count, share, start_ref, hidden_ref, down_ref, *outs):
    for turn in range(turn_count):
        here = pl.ds(pl.multiple_of(start_ref[turn], share), share)
        outs[turn][0] = lax.dot_general(
            hidden_ref[0],
            down_ref[0, here, :],
            (((1,), (1,)), ((), ())),
            preferred_element_type=jnp.float32,
        ).astype(jnp.bfloat16)


def down_rows(starts, hidden, down):
    local_experts, row_count, width = hidden.shape
    columns, count = (down.shape[1], starts.shape[0])
    share = columns // count
    block = pl.BlockSpec((1, row_count, share), lambda e, a: (e, 0, 0))
    return pl.pallas_call(
        lambda *refs: down_body(count, share, *refs),
        grid_spec=pltpu.PrefetchScalarGridSpec(
            num_scalar_prefetch=1,
            grid=(local_experts,),
            in_specs=[
                pl.BlockSpec((1, row_count, width), lambda e, a: (e, 0, 0)),
                pl.BlockSpec((1, columns, width), lambda e, a: (e, 0, 0)),
            ],
            out_specs=[block] * count,
        ),
        out_shape=[jax.ShapeDtypeStruct((local_experts, row_count, share), jnp.bfloat16)] * count,
        compiler_params=pltpu.CompilerParams(vmem_limit_bytes=52 * 2**20),
        cost_estimate=SMALL,
        name="down_rows",
    )(starts, hidden, down)


def shards(
    tokens,
    attn_gain,
    mlp_gain,
    w_query,
    w_key,
    w_value,
    w_out,
    sink_logits,
    router,
    expert_gate,
    expert_up,
    expert_down,
    layout_map,
    real_lengths,
    routes,
):
    token_count, model_width = tokens.shape
    seq_count = lax.axis_size("seq")
    tp_count = lax.axis_size("tp")
    expert_count = router.shape[1]
    route_count = routes.shape[1]
    head_count = sink_logits.shape[0]
    col_share = model_width // tp_count
    total_slots = token_count * seq_count
    prompt_count = real_lengths.shape[0]
    slot_len = total_slots // prompt_count
    stagger = token_count // 2
    capacity = max(2, min(token_count, 9 * token_count * route_count // (8 * expert_count)))
    part_count = seq_count // head_count
    part_slots = head_count * token_count
    local_experts = expert_count // seq_count
    seq_place = lax.axis_index("seq")
    tp_place = lax.axis_index("tp")
    part = seq_place // head_count
    head = seq_place % head_count

    def tp_blocks(value):
        return [value] + [from_turned(value, "tp", turn) for turn in range(1, tp_count)]

    offsets = jnp.arange(token_count, dtype=jnp.int32)
    turns = jnp.arange(head_count, dtype=jnp.int32)
    aligned = part_count == prompt_count and part_slots + stagger <= HALF_WIN
    group_masks = masks_below(head_count)
    groups = [[first + k for k in range(head_count)] for first in range(0, seq_count, head_count)]
    part_masks = masks_below(seq_count, head_count)

    packed = pack_heads(w_query, w_key, w_value, part_count)
    packed, tokens = lax.optimization_barrier((packed, tokens))
    head_weights = lax.all_to_all(
        packed,
        "seq",
        split_axis=0,
        concat_axis=0,
        tiled=True,
    ).reshape(model_width, 3 * HEAD)

    normed = rms_scale(tokens.astype(jnp.float32), attn_gain).astype(jnp.bfloat16)
    share = lax.dynamic_slice_in_dim(normed, tp_place * col_share, col_share, 1)
    all_routes, part_turns = doubled(routes[None], part_masks, 0)
    out_all, _ = doubled(
        jnp.concatenate([w_out, router.T], axis=0).astype(jnp.bfloat16), part_masks, 1
    )
    first_rows, first_turns = doubled(share[None], group_masks[:1], 0)
    first_rows, layout_map = lax.optimization_barrier((first_rows, layout_map))
    own_first, own_second, own_up, own_down = order_experts(
        layout_map, expert_gate, expert_up, expert_down
    )
    part_ids = (part * head_count + (head ^ turns))[:, None] * token_count + offsets[None, :]
    part_ids = part_ids.reshape(-1)
    part_positions = prompt_split(part_ids, slot_len, stagger, prompt_count)[1]
    half_dim = HEAD // 2
    frequency = ROPE_BASE ** (-jnp.arange(half_dim, dtype=jnp.float32) / half_dim)
    angles = part_positions.astype(jnp.float32)[:, None] * frequency[None, :]
    cosine = jnp.cos(angles)
    sine_part = jnp.sin(angles)
    pieces = []
    for piece, masks in (
        (first_rows[:, :, : col_share // 2], group_masks[1:]),
        (first_rows[:, :, col_share // 2 :], group_masks[1:][::-1]),
    ):
        known = first_turns
        for mask in masks:
            if mask == masks[-1]:
                piece, own_first, cosine, sine_part, all_routes = lax.optimization_barrier(
                    (piece, own_first, cosine, sine_part, all_routes)
                )
            piece = jnp.concatenate([piece, swapped(piece, "seq", mask)], axis=0)
            known = known + [turn ^ mask for turn in known]
        pieces.append(jnp.concatenate([piece[known.index(m)] for m in range(head_count)], axis=0))
    part_rows = jnp.concatenate(pieces, axis=1)

    def to_owner(blocks):
        taken = lax.all_to_all(blocks, "seq", split_axis=0, concat_axis=0, tiled=True)
        taken = taken.reshape(seq_count, local_experts, *blocks.shape[1:])
        return jnp.swapaxes(taken, 0, 1).reshape(local_experts, model_width, blocks.shape[2])

    out_all, _ = doubled(out_all, group_masks[:-2], 1)
    out_rows = out_all.shape[0] // 32 * 16
    out_halves = [
        (out_all[:out_rows], group_masks[-2:]),
        (out_all[out_rows:], group_masks[-2:][::-1]),
    ]
    halves, head_weights, part_rows, own_first = lax.optimization_barrier(
        ([half for half, _ in out_halves], head_weights, part_rows, own_first)
    )
    server_first = to_owner(own_first)
    out_halves = [
        (doubled(half, masks[:1], 1)[0], masks[1:]) for half, (_, masks) in zip(halves, out_halves)
    ]

    def by_place(blocks):
        return jnp.stack(
            [
                lax.dynamic_index_in_dim(blocks, head ^ place, 0, keepdims=False)
                for place in range(head_count)
            ]
        )

    expert_ids = jnp.arange(expert_count, dtype=jnp.int32)
    block_rows = local_experts * capacity
    columns = jnp.arange(head_count * block_rows, dtype=jnp.int32)
    column_owner = part * head_count + columns // block_rows
    column_expert = column_owner * local_experts + columns // capacity % local_experts
    spread = (column_expert[None, :] == expert_ids[:, None]).astype(jnp.bfloat16)
    wanted = (columns % capacity).astype(jnp.float32)
    earlier = (offsets[:, None] > offsets[None, :]).astype(jnp.bfloat16)

    def routing(turn, own_routes):
        ids = (seq_place ^ turn) * token_count + offsets
        prompt, position = prompt_split(ids, slot_len, stagger, prompt_count)
        valid_token = position < length_of(prompt, real_lengths)
        chosen = jnp.any(own_routes[:, :, None] == expert_ids[None, None, :], axis=1)
        live = chosen & valid_token[:, None]
        rank = jnp.dot(earlier, live.astype(jnp.bfloat16), preferred_element_type=jnp.float32)
        rank = jnp.where(live, rank, -1.0).astype(jnp.bfloat16)
        placed = jnp.dot(rank, spread, preferred_element_type=jnp.float32) == wanted[None, :]
        return (chosen, valid_token, placed)

    routings = [routing(turn, all_routes[k]) for k, turn in enumerate(part_turns)]
    chosen, valid_token, _ = routings[0]

    starts = (tp_place + jnp.arange(tp_count, dtype=jnp.int32)) % tp_count * col_share
    rows = project(starts, tp_blocks(part_rows), head_weights, cosine, sine_part)
    sink = lax.dynamic_slice_in_dim(sink_logits, head, 1, 0)

    def start_state(row_count):
        return (
            jnp.broadcast_to(sink[:, None], (row_count, 1)),
            jnp.ones((row_count, 1), jnp.float32),
            jnp.zeros((row_count, HEAD), jnp.float32),
        )

    if aligned:
        edge_start = (head ^ (head_count - 1)) * token_count + token_count - stagger
        edge = from_behind(
            lax.dynamic_slice_in_dim(rows, edge_start, stagger, 0), "seq", head_count
        )
        edge_ids = part * part_slots - stagger + jnp.arange(stagger, dtype=jnp.int32)
        row_ids = jnp.concatenate([part_ids, edge_ids])
        row_prompt, row_position = prompt_split(row_ids, slot_len, stagger, prompt_count)
        row_live = (row_ids >= 0) & (row_position < length_of(row_prompt, real_lengths))
        halves, edge = lax.optimization_barrier(([half for half, _ in out_halves], edge))
        out_halves = [(half, masks) for half, (_, masks) in zip(halves, out_halves)]
        mixed = attend_once(
            sink,
            row_prompt,
            jnp.where(row_live, row_prompt, -1),
            jnp.concatenate([rows, edge], axis=0),
        )
        edge_back = from_behind(mixed[part_slots:], "seq", -head_count)
        mixed = mixed[:part_slots]
        kept = lax.dynamic_slice_in_dim(mixed, edge_start, stagger, 0)
        mixed = lax.dynamic_update_slice_in_dim(
            mixed, jnp.where(part < part_count - 1, edge_back, kept), edge_start, 0
        )
    else:
        query_rows, key_rows, value_rows = (rows[:, k * HEAD : (k + 1) * HEAD] for k in range(3))
        softmax_state = attend(
            start_state(part_slots),
            query_rows,
            key_rows,
            value_rows,
            key_rules(part_ids, part_ids, slot_len, stagger, total_slots, real_lengths),
        )
        from_below = from_above = jnp.concatenate([key_rows, value_rows], axis=1)
        for turn in range(1, min(part_count - 1, -(-HALF_WIN // part_slots)) + 1):
            from_below = from_behind(from_below, "seq", head_count)
            from_above = from_behind(from_above, "seq", -head_count)
            reach = turn * part_slots
            key_ids = jnp.concatenate([part_ids - reach, part_ids + reach])
            pair = jnp.concatenate([from_below, from_above], axis=0)
            softmax_state = attend(
                softmax_state,
                query_rows,
                pair[:, :HEAD],
                pair[:, HEAD:],
                key_rules(part_ids, key_ids, slot_len, stagger, total_slots, real_lengths),
            )
        _, denominator, accumulated = softmax_state
        mixed = (accumulated / denominator).astype(jnp.bfloat16)
    blocks = by_place(mixed.reshape(head_count, token_count, HEAD))
    out_halves = [(half, swapped(half, "seq", masks[0])) for half, masks in out_halves]
    blocks, out_halves, server_first = lax.optimization_barrier((blocks, out_halves, server_first))
    attention_result = lax.all_to_all(
        blocks, "seq", split_axis=0, concat_axis=0, tiled=True, axis_index_groups=groups
    )
    attention_result, own_second = lax.optimization_barrier((attention_result, own_second))
    server_second = to_owner(own_second)

    proj_width = head_count * HEAD
    def joined(pieces, half):
        if half == 0:
            return jnp.concatenate(pieces, axis=1)
        span = pieces[0].shape[1] // 2
        low, high = ([piece[:, k * span : (k + 1) * span] for piece in pieces] for k in range(2))
        return jnp.concatenate([*low, *high], axis=1)

    if out_rows % HEAD == 0 and out_rows < proj_width:
        partial_out = out_project(attention_result, [*out_halves[0], *out_halves[1]])
    else:
        attention_result = jnp.swapaxes(attention_result, 0, 1).reshape(token_count, proj_width)
        partial_out = sum(
            joined([jnp.dot(rows, piece, preferred_element_type=jnp.float32) for piece in pieces], half)
            for half, (rows, pieces) in enumerate(
                (
                    (attention_result[:, :out_rows], out_halves[0]),
                    (
                        attention_result[:, out_rows:],
                        [piece[: proj_width - out_rows] for piece in out_halves[1]],
                    ),
                )
            )
        )
    if tp_count == 2:
        out_pieces = [partial_out, from_turned(partial_out, "tp", 1)]
    else:
        out_pieces = [lax.psum(partial_out, "tp")]
    router_rows = joined([piece[proj_width - out_rows :] for piece in out_halves[1]], 1)
    slots = jnp.arange(seq_count, dtype=jnp.int32)
    turn = seq_place ^ slots
    bits = len(part_masks) + len(group_masks)
    out_places = sum(((turn >> k) & 1) << (bits - 1 - k) for k in range(bits))
    width = w_out.shape[1]
    if width % 128:

        def in_order(value):
            blocks = [
                lax.dynamic_slice_in_dim(value, out_places[place] * width, width, 1)
                for place in range(seq_count)
            ]
            return jnp.concatenate(blocks, axis=1)

        out_pieces, router_rows = ([in_order(piece) for piece in out_pieces], in_order(router_rows))
        out_places, width = (jnp.zeros((1,), jnp.int32), model_width)
    full_rows, outgoing, logits = settle(
        out_places, out_pieces, tokens, mlp_gain, router_rows, width
    )
    residual = lax.dynamic_slice_in_dim(full_rows, tp_place * col_share, col_share, 1)
    outgoing_share = lax.dynamic_slice_in_dim(outgoing, tp_place * col_share, col_share, 1)


    route_logits = jnp.where(chosen, logits, -jnp.inf)
    route_exp = jnp.exp(route_logits - jnp.max(route_logits, axis=1, keepdims=True))
    route_weight = route_exp / jnp.sum(route_exp, axis=1, keepdims=True)
    route_weight = route_weight * valid_token[:, None]
    all_weights, _ = doubled(route_weight[None], part_masks, 0)
    all_rows, _ = doubled(outgoing_share[None], part_masks, 0)
    all_rows, all_weights, server_second, own_up = lax.optimization_barrier(
        (all_rows, all_weights, server_second, own_up)
    )
    server_up = to_owner(own_up)
    buffer = jnp.stack(
        [
            lax.dot_general(
                placed.astype(jnp.bfloat16),
                all_rows[k],
                (((0,), (0,)), ((), ())),
                preferred_element_type=jnp.float32,
            )
            .astype(jnp.bfloat16)
            .reshape(head_count, block_rows, col_share)
            for k, (_, _, placed) in enumerate(routings)
        ],
        axis=1,
    )
    def to_mate(m):
        block = lax.dynamic_index_in_dim(buffer, head ^ m, 0, keepdims=False)
        return swapped(block, "seq", m) if m else block

    received = [to_mate(m) for m in range(head_count)]
    received[1:3], server_up, own_down = lax.optimization_barrier(
        (received[1:3], server_up, own_down)
    )
    server_down = to_owner(own_down)
    received = by_place(jnp.stack(received))
    received = received.reshape(head_count, part_count, local_experts, capacity, col_share)
    turn_ids = jnp.arange(tp_count, dtype=jnp.int32)
    in_starts = (tp_place + turn_ids) % tp_count * col_share
    out_starts = (tp_place - turn_ids) % tp_count * col_share

    halves = [
        tp_blocks(jnp.moveaxis(rows, 2, 0).reshape(local_experts, -1, col_share))
        for rows in (received[:, 1:], received[:, :1])
    ]
    server = (server_first, server_second, server_up)
    hidden = hidden_units(in_starts, halves[0], server)
    hidden, own_half, server_down = lax.optimization_barrier((hidden, halves[1], server_down))
    hidden = [hidden, hidden_units(in_starts, own_half, server)]

    def through_experts(rows, parts):
        outs = down_rows(out_starts, rows, server_down)
        outs = [outs[0]] + [from_turned(outs[k], "tp", k) for k in range(1, tp_count)]
        summed = sum(piece.astype(jnp.float32) for piece in outs).astype(jnp.bfloat16)
        summed = summed.reshape(local_experts, head_count, parts, capacity, col_share)
        return jnp.moveaxis(summed, 0, 2).reshape(head_count, parts, block_rows, col_share)

    others = through_experts(hidden[0], part_count - 1)
    own_rows = through_experts(hidden[1], 1)

    def weighted(k, rows):
        placed = routings[k][2]
        stacked = jnp.concatenate(
            [
                jnp.where(
                    placed, jnp.dot(piece, spread, preferred_element_type=jnp.float32), 0.0
                ).astype(jnp.bfloat16)
                for piece in parts_of(all_weights[k], 3)
            ],
            axis=0,
        )
        mixes = jnp.dot(stacked, rows, preferred_element_type=jnp.float32)
        return sum(mixes[k * token_count : (k + 1) * token_count] for k in range(3))

    def back(blocks):
        return lax.all_to_all(
            blocks, "seq", split_axis=0, concat_axis=0, tiled=True, axis_index_groups=groups
        )

    others = back(others)
    others, own_rows = lax.optimization_barrier((others, own_rows))
    mixes = [
        weighted(k, others[:, k - 1].reshape(-1, col_share)) for k in range(1, len(part_turns))
    ]
    expert_mix = sum(
        swapped(mix.astype(jnp.bfloat16), "seq", turn).astype(jnp.float32)
        for mix, turn in zip(mixes, part_turns[1:])
    )
    own_mix = weighted(0, back(own_rows)[:, 0].reshape(-1, col_share))
    return (residual + (expert_mix + own_mix)).astype(jnp.bfloat16)


def solution(mesh):
    placed = (
        P("seq", None),
        P(),
        P(),
        P("seq", "tp"),
        P("seq", "tp"),
        P("seq", "tp"),
        P("tp", "seq"),
        P("tp"),
        P("seq", None),
        P(None, "seq", "tp"),
        P(None, "seq", "tp"),
        P(None, "seq", "tp"),
        P(),
        P(),
        P("seq", None),
    )
    return jax.shard_map(
        shards, mesh=mesh, in_specs=placed, out_specs=P("seq", "tp"), check_vma=False
    )
```
